32 devices in a mesh: dev: 2 (over x), sa: 16 (over z, y, core).
Axes of the slice: x: 2, y: 2, z: 4, core: 2. Of those that a mesh axis runs over, the one named last changes fastest.
Arguments:
- patches: bfloat16 [8, 1024, 1152], P('dev', 'sa'), may hold values from -6 to 6
- patch_mask: int32 [8, 1024], P('dev', 'sa'), may hold values from 0 to 1, as said below
- cotangent: bfloat16 [8, 1024, 1152], P('dev', 'sa'), may hold values from -6 to 6
- w_qkv: bfloat16 [1152, 3456], P('sa', 'dev'), may hold values from -0.1875 to 0.1875
- w_out: bfloat16 [1152, 1152], P('sa', 'dev'), may hold values from -0.75 to 0.75
- w_up: bfloat16 [1152, 4304], P('sa', 'dev'), may hold values from -0.1875 to 0.1875
- w_down: bfloat16 [1152, 4304], P('sa', 'dev'), may hold values from -0.125 to 0.125
- gain_one: bfloat16 [1, 1152], P(None, 'dev'), may hold values from 0.25 to 1.75
- shift_one: bfloat16 [1, 1152], P(None, 'dev'), may hold values from -4 to 4
- gain_two: bfloat16 [1, 1152], P(None, 'dev'), may hold values from 0.25 to 1.75
- shift_two: bfloat16 [1, 1152], P(None, 'dev'), may hold values from -4 to 4
- bias_query: bfloat16 [1, 1152], P(None, 'dev'), may hold values from -4 to 4
- bias_value: bfloat16 [1, 1152], P(None, 'dev'), may hold values from -4 to 4
- bias_out: bfloat16 [1, 1152], P(None, 'dev'), may hold values from -4 to 4
- bias_up: bfloat16 [1, 4304], P(None, 'dev'), may hold values from -4 to 4
- bias_down: bfloat16 [1, 1152], P(None, 'dev'), may hold values from -4 to 4
Outputs:
- result: bfloat16 [8, 1024, 1152], P('dev', 'sa')
- grad_patches: bfloat16 [8, 1024, 1152], P('dev', 'sa')
- grad_w_qkv: float32 [1152, 3456], P('sa', 'dev')
- grad_w_out: float32 [1152, 1152], P('sa', 'dev')
- grad_w_up: float32 [1152, 4304], P('sa', 'dev')
- grad_w_down: float32 [1152, 4304], P('sa', 'dev')
- grad_gain_one: float32 [1, 1152], P(None, 'dev')
- grad_shift_one: float32 [1, 1152], P(None, 'dev')
- grad_gain_two: float32 [1, 1152], P(None, 'dev')
- grad_shift_two: float32 [1, 1152], P(None, 'dev')
- grad_bias_query: float32 [1, 1152], P(None, 'dev')
- grad_bias_value: float32 [1, 1152], P(None, 'dev')
- grad_bias_out: float32 [1, 1152], P(None, 'dev')
- grad_bias_up: float32 [1, 4304], P(None, 'dev')
- grad_bias_down: float32 [1, 1152], P(None, 'dev')
The draws below stay inside these ranges and needn't reach their ends.
Inputs may be any that keep to these rules, and one draw needn't show every extreme that they name: `patch_mask`: each image's ones are its first patches, 256 of them or more.
All inputs are finite; a program needn't handle non-finite values.
Results may differ from the reference program's by a relative error of at most 0.018.
Values may be sent and summed in bfloat16 or wider, within the bound.
No kernel may reach another device: no remote copies, remote signals or barrier semaphores. Data moves between devices by JAX's collectives and lax.ppermute only.
A program may use at most 256 MiB of HBM per device.

```python
import jax
import jax.numpy as jnp
from jax import lax

D = 1152
HEADS = 16
HEAD_DIM = 72
FF = 4304
SEQ = 1024
IMAGES = 8


def draw_patch_mask(key, part):
    lengths = jax.random.randint(key, (IMAGES,), SEQ // 4, SEQ + 1)
    positions = jnp.arange(SEQ, dtype=jnp.int32)
    return (positions[None, :] < lengths[:, None]).astype(jnp.int32)


def steps_of(own_key, shape, pieces, least, largest):
    def one(position, shards_of):
        heights = jax.random.uniform(jax.random.fold_in(jax.random.fold_in(own_key, 6), position), (shards_of,), jnp.float32, least / len(pieces), largest / len(pieces))
        return jnp.repeat(jnp.exp(heights), shape[position] // shards_of).reshape((-1,) + (1,) * (len(shape) - position - 1))

    level = one(*pieces[0])
    for cut in pieces[1:]:
        level = level * one(*cut)
    return level


def noise(stream_key, extent, scale, reach, shards=(), held_as=jnp.bfloat16):
    values = scale * jax.random.normal(stream_key, extent, jnp.float32)
    if shards:
        values = values * steps_of(stream_key, extent, shards, -0.22, 0.18)
    return jnp.clip(values, -reach, reach).astype(held_as)


def setup_inputs(seed: int = 0) -> dict:
    splits = jax.random.split(jax.random.key(seed), 17)
    patches = noise(splits[0], (IMAGES, SEQ, D), 1.0, 6.0, ((0, 2), (1, 16)))
    patch_mask = draw_patch_mask(jax.random.fold_in(splits[16], 71), 0)
    cotangent = noise(splits[2], (IMAGES, SEQ, D), 1.0, 6.0, ((0, 2), (1, 16)))
    w_qkv = noise(splits[3], (D, 3 * D), D ** -0.5, 0.1875, ((0, 16), (1, 2)))
    w_out = noise(splits[4], (D, D), (D // 16) ** -0.5, 0.75, ((0, 16), (1, 2)))
    w_up = noise(splits[5], (D, FF), D ** -0.5, 0.1875, ((0, 16), (1, 2)))
    w_down = noise(splits[6], (D, FF), (FF // 2) ** -0.5, 0.125, ((0, 16), (1, 2)))
    gain_one = jnp.clip(1.0 + 0.15 * jax.random.normal(splits[7], (1, D), jnp.float32), 0.25, 1.75).astype(jnp.bfloat16)
    shift_one = noise(splits[8], (1, D), 0.3, 4.0, ((1, 2),))
    gain_two = jnp.clip(1.0 + 0.15 * jax.random.normal(splits[9], (1, D), jnp.float32), 0.25, 1.75).astype(jnp.bfloat16)
    shift_two = noise(splits[10], (1, D), 0.3, 4.0, ((1, 2),))
    bias_query = noise(splits[11], (1, D), 0.3, 4.0, ((1, 2),))
    bias_value = noise(splits[12], (1, D), 0.3, 4.0, ((1, 2),))
    bias_out = noise(splits[13], (1, D), 0.3, 4.0, ((1, 2),))
    bias_up = noise(splits[14], (1, FF), 0.3, 4.0, ((1, 2),))
    bias_down = noise(splits[15], (1, D), 0.3, 4.0, ((1, 2),))
    return {"patches": patches, "patch_mask": patch_mask, "cotangent": cotangent, "w_qkv": w_qkv, "w_out": w_out, "w_up": w_up, "w_down": w_down, "gain_one": gain_one, "shift_one": shift_one, "gain_two": gain_two, "shift_two": shift_two, "bias_query": bias_query, "bias_value": bias_value, "bias_out": bias_out, "bias_up": bias_up, "bias_down": bias_down}


@jax.custom_vjp
def low(v):
    return lax.optimization_barrier(v.astype(jnp.bfloat16)).astype(jnp.float32)

@jax.custom_vjp
def low_back(v):
    return v

def low_keep(v):
    return (low(v), None)

def low_pass(kept, grad):
    return (grad,)

def back_keep(v):
    return (v, None)

def back_low(kept, grad):
    return (low(grad),)
low.defvjp(low_keep, low_pass)
low_back.defvjp(back_keep, back_low)

def normalize(values, gain, shift):
    centre = values - lax.optimization_barrier(jnp.mean(values, axis=-1, keepdims=True))
    spread = lax.optimization_barrier(jnp.mean(centre * centre, axis=-1, keepdims=True))
    return centre * lax.rsqrt(spread + 1e-06) * gain + shift

def matmul(left, right):
    return jnp.dot(left, right, precision=lax.Precision.HIGHEST)

def attend_image(packed):
    query, keyed, valued, valid = packed
    q_heads = query.reshape(SEQ, HEADS, HEAD_DIM)
    k_heads = keyed.reshape(SEQ, HEADS, HEAD_DIM)
    v_heads = valued.reshape(SEQ, HEADS, HEAD_DIM)
    raw = jnp.einsum('qhd,khd->hqk', q_heads, k_heads, precision=lax.Precision.HIGHEST)
    scores = low_back(raw * HEAD_DIM ** (-0.5))
    scores = jnp.where(valid[None, None, :] > 0, scores, -1e+30)
    probs = low(jax.nn.softmax(scores, axis=-1))
    output = jnp.einsum('hqk,khd->qhd', probs, v_heads, precision=lax.Precision.HIGHEST)
    return output.reshape(SEQ, D)

def reference(patches, patch_mask, cotangent, w_qkv, w_out, w_up, w_down, gain_one, shift_one, gain_two, shift_two, bias_query, bias_value, bias_out, bias_up, bias_down):

    def layer(inputs, wq, wo, wu, wd, gone, sone, gtwo, stwo, bquery, bvalue, bout, bup, bdown):
        tokens = inputs.reshape(IMAGES * SEQ, D)
        normed_one = low(normalize(tokens, gone[0], sone[0]))
        qkv_bias = jnp.concatenate([bquery[0], jnp.zeros((D,), jnp.float32), bvalue[0]])
        projected = low(low_back(matmul(normed_one, wq) + qkv_bias))
        projected = projected.reshape(IMAGES, SEQ, 3 * D)
        attended = lax.map(jax.checkpoint(attend_image), (projected[:, :, :D], projected[:, :, D:2 * D], projected[:, :, 2 * D:], patch_mask))
        attended = low(low_back(attended.reshape(IMAGES * SEQ, D)))
        branch = low_back(matmul(attended, wo) + bout[0])
        middle = tokens + branch
        normed_two = low(normalize(middle, gtwo[0], stwo[0]))
        hidden_pre = low_back(matmul(normed_two, wu) + bup[0])
        activated = low(jax.nn.gelu(hidden_pre, approximate=True))
        mlp_out = low_back(matmul(activated, wd.T) + bdown[0])
        return (middle + mlp_out).reshape(IMAGES, SEQ, D)
    primals = [a.astype(jnp.float32) for a in (patches, w_qkv, w_out, w_up, w_down, gain_one, shift_one, gain_two, shift_two, bias_query, bias_value, bias_out, bias_up, bias_down)]
    output, pullback = jax.vjp(layer, *primals)
    grads = pullback(cotangent.astype(jnp.float32))
    return (output.astype(jnp.bfloat16), grads[0].astype(jnp.bfloat16), grads[1], grads[2], grads[3], grads[4], grads[5], grads[6], grads[7], grads[8], grads[9], grads[10], grads[11], grads[12], grads[13])
```

```python
import functools

import jax
import jax.numpy as jnp
from jax import lax
from jax.experimental import pallas as pl
from jax.experimental.pallas import tpu as pltpu
from jax.sharding import Mesh
from jax.sharding import PartitionSpec as P

HEADS = 16
HEAD_DIM = 72
SCALE = HEAD_DIM ** (-0.5)
Q_BLOCK = 256
F32 = jnp.float32
BF16 = jnp.bfloat16


def dot(left, right):
    return jnp.dot(left, right, preferred_element_type=F32)


def dot_tn(left, right):
    return lax.dot_general(left, right, (((0,), (0,)), ((), ())), preferred_element_type=F32)


def dot_nt(left, right):
    return lax.dot_general(left, right, (((1,), (1,)), ((), ())), preferred_element_type=F32)


def attend_fwd_body(heads, qkv_ref, bias_ref, out_ref, lse_ref):
    width = heads * HEAD_DIM
    begin = pl.program_id(1) * Q_BLOCK
    bias = bias_ref[0]
    lane = lax.broadcasted_iota(jnp.int32, (Q_BLOCK, 128), 1)
    stats = jnp.zeros((Q_BLOCK, 128), F32)
    for head in range(heads):
        low = head * HEAD_DIM
        query = qkv_ref[0, pl.ds(begin, Q_BLOCK), low : low + HEAD_DIM]
        keys = qkv_ref[0, :, width + low : width + low + HEAD_DIM]
        values = qkv_ref[0, :, 2 * width + low : 2 * width + low + HEAD_DIM]
        scores = dot_nt(query, keys) * SCALE + bias
        peak = jnp.max(scores, axis=1, keepdims=True)
        expo = jnp.exp(scores - peak)
        total = jnp.sum(expo, axis=1, keepdims=True)
        mixed = dot(expo.astype(BF16), values) / total
        out_ref[0, :, low : low + HEAD_DIM] = mixed.astype(BF16)
        stats = jnp.where(lane == head, peak + jnp.log(total), stats)
    lse_ref[0] = jnp.transpose(stats)[:8]


def attend_bwd_body(heads, qkv_ref, bias_ref, lse_ref, grad_ref, out_ref, key_acc, value_acc):
    width = heads * HEAD_DIM
    step = pl.program_id(1)
    begin = step * Q_BLOCK
    bias = bias_ref[0]

    @pl.when(step == 0)
    def _():
        key_acc[...] = jnp.zeros_like(key_acc)
        value_acc[...] = jnp.zeros_like(value_acc)

    for head in range(heads):
        low = head * HEAD_DIM
        rows = pl.ds(begin, Q_BLOCK)
        query = qkv_ref[0, rows, low : low + HEAD_DIM]
        grad = grad_ref[0, :, low : low + HEAD_DIM]
        keys = qkv_ref[0, :, width + low : width + low + HEAD_DIM]
        values = qkv_ref[0, :, 2 * width + low : 2 * width + low + HEAD_DIM]
        scores = dot_nt(keys, query) * SCALE + bias
        probs = jnp.exp(scores - lse_ref[0, head : head + 1, :])
        value_acc[head] += dot(probs.astype(BF16), grad)
        grad_probs = dot_nt(values, grad)
        term = jnp.sum(probs * grad_probs, axis=0, keepdims=True)
        grad_scores = (probs * (grad_probs - term)).astype(BF16)
        key_acc[head] += dot(grad_scores, query)
        grad_query = dot_tn(grad_scores, keys) * SCALE
        out_ref[0, rows, low : low + HEAD_DIM] = grad_query.astype(BF16)

    @pl.when(step == pl.num_programs(1) - 1)
    def _():
        for head in range(heads):
            low = head * HEAD_DIM
            out_ref[0, :, width + low : width + low + HEAD_DIM] = (key_acc[head] * SCALE).astype(BF16)
            out_ref[0, :, 2 * width + low : 2 * width + low + HEAD_DIM] = value_acc[head].astype(BF16)


def attend_fwd(qkv, bias, heads):
    images, seq, wide = qkv.shape
    width = heads * HEAD_DIM
    steps = seq // Q_BLOCK
    work = images * heads * seq * seq
    return pl.pallas_call(
        functools.partial(attend_fwd_body, heads),
        name="attend_fwd",
        grid=(images, steps),
        in_specs=[
            pl.BlockSpec((1, seq, wide), lambda i, j: (i, 0, 0)),
            pl.BlockSpec((1, 1, seq), lambda i, j: (i, 0, 0)),
        ],
        out_specs=[
            pl.BlockSpec((1, Q_BLOCK, width), lambda i, j: (i, j, 0)),
            pl.BlockSpec((1, 8, Q_BLOCK), lambda i, j: (i, 0, j)),
        ],
        out_shape=[
            jax.ShapeDtypeStruct((images, seq, width), BF16),
            jax.ShapeDtypeStruct((images, 8, seq), F32),
        ],
        cost_estimate=pl.CostEstimate(
            flops=4 * work * 128, transcendentals=work, bytes_accessed=images * seq * wide * 3
        ),
        compiler_params=pltpu.CompilerParams(vmem_limit_bytes=40 << 20),
    )(qkv, bias)


def attend_bwd(qkv, bias, lse, grad, heads):
    images, seq, wide = qkv.shape
    width = heads * HEAD_DIM
    steps = seq // Q_BLOCK
    work = images * heads * seq * seq
    return pl.pallas_call(
        functools.partial(attend_bwd_body, heads),
        name="attend_bwd",
        grid=(images, steps),
        in_specs=[
            pl.BlockSpec((1, seq, wide), lambda i, j: (i, 0, 0)),
            pl.BlockSpec((1, seq, 1), lambda i, j: (i, 0, 0)),
            pl.BlockSpec((1, 8, Q_BLOCK), lambda i, j: (i, 0, j)),
            pl.BlockSpec((1, Q_BLOCK, width), lambda i, j: (i, j, 0)),
        ],
        out_specs=pl.BlockSpec((1, seq, wide), lambda i, j: (i, 0, 0)),
        out_shape=jax.ShapeDtypeStruct((images, seq, wide), BF16),
        scratch_shapes=[
            pltpu.VMEM((heads, seq, HEAD_DIM), F32),
            pltpu.VMEM((heads, seq, HEAD_DIM), F32),
        ],
        cost_estimate=pl.CostEstimate(
            flops=10 * work * 128, transcendentals=work, bytes_accessed=images * seq * wide * 5
        ),
        compiler_params=pltpu.CompilerParams(vmem_limit_bytes=48 << 20),
    )(qkv, bias, lse, grad)


class Native:
    def __init__(self, sizes, images, tokens):
        self.dev, self.zed, self.why = sizes
        self.images = images
        self.tokens = tokens
        self.team = self.dev * 2
        self.groups = self.zed * self.why
        self.each = images * self.dev // self.groups
        self.piece = tokens // self.dev
        self.rows = self.each * self.groups * self.piece

    def image_ids(self):
        group = lax.axis_index(("z", "y"))
        return group * self.each + jnp.arange(self.each)

    def positions(self):
        shape = (self.team, self.groups, self.piece)
        team = lax.broadcasted_iota(jnp.int32, shape, 0)
        group = lax.broadcasted_iota(jnp.int32, shape, 1)
        place = lax.broadcasted_iota(jnp.int32, shape, 2)
        owner = group * 2 + team % 2
        return (owner * self.tokens + (team // 2) * self.piece + place).reshape(-1)

    def tokens_in(self, values):
        wide = values.shape[-1]
        split = values.reshape(self.images, self.dev, self.piece, wide)
        split = lax.all_to_all(split, "dev", 1, 0, tiled=True)
        split = split.reshape(self.groups, self.each, self.piece, wide)
        split = lax.all_to_all(split, ("z", "y"), 0, 0, tiled=True)
        return split.transpose(1, 0, 2, 3).reshape(self.rows, wide)

    def tokens_out(self, values):
        wide = values.shape[-1]
        split = values.reshape(self.each, self.groups, self.piece, wide).transpose(1, 0, 2, 3)
        split = lax.all_to_all(split, ("z", "y"), 0, 0, tiled=True)
        split = split.reshape(self.dev * self.images, 1, self.piece, wide)
        split = lax.all_to_all(split, "dev", 0, 1, tiled=True)
        return split.reshape(self.images, self.tokens, wide)

    def rows_gather(self, values):
        wide = values.shape[-1]
        whole = lax.all_gather(values, ("dev", "core"), axis=0, tiled=True)
        whole = whole.reshape(self.team, self.each, -1, wide).transpose(1, 0, 2, 3)
        return whole.reshape(self.team * self.rows, wide)

    def rows_scatter(self, values):
        wide = values.shape[-1]
        split = values.astype(BF16).reshape(self.each, self.team, -1, wide).transpose(1, 0, 2, 3)
        split = split.reshape(self.team * self.rows, wide)
        return lax.psum_scatter(
            split, ("dev", "core"), scatter_dimension=0, tiled=True
        ).astype(F32)

    def own_rows(self, values):
        wide = values.shape[-1]
        me = lax.axis_index(("dev", "core"))
        split = values.reshape(self.each, self.team, -1, wide)
        return lax.dynamic_slice_in_dim(split, me, 1, 1).reshape(self.rows, wide)

    def columns_gather(self, values):
        return lax.all_gather(values, ("dev", "core"), axis=1, tiled=True)

    def heads_gather(self, values):
        return self.columns_gather(values)

    def heads_in(self, shard):
        whole = lax.all_gather(shard, "dev", axis=1, tiled=True)
        rows, wide = whole.shape
        split = whole.reshape(rows, 3, self.dev, wide // (3 * self.dev))
        split = lax.dynamic_slice_in_dim(split, lax.axis_index("dev"), 1, 2)
        return split.reshape(rows, 3, wide // (3 * self.dev))

    def heads_out(self, block):
        rows, _, wide = block.shape
        whole = lax.all_gather(block[:, :, None, :], "dev", axis=2, tiled=True)
        whole = whole.reshape(rows, self.dev, 3 * wide)
        return lax.dynamic_slice_in_dim(whole, lax.axis_index("dev"), 1, 1)[:, 0]


def joint(move):
    pairs = []
    for dev in range(2):
        for zed in range(4):
            for why in range(2):
                for core in range(2):
                    to = move(dev, zed, why, core)
                    source = ((dev * 4 + zed) * 2 + why) * 2 + core
                    pairs.append((source, ((to[0] * 4 + to[1]) * 2 + to[2]) * 2 + to[3]))
    return pairs


def send(values, move):
    return lax.ppermute(values, ("dev", "z", "y", "core"), joint(move))


def across(values):
    return send(values, lambda d, z, y, c: (1 - d, z, y, c))


def beside(values):
    return send(values, lambda d, z, y, c: (d, z, y, 1 - c))


class Paired(Native):
    def image_ids(self):
        return (lax.axis_index("y") * 4 + lax.axis_index("z")).reshape(1)

    def positions(self):
        shape = (4, 4, self.tokens)
        block = lax.broadcasted_iota(jnp.int32, shape, 0)
        turn = lax.broadcasted_iota(jnp.int32, shape, 1)
        place = lax.broadcasted_iota(jnp.int32, shape, 2)
        why = lax.axis_index("dev") ^ (block // 2)
        core = lax.axis_index("core") ^ (block % 2)
        zed = (lax.axis_index("z") - turn) % 4
        return (((zed * 2 + why) * 2 + core) * self.tokens + place).reshape(-1)

    def tokens_in(self, values):
        zed = lax.axis_index("z")
        pieces = []
        for turn in range(4):
            piece = lax.dynamic_slice_in_dim(values, (zed + turn) % 4, 1, 0)[0]
            pieces.append(send(piece, lambda d, z, y, c: (y, (z + turn) % 4, d, c)))
        return jnp.concatenate(pieces, axis=0)

    def tokens_out(self, values):
        zed = lax.axis_index("z")
        rows = self.tokens
        pieces = []
        for turn in range(4):
            piece = values[turn * rows : (turn + 1) * rows]
            pieces.append(send(piece, lambda d, z, y, c: (y, (z - turn) % 4, d, c)))
        stacked = jnp.stack(pieces, axis=0)
        order = (jnp.arange(4) - zed) % 4
        return sum(
            jnp.where((order == turn)[:, None, None], stacked[turn][None], 0) for turn in range(4)
        ).astype(values.dtype)

    def rows_gather(self, values):
        far = across(values)
        return jnp.concatenate([values, beside(values), far, beside(far)], axis=0)

    def rows_scatter(self, values):
        rows = self.rows
        near = jnp.concatenate([values[rows : 2 * rows], values[3 * rows :]], axis=0)
        came = beside(near.astype(BF16)).astype(F32)
        held = values[:rows] + came[:rows]
        away = values[2 * rows : 3 * rows] + came[rows:]
        return held + across(away.astype(BF16)).astype(F32)

    def own_rows(self, values):
        return values[: self.rows]

    def heads_gather(self, values):
        return self.columns_gather(values, True)

    def columns_gather(self, values, by_rows=False):
        far = across(values)
        pieces = [values, beside(values), far, beside(far)]
        if by_rows:
            rows = self.rows
            for step in range(1, 4):
                pieces[step] = jnp.concatenate(
                    [pieces[step][(k ^ step) * rows : ((k ^ step) + 1) * rows] for k in range(4)]
                )
        me = lax.axis_index(("dev", "core"))
        ordered = []
        for place in range(4):
            pick = place ^ me
            out = pieces[0]
            for other in range(1, 4):
                out = jnp.where(pick == other, pieces[other], out)
            ordered.append(out)
        return jnp.concatenate(ordered, axis=1)

    def heads_in(self, shard):
        half = shard.shape[1] // 3
        first = lax.axis_index("dev") == 0
        came = across(shard[:, half : 2 * half])
        low, high = shard[:, :half], shard[:, 2 * half :]
        query = jnp.where(first, low, came)
        keys = jnp.where(first, high, low)
        values = jnp.where(first, came, high)
        return jnp.stack([query, keys, values], axis=1)

    def heads_out(self, block):
        first = lax.axis_index("dev") == 0
        query, keys, values = block[:, 0], block[:, 1], block[:, 2]
        came = across(jnp.where(first, values, query))
        return jnp.concatenate(
            [jnp.where(first, query, keys), came, jnp.where(first, keys, values)], axis=1
        )


def core_in(shard):
    return lax.all_to_all(shard, "core", 1, 0, tiled=True)


def core_out(block):
    return lax.all_to_all(block, "core", 0, 1, tiled=True)


def centred(values):
    centre = values - jnp.mean(values, axis=-1, keepdims=True)
    spread = jnp.mean(centre * centre, axis=-1, keepdims=True)
    inverse = lax.rsqrt(spread + 1e-06)
    return centre * inverse, inverse


def norm_back(grad, unit, inverse, gain):
    scaled = grad * gain
    mean = jnp.mean(scaled, axis=-1, keepdims=True)
    along = jnp.mean(scaled * unit, axis=-1, keepdims=True)
    return (scaled - mean - unit * along) * inverse


def gelu_pair(hidden):
    root = 0.7978845608028654
    inner = jnp.tanh(root * (hidden + 0.044715 * hidden * hidden * hidden))
    half = 0.5 * (1.0 + inner)
    slope = half + 0.5 * hidden * (1.0 - inner * inner) * root * (
        1.0 + 3 * 0.044715 * hidden * hidden
    )
    return hidden * half, slope


def per_device(
    sizes,
    patches,
    patch_mask,
    cotangent,
    w_qkv,
    w_out,
    w_up,
    w_down,
    *vectors,
):
    images, tokens, width = patches.shape
    paired = sizes == (2, 4, 2) and images == 4 and Paired is not Native
    route = (Paired if paired else Native)(sizes, images, tokens)
    dev_count = sizes[0]
    team = route.team
    everyone = ("dev", "z", "y", "core")
    plane = ("z", "y")
    dev = lax.axis_index("dev")
    me = lax.axis_index(("dev", "core"))
    head_count = HEADS // team
    block = head_count * HEAD_DIM
    hidden = w_up.shape[1] // 2

    counts = jnp.zeros((dev_count, images), F32)
    counts = lax.dynamic_update_slice(
        counts, jnp.sum(patch_mask, axis=1).astype(F32)[None], (dev, 0)
    )
    lengths = lax.psum(counts.reshape(1, -1), everyone)[0]

    packed = jnp.concatenate(vectors, axis=1)
    if paired:
        other = across(packed)
        lower = jnp.where(dev == 0, packed, other)[0].astype(F32)
        upper = jnp.where(dev == 0, other, packed)[0].astype(F32)
        halves = jnp.stack([lower, upper])
    else:
        halves = lax.all_gather(packed, "dev", axis=0, tiled=True).astype(F32)
    full = []
    spot = 0
    for item in vectors:
        full.append(halves[:, spot : spot + item.shape[1]].reshape(-1))
        spot += item.shape[1]
    gain_one, shift_one, gain_two, shift_two = full[:4]
    bias_query, bias_value, bias_out, bias_up, bias_down = full[4:]

    own_in = route.tokens_in(patches)
    rows_in = route.rows_gather(own_in)

    qkv_shard = route.heads_in(w_qkv)
    parts = qkv_shard.shape[2] // 2
    qkv_shard = core_in(
        qkv_shard.reshape(-1, 3, 2, parts).transpose(0, 2, 1, 3).reshape(-1, 6 * parts)
    )
    own_qkv = lax.all_gather(qkv_shard, plane, axis=0, tiled=True)
    shards = [core_in(w_out), core_in(w_up), core_in(w_down)]
    rest = lax.all_gather(jnp.concatenate(shards, axis=1), plane, axis=0, tiled=True)
    column_out = rest[:, :block]
    own_up = rest[:, block : block + hidden]
    own_down = rest[:, block + hidden :]
    full_out = route.columns_gather(column_out)
    rows_out = lax.dynamic_slice_in_dim(full_out, me * block, block, 0)

    own_grad = route.tokens_in(cotangent)
    rows_grad = route.rows_gather(own_grad)

    inputs = rows_in.astype(F32)
    unit_one, inverse_one = centred(inputs)
    normed_one = (unit_one * gain_one + shift_one).astype(BF16)
    qkv_bias = jnp.concatenate(
        [
            lax.dynamic_slice_in_dim(bias_query, me * block, block),
            jnp.zeros((block,), F32),
            lax.dynamic_slice_in_dim(bias_value, me * block, block),
        ]
    )
    projected = (dot(normed_one, own_qkv) + qkv_bias).astype(BF16)
    seq = projected.shape[0] // route.each
    projected = projected.reshape(route.each, seq, 3 * block)
    own_lengths = lengths[route.image_ids()]
    valid = route.positions()[None, :].astype(F32) < own_lengths[:, None]
    mask_bias = jnp.where(valid, 0.0, -1e30).astype(F32)
    attended, lse = attend_fwd(projected, mask_bias[:, None, :], head_count)
    all_attended = route.heads_gather(attended.reshape(-1, block))
    middle = inputs + dot(all_attended, full_out) + bias_out
    unit_two, inverse_two = centred(middle)
    normed_two = (unit_two * gain_two + shift_two).astype(BF16)
    up_bias = lax.dynamic_slice_in_dim(bias_up, me * hidden, hidden)
    hidden_pre = dot(normed_two, own_up) + up_bias
    active, slope = gelu_pair(hidden_pre)
    active = active.astype(BF16)

    grad_active = dot(rows_grad, own_down)
    grad_hidden = (grad_active * slope).astype(BF16)
    grad_normed_two = route.rows_scatter(dot_nt(grad_hidden, own_up))
    own_unit_two = route.own_rows(unit_two)
    own_inverse_two = route.own_rows(inverse_two)
    grad_middle = own_grad.astype(F32) + norm_back(
        grad_normed_two, own_unit_two, own_inverse_two, gain_two
    )
    own_branch = grad_middle.astype(BF16)
    grad_branch = route.rows_gather(own_branch)

    mlp_part = route.rows_scatter(dot_nt(active, own_down))
    result = (route.own_rows(middle) + mlp_part + bias_down).astype(BF16)
    result = route.tokens_out(result)

    grad_down = dot_tn(rows_grad, active)
    grad_up = dot_tn(normed_two, grad_hidden)

    grad_attended = dot_nt(grad_branch, rows_out).astype(BF16)
    grad_projected = attend_bwd(
        projected,
        mask_bias[:, :, None],
        lse,
        grad_attended.reshape(route.each, seq, block),
        head_count,
    ).reshape(-1, 3 * block)
    grad_normed_one = route.rows_scatter(dot_nt(grad_projected, own_qkv))
    own_unit_one = route.own_rows(unit_one)
    grad_inputs = grad_middle + norm_back(
        grad_normed_one, own_unit_one, route.own_rows(inverse_one), gain_one
    )
    grad_patches = route.tokens_out(grad_inputs.astype(BF16))

    my_branch = lax.dynamic_slice_in_dim(grad_branch, me * block, block, 1)
    grad_out = dot_tn(all_attended, my_branch)
    grad_qkv = dot_tn(normed_one, grad_projected)

    def summed(values):
        return lax.psum_scatter(values.astype(BF16), plane, scatter_dimension=0, tiled=True)

    sum_mlp = summed(jnp.concatenate([grad_down, grad_up], axis=1))
    sum_attn = summed(jnp.concatenate([grad_out, grad_qkv], axis=1))
    out_down = core_out(sum_mlp[:, :hidden]).astype(F32)
    out_up = core_out(sum_mlp[:, hidden:]).astype(F32)
    out_out = core_out(sum_attn[:, :block]).astype(F32)
    piece = core_out(sum_attn[:, block:])
    piece = piece.reshape(-1, 2, 3, block).transpose(0, 2, 1, 3).reshape(-1, 3, 2 * block)
    out_qkv = route.heads_out(piece).astype(F32)

    def spread(values, size):
        return lax.dynamic_update_slice(
            jnp.zeros((size,), F32), values, (me * values.shape[0],)
        )

    proj_sums = jnp.sum(grad_projected.astype(F32), axis=0)
    sums = [
        jnp.sum(grad_normed_one * own_unit_one, axis=0),
        jnp.sum(grad_normed_one, axis=0),
        jnp.sum(grad_normed_two * own_unit_two, axis=0),
        jnp.sum(grad_normed_two, axis=0),
        spread(proj_sums[:block], width),
        spread(proj_sums[2 * block :], width),
        jnp.sum(own_branch.astype(F32), axis=0),
        spread(jnp.sum(grad_hidden.astype(F32), axis=0), hidden * team),
        jnp.sum(cotangent.astype(F32), axis=(0, 1)),
    ]
    flat = lax.psum(jnp.concatenate(sums)[None], everyone)
    out_vectors = []
    spot = 0
    for item in sums:
        size = item.shape[0]
        half = size // dev_count
        out_vectors.append(lax.dynamic_slice(flat, (0, spot + dev * half), (1, half)))
        spot += size
    return (result, grad_patches, out_qkv, out_out, out_up, out_down, *out_vectors)


def solution(mesh):
    dev_count, sa_count = mesh.devices.shape

    def whole(*args):
        zed = args[0].shape[0] // dev_count
        why = sa_count // (2 * zed)
        sizes = (dev_count, zed, why)
        inner = Mesh(mesh.devices.reshape(dev_count, zed, why, 2), ("dev", "z", "y", "core"))
        rows = ("z", "y", "core")
        token = P("dev", rows, None)
        weight = P(rows, "dev")
        vector = P(None, "dev")
        return jax.shard_map(
            functools.partial(per_device, sizes),
            mesh=inner,
            in_specs=(token, P("dev", rows), token) + (weight,) * 4 + (vector,) * 9,
            out_specs=(token, token) + (weight,) * 4 + (vector,) * 9,
            check_vma=False,
        )(*args)

    return whole
```

```python
import functools

import jax
import jax.numpy as jnp
from jax import lax
from jax.experimental import pallas as pl
from jax.experimental.pallas import tpu as pltpu
from jax.experimental.layout import Layout, with_layout_constraint
from jax.sharding import Mesh
from jax.sharding import PartitionSpec as P

HEADS = 16
HEAD_DIM = 72
SCALE = HEAD_DIM ** (-0.5)
Q_BLOCK = 256
F32 = jnp.float32
BF16 = jnp.bfloat16


def dot(left, right):
    return jnp.dot(left, right, preferred_element_type=F32)


def dot_tn(left, right):
    return lax.dot_general(left, right, (((0,), (0,)), ((), ())), preferred_element_type=F32)


def dot_nt(left, right):
    return lax.dot_general(left, right, (((1,), (1,)), ((), ())), preferred_element_type=F32)


def row_major(values):
    return with_layout_constraint(values, Layout(tuple(range(values.ndim))))


def after(value, *others):
    if not others:
        return value
    return lax.optimization_barrier((value, *others))[0]


def attend_fwd_body(heads, qkv_ref, bias_ref, out_ref, lse_ref):
    width = heads * HEAD_DIM
    rows = pl.ds(pl.program_id(1) * Q_BLOCK, Q_BLOCK)
    bias = bias_ref[0]
    for head in range(heads):
        low = head * HEAD_DIM
        query = qkv_ref[0, rows, low : low + HEAD_DIM]
        keys = qkv_ref[0, :, width + low : width + low + HEAD_DIM]
        values = qkv_ref[0, :, 2 * width + low : 2 * width + low + HEAD_DIM]
        scores = dot_nt(keys, query) * SCALE + bias
        peak = jnp.max(scores, axis=0, keepdims=True)
        expo = jnp.exp(scores - peak)
        total = jnp.sum(expo, axis=0, keepdims=True)
        mixed = dot_tn(values, expo.astype(BF16)) / total
        out_ref[0, low : low + HEAD_DIM, :] = mixed.astype(BF16)
        lse_ref[0, head : head + 1, :] = peak + jnp.log(total)
    if heads < 8:
        lse_ref[0, heads:, :] = jnp.zeros((8 - heads, Q_BLOCK), F32)


def attend_bwd_body(
    heads, qkv_ref, bias_ref, lse_ref, branch_ref, w_ref, out_ref, key_acc, value_acc, grad_ref
):
    width = heads * HEAD_DIM
    step = pl.program_id(1)
    begin = step * Q_BLOCK
    bias = bias_ref[0]

    @pl.when(step == 0)
    def _():
        key_acc[...] = jnp.zeros_like(key_acc)
        value_acc[...] = jnp.zeros_like(value_acc)

    grad_ref[...] = dot_nt(branch_ref[0], w_ref[...]).astype(BF16)
    for head in range(heads):
        low = head * HEAD_DIM
        rows = pl.ds(begin, Q_BLOCK)
        query = qkv_ref[0, rows, low : low + HEAD_DIM]
        grad = grad_ref[:, low : low + HEAD_DIM]
        keys = qkv_ref[0, :, width + low : width + low + HEAD_DIM]
        values = qkv_ref[0, :, 2 * width + low : 2 * width + low + HEAD_DIM]
        scores = dot_nt(keys, query) * SCALE + bias
        probs = jnp.exp(scores - lse_ref[0, head : head + 1, :])
        value_acc[head] += dot(probs.astype(BF16), grad)
        grad_probs = dot_nt(values, grad)
        term = jnp.sum(probs * grad_probs, axis=0, keepdims=True)
        grad_scores = (probs * (grad_probs - term)).astype(BF16)
        key_acc[head] += dot(grad_scores, query)
        grad_query = dot_tn(grad_scores, keys) * SCALE
        out_ref[0, rows, low : low + HEAD_DIM] = grad_query.astype(BF16)

    @pl.when(step == pl.num_programs(1) - 1)
    def _():
        for head in range(heads):
            low = head * HEAD_DIM
            out_ref[0, :, width + low : width + low + HEAD_DIM] = (key_acc[head] * SCALE).astype(BF16)
            out_ref[0, :, 2 * width + low : 2 * width + low + HEAD_DIM] = value_acc[head].astype(BF16)


def run(body, name, steps, operands, specs, outs, out_specs, flops, scratch=(), pick=None):
    size = sum(item.size * item.dtype.itemsize for item in operands)
    picks = () if pick is None else (pick,)
    return pl.pallas_call(
        body,
        name=name,
        grid_spec=pltpu.PrefetchScalarGridSpec(
            num_scalar_prefetch=len(picks),
            grid=steps,
            in_specs=specs,
            out_specs=out_specs,
            scratch_shapes=scratch,
        ),
        out_shape=outs,
        cost_estimate=pl.CostEstimate(flops=flops, transcendentals=0, bytes_accessed=size),
        compiler_params=pltpu.CompilerParams(vmem_limit_bytes=50 << 20),
    )(*picks, *operands)


def rows_spec(wide):
    return pl.BlockSpec((Q_BLOCK, wide), lambda i, *_: (i, 0))


def fixed(item):
    shape = item.shape
    return pl.BlockSpec(shape, lambda *_: (0,) * len(shape))


def picked(item, wide):
    return pl.BlockSpec((item.shape[0], wide), lambda i, pick: (0, pick[0]))


def shaped(shape, dtype):
    return jax.ShapeDtypeStruct(shape, dtype)


def attend_fwd(qkv, bias, heads):
    images, seq, wide = qkv.shape
    width = heads * HEAD_DIM
    return run(
        functools.partial(attend_fwd_body, heads),
        "attend_fwd",
        (images, seq // Q_BLOCK),
        (qkv, bias),
        [
            pl.BlockSpec((1, seq, wide), lambda i, j: (i, 0, 0)),
            pl.BlockSpec((1, seq, 1), lambda i, j: (i, 0, 0)),
        ],
        [shaped((images, width, seq), BF16), shaped((images, 8, seq), F32)],
        [
            pl.BlockSpec((1, width, Q_BLOCK), lambda i, j: (i, 0, j)),
            pl.BlockSpec((1, 8, Q_BLOCK), lambda i, j: (i, 0, j)),
        ],
        4 * images * heads * seq * seq * 128,
    )


def attend_bwd(qkv, bias, lse, branch, w_rows, heads):
    images, seq, wide = qkv.shape
    return run(
        functools.partial(attend_bwd_body, heads),
        "attend_bwd",
        (images, seq // Q_BLOCK),
        (qkv, bias, lse, branch, w_rows),
        [
            pl.BlockSpec((1, seq, wide), lambda i, j: (i, 0, 0)),
            pl.BlockSpec((1, seq, 1), lambda i, j: (i, 0, 0)),
            pl.BlockSpec((1, 8, Q_BLOCK), lambda i, j: (i, 0, j)),
            pl.BlockSpec((1, Q_BLOCK, branch.shape[2]), lambda i, j: (i, j, 0)),
            fixed(w_rows),
        ],
        shaped((images, seq, wide), BF16),
        pl.BlockSpec((1, seq, wide), lambda i, j: (i, 0, 0)),
        10 * images * heads * seq * seq * 128,
        [
            pltpu.VMEM((heads, seq, HEAD_DIM), F32),
            pltpu.VMEM((heads, seq, HEAD_DIM), F32),
            pltpu.VMEM((Q_BLOCK, heads * HEAD_DIM), BF16),
        ],
    )


def centred(values):
    centre = values - jnp.mean(values, axis=-1, keepdims=True)
    spread = jnp.mean(centre * centre, axis=-1, keepdims=True)
    inverse = lax.rsqrt(spread + 1e-06)
    return centre * inverse, inverse


def project(pick, rows_all, gain, shift, weight, block, bias):
    count, width = rows_all.shape[0], gain.shape[1]
    wide = bias.shape[1]

    def body(_, rows_ref, gain_ref, shift_ref, weight_ref, bias_ref, normed_ref, out_ref):
        unit = centred(rows_ref[:, :width].astype(F32))[0]
        normed = (unit * gain_ref[...] + shift_ref[...]).astype(BF16)
        normed_ref[...] = normed
        out_ref[...] = (dot(normed, weight_ref[:, :wide]) + bias_ref[...]).astype(BF16)

    operands = (rows_all, gain, shift, weight, bias)
    return run(
        body,
        "project",
        (count // Q_BLOCK,),
        operands,
        [rows_spec(rows_all.shape[1]), fixed(gain), fixed(shift), picked(weight, block), fixed(bias)],
        [shaped((count, width), BF16), shaped((count, wide), BF16)],
        [rows_spec(width), rows_spec(wide)],
        2 * count * width * wide,
        pick=pick,
    )


def attend_out(pieces, weights, rows_all, bias, gain, shift):
    count, width = rows_all.shape[0], gain.shape[1]
    total = len(pieces)
    piece = pieces[0].shape[0]

    def body(*refs):
        piece_refs = refs[:total]
        weight_ref, rows_ref, bias_ref, gain_ref, shift_ref = refs[total:-2]
        middle_ref, normed_ref = refs[-2:]
        branch = dot_tn(piece_refs[0][...], weight_ref[0])
        for k in range(1, total):
            branch += dot_tn(piece_refs[k][...], weight_ref[k])
        middle = rows_ref[:, :width].astype(F32) + (branch + bias_ref[...])
        middle_ref[...] = middle
        normed_ref[...] = (centred(middle)[0] * gain_ref[...] + shift_ref[...]).astype(BF16)

    return run(
        body,
        "attend_out",
        (count // Q_BLOCK,),
        (*pieces, weights, rows_all, bias, gain, shift),
        [pl.BlockSpec((piece, Q_BLOCK), lambda i: (0, i))] * total
        + [fixed(weights), rows_spec(rows_all.shape[1])]
        + [fixed(bias), fixed(gain), fixed(shift)],
        [shaped((count, width), F32), shaped((count, width), BF16)],
        [rows_spec(width), rows_spec(width)],
        2 * count * width * width,
    )


def mlp_turn(pick, normed, grad, mlp, bias):
    count, width = normed.shape
    hidden = bias.shape[1]

    def body(_, normed_ref, grad_ref, mlp_ref, bias_ref, active_ref, slope_ref, back_ref, sums_ref):
        pre = dot(normed_ref[...], mlp_ref[:, :hidden]) + bias_ref[...]
        active, slope = gelu_pair(pre)
        active_ref[...] = active.astype(BF16)
        grad_hidden = (dot(grad_ref[...], mlp_ref[:, hidden : 2 * hidden]) * slope).astype(BF16)
        slope_ref[...] = grad_hidden
        back_ref[...] = dot_nt(grad_hidden, mlp_ref[:, :hidden]).astype(BF16)
        sums = jnp.sum(grad_hidden.astype(F32), axis=0, keepdims=True)

        @pl.when(pl.program_id(0) == 0)
        def _():
            sums_ref[...] = sums

        @pl.when(pl.program_id(0) > 0)
        def _():
            sums_ref[...] += sums

    return run(
        body,
        "mlp_turn",
        (count // Q_BLOCK,),
        (normed, grad, mlp, bias),
        [rows_spec(width), rows_spec(width), picked(mlp, 2 * hidden), fixed(bias)],
        [
            shaped((count, hidden), BF16),
            shaped((count, hidden), BF16),
            shaped((count, width), BF16),
            shaped((1, hidden), F32),
        ],
        [rows_spec(hidden), rows_spec(hidden), rows_spec(width), fixed(bias)],
        6 * count * width * hidden,
        pick=pick,
    )


def mlp_out(pick, active, mlp):
    count, hidden = active.shape
    width = mlp.shape[0]

    def body(_, active_ref, mlp_ref, out_ref):
        out_ref[...] = dot_nt(active_ref[...], mlp_ref[:, hidden : 2 * hidden]).astype(BF16)

    return run(
        body,
        "mlp_out",
        (count // Q_BLOCK,),
        (active, mlp),
        [rows_spec(hidden), picked(mlp, 2 * hidden)],
        shaped((count, width), BF16),
        rows_spec(width),
        2 * count * width * hidden,
        pick=pick,
    )


def weight_grads(lefts, rights, name):
    count, width = lefts[0].shape
    wides = [item.shape[1] for item in rights]
    tile = 384
    total = len(lefts)

    def body(*refs):
        out_ref = refs[-1]
        spot = 0
        for k in range(total):
            product = dot_tn(refs[k][...], refs[total + k][...])
            out_ref[:, spot : spot + wides[k]] = product.astype(BF16)
            spot += wides[k]

    return run(
        body,
        name,
        (width // tile,),
        (*lefts, *rights),
        [pl.BlockSpec((count, tile), lambda i, *_: (0, i))] * total + [fixed(item) for item in rights],
        shaped((width, sum(wides)), BF16),
        pl.BlockSpec((tile, sum(wides)), lambda i: (i, 0)),
        2 * count * width * sum(wides),
    )


def out_grads(pieces, branch):
    total = len(pieces)
    piece = pieces[0].shape[0]
    wide = branch.shape[1]

    def body(*refs):
        for k in range(total):
            product = dot(refs[k][...], refs[total][...])
            refs[-1][k * piece : (k + 1) * piece, :] = product.astype(BF16)

    operands = (*pieces, branch)
    out = shaped((total * piece, wide), BF16)
    return run(
        body,
        "out_grads",
        (1,),
        operands,
        [fixed(item) for item in operands],
        out,
        fixed(out),
        2 * branch.shape[0] * total * piece * wide,
    )


def project_back(pick, grad, weight, block, rows_all, width):
    count, wide = grad.shape

    def body(_, grad_ref, weight_ref, rows_ref, back_ref, norm_ref, bias_ref):
        back = dot_nt(grad_ref[...], weight_ref[:, :wide])
        back_ref[...] = back.astype(BF16)
        unit = centred(rows_ref[:, :width].astype(F32))[0]
        gain = jnp.sum(back * unit, axis=0, keepdims=True)
        shift = jnp.sum(back, axis=0, keepdims=True)
        bias = jnp.sum(grad_ref[...].astype(F32), axis=0, keepdims=True)

        @pl.when(pl.program_id(0) == 0)
        def _():
            norm_ref[...] = jnp.zeros_like(norm_ref)
            bias_ref[...] = jnp.zeros_like(bias_ref)

        norm_ref[0:1] += gain
        norm_ref[1:2] += shift
        bias_ref[...] += bias

    return run(
        body,
        "project_back",
        (count // Q_BLOCK,),
        (grad, weight, rows_all),
        [rows_spec(wide), picked(weight, block), rows_spec(rows_all.shape[1])],
        [shaped((count, width), BF16), shaped((2, width), F32), shaped((1, wide), F32)],
        [
            rows_spec(width),
            pl.BlockSpec((2, width), lambda *_: (0, 0)),
            pl.BlockSpec((1, wide), lambda *_: (0, 0)),
        ],
        2 * count * width * wide,
        pick=pick,
    )


class Native:
    def __init__(self, sizes, images, tokens):
        self.dev, self.zed, self.why = sizes
        self.images = images
        self.tokens = tokens
        self.team = self.dev * 2
        self.groups = self.zed * self.why
        self.each = images * self.dev // self.groups
        self.piece = tokens // self.dev
        self.rows = self.each * self.groups * self.piece

    def positions(self, row):
        place = row % self.piece
        group = (row // self.piece) % self.groups
        team = row // (self.piece * self.groups)
        owner = group * 2 + team % 2
        return owner * self.tokens + (team // 2) * self.piece + place

    def tokens_in(self, values):
        wide = values.shape[-1]
        split = values.reshape(self.images, self.dev, self.piece, wide)
        split = lax.all_to_all(split, "dev", 1, 0, tiled=True)
        split = split.reshape(self.groups, self.each, self.piece, wide)
        split = lax.all_to_all(split, ("z", "y"), 0, 0, tiled=True)
        return split.transpose(1, 0, 2, 3).reshape(self.rows, wide)

    def tokens_out(self, values):
        wide = values.shape[-1]
        split = values.reshape(self.each, self.groups, self.piece, wide).transpose(1, 0, 2, 3)
        split = lax.all_to_all(split, ("z", "y"), 0, 0, tiled=True)
        split = split.reshape(self.dev * self.images, 1, self.piece, wide)
        split = lax.all_to_all(split, "dev", 0, 1, tiled=True)
        return split.reshape(self.images, self.tokens, wide)

    def rows_gather(self, values, *gates):
        wide = values.shape[-1]
        whole = lax.all_gather(values, ("dev", "core"), axis=0, tiled=True)
        whole = whole.reshape(self.team, self.each, -1, wide).transpose(1, 0, 2, 3)
        return whole.reshape(self.team * self.rows, wide)

    def rows_scatter(self, values):
        wide = values.shape[-1]
        split = values.astype(BF16).reshape(self.each, self.team, -1, wide).transpose(1, 0, 2, 3)
        split = split.reshape(self.team * self.rows, wide)
        return lax.psum_scatter(
            split, ("dev", "core"), scatter_dimension=0, tiled=True
        ).astype(F32)

    def rows_near(self, values):
        return values, values

    def rows_end(self, sums):
        return self.rows_scatter(sums[0])

    def own_rows(self, values):
        wide = values.shape[-1]
        me = lax.axis_index(("dev", "core"))
        split = values.reshape(self.each, self.team, -1, wide)
        return lax.dynamic_slice_in_dim(split, me, 1, 1).reshape(self.rows, wide)

    def heads_gather(self, values):
        return [lax.all_gather(values, ("dev", "core"), axis=0, tiled=True)], [[0]]

    def weights(self, w_qkv, w_out, mlp, packed, *gates):
        whole = lax.all_gather(w_qkv, "dev", axis=1, tiled=True)
        rows, wide = whole.shape
        split = whole.reshape(rows, 3, self.team, wide // (3 * self.team))
        split = lax.dynamic_slice_in_dim(split, 2 * lax.axis_index("dev"), 2, 2)
        split = split.transpose(0, 2, 1, 3).reshape(rows, -1)
        split = lax.all_to_all(split, "core", 1, 0, tiled=True)
        full_qkv = lax.all_gather(split, ("z", "y"), axis=0, tiled=True)
        full_out = lax.all_gather(w_out, "dev", axis=1, tiled=True)
        full_out = lax.all_gather(full_out, ("z", "y", "core"), axis=0, tiled=True)
        mlp = jnp.concatenate(mlp, axis=1)
        mlp = lax.all_to_all(mlp, "core", 1, 0, tiled=True)
        mlp = lax.all_gather(mlp, ("z", "y"), axis=0, tiled=True)
        vectors = lax.all_gather(packed, "dev", axis=0, tiled=True)
        return full_qkv, full_qkv.shape[1], full_out, mlp, jnp.zeros((1,), jnp.int32), vectors

    def mlp_grads(self, grads):
        return lax.psum_scatter(grads, ("z", "y"), scatter_dimension=0, tiled=True)

    def mlp_halves(self, grads):
        grads = lax.all_to_all(grads, "core", 0, 1, tiled=True).astype(F32)
        half = grads.shape[1] // 2
        return grads[:, :half], grads[:, half:]

    def attention_grads(self, grad_qkv, grad_out, *gates):
        both = jnp.concatenate([grad_out, grad_qkv], axis=1)
        both = lax.psum_scatter(both, ("z", "y"), scatter_dimension=0, tiled=True)
        block = grad_out.shape[1]
        out = lax.all_to_all(both[:, :block], "core", 0, 1, tiled=True)
        piece = lax.all_to_all(both[:, block:], "core", 0, 1, tiled=True)
        rows = piece.shape[0]
        piece = piece.reshape(rows, 2, 3, block).transpose(0, 2, 1, 3).reshape(rows, 3, 1, -1)
        whole = lax.all_gather(piece, "dev", axis=2, tiled=True)
        whole = whole.reshape(rows, self.dev, 6 * block)
        mine = lax.dynamic_slice_in_dim(whole, lax.axis_index("dev"), 1, 1)[:, 0]
        return mine.astype(F32), out.astype(F32)

    def total(self, values):
        return lax.psum(values, ("dev", "z", "y", "core"))


def joint(move):
    pairs = []
    for dev in range(2):
        for zed in range(4):
            for why in range(2):
                for core in range(2):
                    to = move(dev, zed, why, core)
                    source = ((dev * 4 + zed) * 2 + why) * 2 + core
                    pairs.append((source, ((to[0] * 4 + to[1]) * 2 + to[2]) * 2 + to[3]))
    return pairs


def send(values, move):
    return lax.ppermute(values, ("dev", "z", "y", "core"), joint(move))


def across(values):
    return send(values, lambda d, z, y, c: (1 - d, z, y, c))


def beside(values):
    return send(values, lambda d, z, y, c: (d, z, y, 1 - c))


class Paired(Native):
    def positions(self, row):
        place = row % self.tokens
        turn = (row // self.tokens) % 4
        team = row // (self.tokens * 4)
        zed = (lax.axis_index("z") - turn) % 4
        return ((zed * 2 + team // 2) * 2 + team % 2) * self.tokens + place

    def tokens_in(self, values):
        zed = lax.axis_index("z")
        pieces = []
        for turn in range(4):
            piece = lax.dynamic_slice_in_dim(values, (zed + turn) % 4, 1, 0)[0]
            pieces.append(send(piece, lambda d, z, y, c: (y, (z + turn) % 4, d, c)))
        return jnp.concatenate(pieces, axis=0)

    def tokens_out(self, values):
        zed = lax.axis_index("z")
        rows = self.tokens
        pieces = []
        for turn in range(4):
            piece = values[turn * rows : (turn + 1) * rows]
            pieces.append(send(piece, lambda d, z, y, c: (y, (z - turn) % 4, d, c)))
        order = (jnp.arange(4) - zed) % 4
        result = pieces[0][None]
        for turn in range(1, 4):
            result = jnp.where((order == turn)[:, None, None], pieces[turn][None], result)
        return result

    def rows_gather(self, values, *gates):
        me = lax.axis_index(("dev", "core"))
        rows, wide = values.shape
        mine = jnp.concatenate([values, after(across(values), *gates)], axis=0)
        whole = jnp.zeros((4 * rows, wide), values.dtype)
        for step, pair in enumerate((mine, beside(mine))):
            for far in range(2):
                piece = pair[far * rows : (far + 1) * rows]
                whole = lax.dynamic_update_slice(whole, piece, ((me ^ (step + 2 * far)) * rows, 0))
        return whole

    def rows_scatter(self, values):
        return self.rows_end(self.rows_near(values))

    def rows_near(self, values):
        rows = self.rows
        me = lax.axis_index(("dev", "core"))

        def part(step):
            return lax.dynamic_slice_in_dim(values, (me ^ step) * rows, rows, 0)

        near = jnp.concatenate([part(1), part(3)], axis=0)
        came = beside(near.astype(BF16)).astype(F32)
        return part(0) + came[:rows], (part(2) + came[rows:]).astype(BF16)

    def rows_end(self, sums):
        return sums[0] + across(sums[1]).astype(F32)

    def own_rows(self, values):
        me = lax.axis_index(("dev", "core"))
        return lax.dynamic_slice_in_dim(values, me * self.rows, self.rows, 0)

    def heads_gather(self, values):
        me = lax.axis_index(("dev", "core"))
        mine = jnp.concatenate([values, across(values)], axis=0)
        pieces = [mine, beside(mine)]
        block = values.shape[0]
        spots = [[(me ^ (step + 2 * far)) * block for far in range(2)] for step in range(2)]
        return pieces, spots

    def weights(self, w_qkv, w_out, mlp, packed, *gates):
        third = w_qkv.shape[1] // 3
        half = third // 2
        wide = w_out.shape[1]
        count = packed.shape[1]
        first = lax.axis_index("dev") == 0
        lines = -(-count // ((third + wide) * 8)) * 8
        sheet = jnp.pad(packed[0], (0, lines * (third + wide) - count)).reshape(lines, -1)
        message = jnp.concatenate([w_qkv[:, third : 2 * third], w_out], axis=1)
        came = across(jnp.concatenate([message, sheet], axis=0))
        rows = w_qkv.shape[0]
        vectors = came[rows:].reshape(1, -1)[:, :count]
        vectors = jnp.concatenate(
            [jnp.where(first, packed, vectors), jnp.where(first, vectors, packed)], axis=0
        )
        came_qkv, came_out = came[:rows, :third], came[:rows, third:]
        low, high = w_qkv[:, :third], w_qkv[:, 2 * third :]
        query = jnp.where(first, low, came_qkv)
        keys = jnp.where(first, high, low)
        values = jnp.where(first, came_qkv, high)
        blocks = [
            jnp.concatenate(
                [item[:, side * half : (side + 1) * half] for item in (query, keys, values)], axis=1
            )
            for side in range(2)
        ]
        block = -(-3 * half // 128) * 128
        blocks = [jnp.pad(item, ((0, 0), (0, block - 3 * half))) for item in blocks]
        everyone = ("z", "y", "core")
        full_qkv = lax.all_gather(jnp.concatenate(blocks, axis=1), everyone, axis=0, tiled=True)
        outs = [jnp.where(first, w_out, came_out), jnp.where(first, came_out, w_out)]
        rest = after(jnp.concatenate([*mlp, *outs], axis=1), full_qkv, *gates)
        rest = lax.all_gather(rest, everyone, axis=0, tiled=True)
        pick = lax.axis_index("core").reshape(1)
        return full_qkv, block, rest[:, 2 * mlp[0].shape[1] :], rest, pick, vectors

    def turned(self):
        me = lax.axis_index(("dev", "core"))
        return [((k ^ me) % 2) * 2 + (k ^ me) // 2 for k in range(4)]

    def halve(self, block):
        upper = lax.axis_index("core") == 0
        rows = block.shape[0] // 2
        low, high = block[:rows], block[rows:]
        keep = jnp.where(upper, low, high)
        got = beside(jnp.where(upper, high, low).astype(BF16)).astype(F32)
        return jnp.where(upper, keep, got), jnp.where(upper, got, keep)

    def mlp_grads(self, grads):
        return lax.psum_scatter(grads, ("z", "y"), scatter_dimension=0, tiled=True)

    def mlp_halves(self, grads):
        return self.halve(grads.astype(F32))

    def attention_grads(self, grad_qkv, grad_out, *gates):
        block = grad_out.shape[1]
        rows = grad_qkv.shape[0] // 8
        first = lax.axis_index("dev") == 0
        order = grad_out.reshape(4, 2 * rows, block)
        order = jnp.stack([lax.dynamic_index_in_dim(order, k, 0, False) for k in self.turned()])
        both = jnp.concatenate([order.reshape(8 * rows, block), grad_qkv], axis=1)
        both = lax.psum_scatter(after(both, *gates), ("z", "y"), scatter_dimension=0, tiled=True)
        left, right = self.halve(both.astype(F32))
        out = jnp.concatenate([left[:, :block], right[:, :block]], axis=1)
        query, keys, values = (
            jnp.concatenate([left[:, k * block : (k + 1) * block], right[:, k * block : (k + 1) * block]], axis=1)
            for k in (1, 2, 3)
        )
        came = across(jnp.where(first, values, query).astype(BF16)).astype(F32)
        return (
            jnp.concatenate(
                [jnp.where(first, query, keys), came, jnp.where(first, keys, values)], axis=1
            ),
            out,
        )

    def total(self, values):
        everyone = ("dev", "z", "y", "core")
        wide = values.shape[1]
        each = -(-wide // (32 * 128)) * 128
        parts = jnp.pad(values[0], (0, 32 * each - wide)).reshape(32, each)
        parts = lax.all_to_all(parts, everyone, 0, 0, tiled=True)
        mine = jnp.sum(parts, axis=0, keepdims=True)
        every = jnp.broadcast_to(mine, (32, each))
        return lax.all_to_all(every, everyone, 0, 0, tiled=True).reshape(1, -1)[:, :wide]


def norm_back(grad, unit, inverse, gain):
    scaled = grad * gain
    mean = jnp.mean(scaled, axis=-1, keepdims=True)
    along = jnp.mean(scaled * unit, axis=-1, keepdims=True)
    return (scaled - mean - unit * along) * inverse


def gelu_pair(hidden):
    root = 0.7978845608028654
    inner = jnp.tanh(root * (hidden + 0.044715 * hidden * hidden * hidden))
    half = 0.5 * (1.0 + inner)
    slope = half + 0.5 * hidden * (1.0 - inner * inner) * root * (
        1.0 + 3 * 0.044715 * hidden * hidden
    )
    return hidden * half, slope


def per_device(
    sizes,
    patches,
    patch_mask,
    cotangent,
    w_qkv,
    w_out,
    w_up,
    w_down,
    *vectors,
):
    images, tokens, width = patches.shape
    paired = sizes == (2, 4, 2) and images == 4 and Paired is not Native
    route = (Paired if paired else Native)(sizes, images, tokens)
    dev_count = sizes[0]
    team = route.team
    dev = lax.axis_index("dev")
    me = lax.axis_index(("dev", "core"))
    head_count = HEADS // team
    block = head_count * HEAD_DIM
    hidden = w_up.shape[1] // 2

    padded = -(-hidden // 128) * 128
    sides = [
        jnp.concatenate(
            [
                jnp.pad(item[:, side * hidden : (side + 1) * hidden], ((0, 0), (0, padded - hidden)))
                for item in (w_up, w_down)
            ],
            axis=1,
        )
        for side in range(2)
    ]
    marks = jnp.broadcast_to(patch_mask.astype(BF16)[:, :, None], (images, tokens, 128))
    own_in = route.tokens_in(jnp.concatenate([patches, marks, cotangent], axis=2))
    packed = jnp.concatenate(vectors, axis=1)
    own_qkv, qkv_block, full_out, mlp, pick, halves = route.weights(
        w_qkv, w_out, sides, packed, own_in
    )
    own_in, own_grad = own_in[:, : width + 128], own_in[:, width + 128 :]
    rows_all = route.rows_gather(own_in)
    halves = halves.astype(F32)
    full = []
    spot = 0
    for item in vectors:
        full.append(halves[:, spot : spot + item.shape[1]].reshape(1, -1))
        spot += item.shape[1]
    gain_one, shift_one, gain_two, shift_two = full[:4]
    bias_query, bias_value, bias_out, bias_up, bias_down = full[4:]

    qkv_bias = jnp.concatenate(
        [
            lax.dynamic_slice_in_dim(bias_query, me * block, block, 1),
            jnp.zeros((1, block), F32),
            lax.dynamic_slice_in_dim(bias_value, me * block, block, 1),
        ],
        axis=1,
    )
    normed_one, projected = project(
        pick, rows_all, gain_one, shift_one, own_qkv, qkv_block, qkv_bias
    )
    rows_grad = route.rows_gather(after(own_grad, projected))
    seq = projected.shape[0] // route.each
    projected = projected.reshape(route.each, seq, 3 * block)
    marks = rows_all[:, width : width + 1].astype(F32).reshape(route.each, seq, 1)
    length = jnp.sum(marks, axis=1, keepdims=True)
    spot = route.positions(lax.broadcasted_iota(jnp.int32, (route.each, seq, 1), 1))
    mask_bias = jnp.where(spot.astype(F32) < length, 0.0, -1e30).astype(F32)

    attended, lse = attend_fwd(projected, mask_bias, head_count)
    pieces, spots = route.heads_gather(attended.transpose(1, 0, 2).reshape(block, -1))

    def by_piece(whole):
        size = pieces[0].shape[0] // len(spots[0])
        return jnp.stack(
            [
                jnp.concatenate([lax.dynamic_slice_in_dim(whole, at, size, 0) for at in group])
                for group in spots
            ]
        )

    middle, normed_two = attend_out(
        pieces, by_piece(full_out), rows_all, bias_out, gain_two, shift_two
    )
    up_bias = lax.dynamic_slice_in_dim(bias_up, me * hidden, hidden, 1)
    up_bias = jnp.pad(up_bias, ((0, 0), (0, padded - hidden)))

    active, grad_hidden, grad_part_two, up_sums = mlp_turn(
        pick, normed_two, rows_grad, mlp, up_bias
    )
    near_two = route.rows_near(grad_part_two)
    grad_mlp = weight_grads(
        [rows_grad, normed_two], [active, grad_hidden], "mlp_grads"
    )
    sum_mlp = route.mlp_grads(grad_mlp)
    grad_normed_two = after(route.rows_end(near_two), grad_mlp)
    own_middle = route.own_rows(middle)
    own_unit_two, own_inverse_two = centred(own_middle)
    grad_middle = own_grad.astype(F32) + norm_back(
        grad_normed_two, own_unit_two, own_inverse_two, gain_two
    )
    own_branch = grad_middle.astype(BF16)
    mlp_part = mlp_out(pick, after(active, own_branch), mlp)
    grad_branch = route.rows_gather(own_branch, mlp_part)

    mlp_near = route.rows_near(after(mlp_part, grad_branch))
    result = (own_middle + route.rows_end(mlp_near) + bias_down).astype(BF16)

    grad_projected = attend_bwd(
        projected,
        mask_bias,
        lse,
        after(grad_branch, mlp_near[1]).reshape(route.each, seq, width),
        lax.dynamic_slice_in_dim(full_out, me * block, block, 0),
        head_count,
    ).reshape(-1, 3 * block)
    result = route.tokens_out(after(result, grad_projected))
    grad_part_one, norm_sums, proj_sums = project_back(
        pick, grad_projected, own_qkv, qkv_block, rows_all, width
    )
    near_one = route.rows_near(grad_part_one)
    my_branch = lax.dynamic_slice_in_dim(grad_branch, me * block, block, 1)
    grad_out = out_grads(pieces, after(my_branch, grad_part_one))
    grad_qkv = weight_grads([normed_one], [after(grad_projected, near_one[1])], "qkv_grads")
    grad_normed_one = route.rows_end(near_one)
    own_unit_one, own_inverse_one = centred(route.own_rows(rows_all)[:, :width].astype(F32))
    grad_inputs = grad_middle + norm_back(
        grad_normed_one, own_unit_one, own_inverse_one, gain_one
    )
    grad_inputs = grad_inputs.astype(BF16)
    grad_patches = route.tokens_out(grad_inputs)

    out_qkv, out_out = route.attention_grads(grad_qkv, grad_out, sum_mlp)
    out_mlp = route.mlp_halves(sum_mlp)
    out_down, out_up = (
        jnp.concatenate([side[:, spot : spot + hidden] for side in out_mlp], axis=1)
        for spot in (0, padded)
    )

    def spread(values, size):
        return lax.dynamic_update_slice(
            jnp.zeros((size,), F32), values, (me * values.shape[0],)
        )

    sums = [
        norm_sums[0],
        norm_sums[1],
        jnp.sum(grad_normed_two * own_unit_two, axis=0),
        jnp.sum(grad_normed_two, axis=0),
        spread(proj_sums[0, :block], width),
        spread(proj_sums[0, 2 * block :], width),
        jnp.sum(own_branch.astype(F32), axis=0),
        spread(up_sums[0, :hidden], hidden * team),
        jnp.sum(cotangent.astype(F32), axis=(0, 1)),
    ]
    flat = route.total(after(jnp.concatenate(sums)[None], grad_inputs))
    out_vectors = []
    spot = 0
    for item in sums:
        size = item.shape[0]
        half = size // dev_count
        out_vectors.append(lax.dynamic_slice(flat, (0, spot + dev * half), (1, half)))
        spot += size
    return (result, grad_patches, out_qkv, out_out, out_up, out_down, *out_vectors)


def solution(mesh):
    dev_count, sa_count = mesh.devices.shape

    def whole(*args):
        zed = args[0].shape[0] // dev_count
        why = sa_count // (2 * zed)
        sizes = (dev_count, zed, why)
        inner = Mesh(mesh.devices.reshape(dev_count, zed, why, 2), ("dev", "z", "y", "core"))
        rows = ("z", "y", "core")
        token = P("dev", rows, None)
        weight = P(rows, "dev")
        vector = P(None, "dev")
        return jax.shard_map(
            functools.partial(per_device, sizes),
            mesh=inner,
            in_specs=(token, P("dev", rows), token) + (weight,) * 4 + (vector,) * 9,
            out_specs=(token, token) + (weight,) * 4 + (vector,) * 9,
            check_vma=False,
        )(*args)

    return whole
```

```python
import functools

import jax
import jax.numpy as jnp
from jax import lax
from jax.experimental import pallas as pl
from jax.experimental.pallas import tpu as pltpu
from jax.experimental.layout import Layout, with_layout_constraint
from jax.sharding import Mesh
from jax.sharding import PartitionSpec as P

HEADS = 16
HEAD_DIM = 72
SCALE = HEAD_DIM ** (-0.5)
Q_BLOCK = 256
F32 = jnp.float32
BF16 = jnp.bfloat16


def dot(left, right):
    return jnp.dot(left, right, preferred_element_type=F32)


def dot_tn(left, right):
    return lax.dot_general(left, right, (((0,), (0,)), ((), ())), preferred_element_type=F32)


def dot_nt(left, right):
    return lax.dot_general(left, right, (((1,), (1,)), ((), ())), preferred_element_type=F32)


def row_major(values):
    return with_layout_constraint(values, Layout(tuple(range(values.ndim))))


def after(value, *others):
    if not others:
        return value
    return lax.optimization_barrier((value, *others))[0]


def attend_fwd_body(heads, qkv_ref, bias_ref, out_ref, lse_ref):
    width = heads * HEAD_DIM
    rows = pl.ds(pl.program_id(1) * Q_BLOCK, Q_BLOCK)
    bias = bias_ref[0]
    for head in range(heads):
        low = head * HEAD_DIM
        query = qkv_ref[0, rows, low : low + HEAD_DIM]
        keys = qkv_ref[0, :, width + low : width + low + HEAD_DIM]
        values = qkv_ref[0, :, 2 * width + low : 2 * width + low + HEAD_DIM]
        scores = dot_nt(keys, query) * SCALE + bias
        peak = jnp.max(scores, axis=0, keepdims=True)
        expo = jnp.exp(scores - peak)
        total = jnp.sum(expo, axis=0, keepdims=True)
        mixed = dot_tn(values, expo.astype(BF16)) / total
        out_ref[0, low : low + HEAD_DIM, :] = mixed.astype(BF16)
        lse_ref[0, head : head + 1, :] = peak + jnp.log(total)
    if heads < 8:
        lse_ref[0, heads:, :] = jnp.zeros((8 - heads, Q_BLOCK), F32)


def attend_bwd_body(
    heads, qkv_ref, bias_ref, lse_ref, branch_ref, w_ref, out_ref, key_acc, value_acc, grad_ref
):
    width = heads * HEAD_DIM
    step = pl.program_id(1)
    begin = step * Q_BLOCK
    bias = bias_ref[0]

    @pl.when(step == 0)
    def _():
        key_acc[...] = jnp.zeros_like(key_acc)
        value_acc[...] = jnp.zeros_like(value_acc)

    grad_ref[...] = dot_nt(branch_ref[0], w_ref[...]).astype(BF16)
    for head in range(heads):
        low = head * HEAD_DIM
        rows = pl.ds(begin, Q_BLOCK)
        query = qkv_ref[0, rows, low : low + HEAD_DIM]
        grad = grad_ref[:, low : low + HEAD_DIM]
        keys = qkv_ref[0, :, width + low : width + low + HEAD_DIM]
        values = qkv_ref[0, :, 2 * width + low : 2 * width + low + HEAD_DIM]
        scores = dot_nt(keys, query) * SCALE + bias
        probs = jnp.exp(scores - lse_ref[0, head : head + 1, :])
        value_acc[head] += dot(probs.astype(BF16), grad)
        grad_probs = dot_nt(values, grad)
        term = jnp.sum(probs * grad_probs, axis=0, keepdims=True)
        grad_scores = (probs * (grad_probs - term)).astype(BF16)
        key_acc[head] += dot(grad_scores, query)
        grad_query = dot_tn(grad_scores, keys) * SCALE
        out_ref[0, rows, low : low + HEAD_DIM] = grad_query.astype(BF16)

    @pl.when(step == pl.num_programs(1) - 1)
    def _():
        for head in range(heads):
            low = head * HEAD_DIM
            out_ref[0, :, width + low : width + low + HEAD_DIM] = (key_acc[head] * SCALE).astype(BF16)
            out_ref[0, :, 2 * width + low : 2 * width + low + HEAD_DIM] = value_acc[head].astype(BF16)


def run(body, name, steps, operands, specs, outs, out_specs, flops, scratch=(), pick=None):
    size = sum(item.size * item.dtype.itemsize for item in operands)
    picks = () if pick is None else (pick,)
    return pl.pallas_call(
        body,
        name=name,
        grid_spec=pltpu.PrefetchScalarGridSpec(
            num_scalar_prefetch=len(picks),
            grid=steps,
            in_specs=specs,
            out_specs=out_specs,
            scratch_shapes=scratch,
        ),
        out_shape=outs,
        cost_estimate=pl.CostEstimate(flops=flops, transcendentals=0, bytes_accessed=size),
        compiler_params=pltpu.CompilerParams(vmem_limit_bytes=50 << 20),
    )(*picks, *operands)


def rows_spec(wide):
    return pl.BlockSpec((Q_BLOCK, wide), lambda i, *_: (i, 0))


def fixed(item):
    shape = item.shape
    return pl.BlockSpec(shape, lambda *_: (0,) * len(shape))


def picked(item, wide):
    return pl.BlockSpec((item.shape[0], wide), lambda i, pick: (0, pick[0]))


def shaped(shape, dtype):
    return jax.ShapeDtypeStruct(shape, dtype)


def attend_fwd(qkv, bias, heads):
    images, seq, wide = qkv.shape
    width = heads * HEAD_DIM
    return run(
        functools.partial(attend_fwd_body, heads),
        "attend_fwd",
        (images, seq // Q_BLOCK),
        (qkv, bias),
        [
            pl.BlockSpec((1, seq, wide), lambda i, j: (i, 0, 0)),
            pl.BlockSpec((1, seq, 1), lambda i, j: (i, 0, 0)),
        ],
        [shaped((images, width, seq), BF16), shaped((images, 8, seq), F32)],
        [
            pl.BlockSpec((1, width, Q_BLOCK), lambda i, j: (i, 0, j)),
            pl.BlockSpec((1, 8, Q_BLOCK), lambda i, j: (i, 0, j)),
        ],
        4 * images * heads * seq * seq * 128,
    )


def attend_bwd(qkv, bias, lse, branch, w_rows, heads):
    images, seq, wide = qkv.shape
    return run(
        functools.partial(attend_bwd_body, heads),
        "attend_bwd",
        (images, seq // Q_BLOCK),
        (qkv, bias, lse, branch, w_rows),
        [
            pl.BlockSpec((1, seq, wide), lambda i, j: (i, 0, 0)),
            pl.BlockSpec((1, seq, 1), lambda i, j: (i, 0, 0)),
            pl.BlockSpec((1, 8, Q_BLOCK), lambda i, j: (i, 0, j)),
            pl.BlockSpec((1, Q_BLOCK, branch.shape[2]), lambda i, j: (i, j, 0)),
            fixed(w_rows),
        ],
        shaped((images, seq, wide), BF16),
        pl.BlockSpec((1, seq, wide), lambda i, j: (i, 0, 0)),
        10 * images * heads * seq * seq * 128,
        [
            pltpu.VMEM((heads, seq, HEAD_DIM), F32),
            pltpu.VMEM((heads, seq, HEAD_DIM), F32),
            pltpu.VMEM((Q_BLOCK, heads * HEAD_DIM), BF16),
        ],
    )


def centred(values):
    centre = values - jnp.mean(values, axis=-1, keepdims=True)
    spread = jnp.mean(centre * centre, axis=-1, keepdims=True)
    inverse = lax.rsqrt(spread + 1e-06)
    return centre * inverse, inverse


def project(pick, rows_all, gain, shift, weight, block, bias):
    count, width = rows_all.shape[0], gain.shape[1]
    wide = bias.shape[1]

    def body(_, rows_ref, gain_ref, shift_ref, weight_ref, bias_ref, normed_ref, out_ref):
        unit = centred(rows_ref[:, :width].astype(F32))[0]
        normed = (unit * gain_ref[...] + shift_ref[...]).astype(BF16)
        normed_ref[...] = normed
        out_ref[...] = (dot(normed, weight_ref[:, :wide]) + bias_ref[...]).astype(BF16)

    operands = (rows_all, gain, shift, weight, bias)
    return run(
        body,
        "project",
        (count // Q_BLOCK,),
        operands,
        [rows_spec(rows_all.shape[1]), fixed(gain), fixed(shift), picked(weight, block), fixed(bias)],
        [shaped((count, width), BF16), shaped((count, wide), BF16)],
        [rows_spec(width), rows_spec(wide)],
        2 * count * width * wide,
        pick=pick,
    )


def attend_out(pieces, weights, rows_all, bias, gain, shift):
    count, width = rows_all.shape[0], gain.shape[1]
    total = len(pieces)
    piece = pieces[0].shape[0]

    def body(*refs):
        piece_refs = refs[:total]
        weight_ref, rows_ref, bias_ref, gain_ref, shift_ref = refs[total:-2]
        middle_ref, normed_ref = refs[-2:]
        branch = dot_tn(piece_refs[0][...], weight_ref[0])
        for k in range(1, total):
            branch += dot_tn(piece_refs[k][...], weight_ref[k])
        middle = rows_ref[:, :width].astype(F32) + (branch + bias_ref[...])
        middle_ref[...] = middle
        normed_ref[...] = (centred(middle)[0] * gain_ref[...] + shift_ref[...]).astype(BF16)

    return run(
        body,
        "attend_out",
        (count // Q_BLOCK,),
        (*pieces, weights, rows_all, bias, gain, shift),
        [pl.BlockSpec((piece, Q_BLOCK), lambda i: (0, i))] * total
        + [fixed(weights), rows_spec(rows_all.shape[1])]
        + [fixed(bias), fixed(gain), fixed(shift)],
        [shaped((count, width), F32), shaped((count, width), BF16)],
        [rows_spec(width), rows_spec(width)],
        2 * count * width * width,
    )


def mlp_turn(pick, normed, grad, mlp, bias):
    count, width = normed.shape
    hidden = bias.shape[1]

    def body(_, normed_ref, grad_ref, mlp_ref, bias_ref, active_ref, slope_ref, back_ref, sums_ref):
        pre = dot(normed_ref[...], mlp_ref[:, :hidden]) + bias_ref[...]
        active, slope = gelu_pair(pre)
        active_ref[...] = active.astype(BF16)
        grad_hidden = (dot(grad_ref[...], mlp_ref[:, hidden : 2 * hidden]) * slope).astype(BF16)
        slope_ref[...] = grad_hidden
        back_ref[...] = dot_nt(grad_hidden, mlp_ref[:, :hidden]).astype(BF16)
        sums = jnp.sum(grad_hidden.astype(F32), axis=0, keepdims=True)

        @pl.when(pl.program_id(0) == 0)
        def _():
            sums_ref[...] = sums

        @pl.when(pl.program_id(0) > 0)
        def _():
            sums_ref[...] += sums

    return run(
        body,
        "mlp_turn",
        (count // Q_BLOCK,),
        (normed, grad, mlp, bias),
        [rows_spec(width), rows_spec(width), picked(mlp, 2 * hidden), fixed(bias)],
        [
            shaped((count, hidden), BF16),
            shaped((count, hidden), BF16),
            shaped((count, width), BF16),
            shaped((1, hidden), F32),
        ],
        [rows_spec(hidden), rows_spec(hidden), rows_spec(width), fixed(bias)],
        6 * count * width * hidden,
        pick=pick,
    )


def mlp_out(pick, active, mlp):
    count, hidden = active.shape
    width = mlp.shape[0]

    def body(_, active_ref, mlp_ref, out_ref):
        out_ref[...] = dot_nt(active_ref[...], mlp_ref[:, hidden : 2 * hidden]).astype(BF16)

    return run(
        body,
        "mlp_out",
        (count // Q_BLOCK,),
        (active, mlp),
        [rows_spec(hidden), picked(mlp, 2 * hidden)],
        shaped((count, width), BF16),
        rows_spec(width),
        2 * count * width * hidden,
        pick=pick,
    )


def weight_grads(lefts, rights, name):
    count, width = lefts[0].shape
    wides = [item.shape[1] for item in rights]
    tile = 384
    total = len(lefts)

    def body(*refs):
        out_ref = refs[-1]
        spot = 0
        for k in range(total):
            product = dot_tn(refs[k][...], refs[total + k][...])
            out_ref[:, spot : spot + wides[k]] = product.astype(BF16)
            spot += wides[k]

    return run(
        body,
        name,
        (width // tile,),
        (*lefts, *rights),
        [pl.BlockSpec((count, tile), lambda i, *_: (0, i))] * total + [fixed(item) for item in rights],
        shaped((width, sum(wides)), BF16),
        pl.BlockSpec((tile, sum(wides)), lambda i: (i, 0)),
        2 * count * width * sum(wides),
    )


def out_grads(pieces, branch):
    total = len(pieces)
    piece = pieces[0].shape[0]
    wide = branch.shape[1]

    def body(*refs):
        for k in range(total):
            product = dot(refs[k][...], refs[total][...])
            refs[-1][k * piece : (k + 1) * piece, :] = product.astype(BF16)

    operands = (*pieces, branch)
    out = shaped((total * piece, wide), BF16)
    return run(
        body,
        "out_grads",
        (1,),
        operands,
        [fixed(item) for item in operands],
        out,
        fixed(out),
        2 * branch.shape[0] * total * piece * wide,
    )


def project_back(pick, grad, weight, block, rows_all, width):
    count, wide = grad.shape

    def body(_, grad_ref, weight_ref, rows_ref, back_ref, norm_ref, bias_ref):
        back = dot_nt(grad_ref[...], weight_ref[:, :wide])
        back_ref[...] = back.astype(BF16)
        unit = centred(rows_ref[:, :width].astype(F32))[0]
        gain = jnp.sum(back * unit, axis=0, keepdims=True)
        shift = jnp.sum(back, axis=0, keepdims=True)
        bias = jnp.sum(grad_ref[...].astype(F32), axis=0, keepdims=True)

        @pl.when(pl.program_id(0) == 0)
        def _():
            norm_ref[...] = jnp.zeros_like(norm_ref)
            bias_ref[...] = jnp.zeros_like(bias_ref)

        norm_ref[0:1] += gain
        norm_ref[1:2] += shift
        bias_ref[...] += bias

    return run(
        body,
        "project_back",
        (count // Q_BLOCK,),
        (grad, weight, rows_all),
        [rows_spec(wide), picked(weight, block), rows_spec(rows_all.shape[1])],
        [shaped((count, width), BF16), shaped((2, width), F32), shaped((1, wide), F32)],
        [
            rows_spec(width),
            pl.BlockSpec((2, width), lambda *_: (0, 0)),
            pl.BlockSpec((1, wide), lambda *_: (0, 0)),
        ],
        2 * count * width * wide,
        pick=pick,
    )


class Native:
    def __init__(self, sizes, images, tokens):
        self.dev, self.zed, self.why = sizes
        self.images = images
        self.tokens = tokens
        self.team = self.dev * 2
        self.groups = self.zed * self.why
        self.each = images * self.dev // self.groups
        self.piece = tokens // self.dev
        self.rows = self.each * self.groups * self.piece

    def positions(self, row):
        place = row % self.piece
        group = (row // self.piece) % self.groups
        team = row // (self.piece * self.groups)
        owner = group * 2 + team % 2
        return owner * self.tokens + (team // 2) * self.piece + place

    def tokens_in(self, values):
        wide = values.shape[-1]
        split = values.reshape(self.images, self.dev, self.piece, wide)
        split = lax.all_to_all(split, "dev", 1, 0, tiled=True)
        split = split.reshape(self.groups, self.each, self.piece, wide)
        split = lax.all_to_all(split, ("z", "y"), 0, 0, tiled=True)
        return split.transpose(1, 0, 2, 3).reshape(self.rows, wide)

    def tokens_out(self, values):
        wide = values.shape[-1]
        split = values.reshape(self.each, self.groups, self.piece, wide).transpose(1, 0, 2, 3)
        split = lax.all_to_all(split, ("z", "y"), 0, 0, tiled=True)
        split = split.reshape(self.dev * self.images, 1, self.piece, wide)
        split = lax.all_to_all(split, "dev", 0, 1, tiled=True)
        return split.reshape(self.images, self.tokens, wide)

    def rows_gather(self, values, *gates):
        wide = values.shape[-1]
        whole = lax.all_gather(values, ("dev", "core"), axis=0, tiled=True)
        whole = whole.reshape(self.team, self.each, -1, wide).transpose(1, 0, 2, 3)
        return whole.reshape(self.team * self.rows, wide)

    def rows_scatter(self, values):
        wide = values.shape[-1]
        split = values.astype(BF16).reshape(self.each, self.team, -1, wide).transpose(1, 0, 2, 3)
        split = split.reshape(self.team * self.rows, wide)
        return lax.psum_scatter(
            split, ("dev", "core"), scatter_dimension=0, tiled=True
        ).astype(F32)

    def rows_near(self, values):
        return values, values

    def rows_end(self, sums):
        return self.rows_scatter(sums[0])

    def own_rows(self, values):
        wide = values.shape[-1]
        me = lax.axis_index(("dev", "core"))
        split = values.reshape(self.each, self.team, -1, wide)
        return lax.dynamic_slice_in_dim(split, me, 1, 1).reshape(self.rows, wide)

    def heads_gather(self, values):
        return [lax.all_gather(values, ("dev", "core"), axis=0, tiled=True)], [[0]]

    def weights(self, w_qkv, w_out, mlp, packed, *gates):
        whole = lax.all_gather(w_qkv, "dev", axis=1, tiled=True)
        rows, wide = whole.shape
        split = whole.reshape(rows, 3, self.team, wide // (3 * self.team))
        split = lax.dynamic_slice_in_dim(split, 2 * lax.axis_index("dev"), 2, 2)
        split = split.transpose(0, 2, 1, 3).reshape(rows, -1)
        split = lax.all_to_all(split, "core", 1, 0, tiled=True)
        full_qkv = lax.all_gather(split, ("z", "y"), axis=0, tiled=True)
        full_out = lax.all_gather(w_out, "dev", axis=1, tiled=True)
        full_out = lax.all_gather(full_out, ("z", "y", "core"), axis=0, tiled=True)
        mlp = jnp.concatenate(mlp, axis=1)
        mlp = lax.all_to_all(mlp, "core", 1, 0, tiled=True)
        mlp = lax.all_gather(mlp, ("z", "y"), axis=0, tiled=True)
        vectors = lax.all_gather(packed, "dev", axis=0, tiled=True)
        return full_qkv, full_qkv.shape[1], full_out, mlp, jnp.zeros((1,), jnp.int32), vectors

    def mlp_grads(self, grads):
        return lax.psum_scatter(grads, ("z", "y"), scatter_dimension=0, tiled=True)

    def mlp_halves(self, grads):
        grads = lax.all_to_all(grads, "core", 0, 1, tiled=True).astype(F32)
        half = grads.shape[1] // 2
        return grads[:, :half], grads[:, half:]

    def attention_grads(self, grad_qkv, grad_out, *gates):
        both = jnp.concatenate([grad_out, grad_qkv], axis=1)
        return lax.psum_scatter(both, ("z", "y"), scatter_dimension=0, tiled=True), both

    def attention_ends(self, both, block):
        out = lax.all_to_all(both[:, :block], "core", 0, 1, tiled=True)
        piece = lax.all_to_all(both[:, block:], "core", 0, 1, tiled=True)
        rows = piece.shape[0]
        piece = piece.reshape(rows, 2, 3, block).transpose(0, 2, 1, 3).reshape(rows, 3, 1, -1)
        whole = lax.all_gather(piece, "dev", axis=2, tiled=True)
        whole = whole.reshape(rows, self.dev, 6 * block)
        mine = lax.dynamic_slice_in_dim(whole, lax.axis_index("dev"), 1, 1)[:, 0]
        return mine.astype(F32), out.astype(F32)

    def total(self, values):
        return lax.psum(values, ("dev", "z", "y", "core"))


def joint(move):
    pairs = []
    for dev in range(2):
        for zed in range(4):
            for why in range(2):
                for core in range(2):
                    to = move(dev, zed, why, core)
                    source = ((dev * 4 + zed) * 2 + why) * 2 + core
                    pairs.append((source, ((to[0] * 4 + to[1]) * 2 + to[2]) * 2 + to[3]))
    return pairs


def send(values, move):
    return lax.ppermute(values, ("dev", "z", "y", "core"), joint(move))


def across(values):
    return send(values, lambda d, z, y, c: (1 - d, z, y, c))


def beside(values):
    return send(values, lambda d, z, y, c: (d, z, y, 1 - c))


class Paired(Native):
    def positions(self, row):
        place = row % self.tokens
        turn = (row // self.tokens) % 4
        team = row // (self.tokens * 4)
        zed = (lax.axis_index("z") - turn) % 4
        return ((zed * 2 + team // 2) * 2 + team % 2) * self.tokens + place

    def tokens_in(self, values):
        zed = lax.axis_index("z")
        pieces = []
        for turn in range(4):
            piece = lax.dynamic_slice_in_dim(values, (zed + turn) % 4, 1, 0)[0]
            pieces.append(send(piece, lambda d, z, y, c: (y, (z + turn) % 4, d, c)))
        return jnp.concatenate(pieces, axis=0)

    def tokens_out(self, values):
        zed = lax.axis_index("z")
        rows = self.tokens
        pieces = []
        for turn in range(4):
            piece = values[turn * rows : (turn + 1) * rows]
            pieces.append(send(piece, lambda d, z, y, c: (y, (z - turn) % 4, d, c)))
        order = (jnp.arange(4) - zed) % 4
        result = pieces[0][None]
        for turn in range(1, 4):
            result = jnp.where((order == turn)[:, None, None], pieces[turn][None], result)
        return result

    def rows_gather(self, values, *gates):
        me = lax.axis_index(("dev", "core"))
        rows, wide = values.shape
        mine = jnp.concatenate([values, after(across(values), *gates)], axis=0)
        whole = jnp.zeros((4 * rows, wide), values.dtype)
        for step, pair in enumerate((mine, beside(mine))):
            for far in range(2):
                piece = pair[far * rows : (far + 1) * rows]
                whole = lax.dynamic_update_slice(whole, piece, ((me ^ (step + 2 * far)) * rows, 0))
        return whole

    def rows_scatter(self, values):
        return self.rows_end(self.rows_near(values))

    def rows_near(self, values):
        rows = self.rows
        me = lax.axis_index(("dev", "core"))

        def part(step):
            return lax.dynamic_slice_in_dim(values, (me ^ step) * rows, rows, 0)

        near = jnp.concatenate([part(1), part(3)], axis=0)
        came = beside(near.astype(BF16))
        low, high = came[:rows].astype(F32), came[rows:].astype(F32)
        return part(0) + low, (part(2) + high).astype(BF16)

    def rows_end(self, sums):
        return sums[0] + across(sums[1]).astype(F32)

    def own_rows(self, values):
        me = lax.axis_index(("dev", "core"))
        return lax.dynamic_slice_in_dim(values, me * self.rows, self.rows, 0)

    def heads_gather(self, values):
        me = lax.axis_index(("dev", "core"))
        mine = jnp.concatenate([values, across(values)], axis=0)
        pieces = [mine, beside(mine)]
        block = values.shape[0]
        spots = [[(me ^ (step + 2 * far)) * block for far in range(2)] for step in range(2)]
        return pieces, spots

    def weights(self, w_qkv, w_out, mlp, packed, *gates):
        third = w_qkv.shape[1] // 3
        half = third // 2
        wide = w_out.shape[1]
        count = packed.shape[1]
        first = lax.axis_index("dev") == 0
        lines = -(-count // ((third + wide) * 8)) * 8
        sheet = jnp.pad(packed[0], (0, lines * (third + wide) - count)).reshape(lines, -1)
        message = jnp.concatenate([w_qkv[:, third : 2 * third], w_out], axis=1)
        came = across(jnp.concatenate([message, sheet], axis=0))
        rows = w_qkv.shape[0]
        vectors = came[rows:].reshape(1, -1)[:, :count]
        vectors = jnp.concatenate(
            [jnp.where(first, packed, vectors), jnp.where(first, vectors, packed)], axis=0
        )
        came_qkv, came_out = came[:rows, :third], came[:rows, third:]
        low, high = w_qkv[:, :third], w_qkv[:, 2 * third :]
        query = jnp.where(first, low, came_qkv)
        keys = jnp.where(first, high, low)
        values = jnp.where(first, came_qkv, high)
        blocks = [
            jnp.concatenate(
                [item[:, side * half : (side + 1) * half] for item in (query, keys, values)], axis=1
            )
            for side in range(2)
        ]
        block = -(-3 * half // 128) * 128
        blocks = [jnp.pad(item, ((0, 0), (0, block - 3 * half))) for item in blocks]
        everyone = ("z", "y", "core")
        outs = [jnp.where(first, w_out, came_out), jnp.where(first, came_out, w_out)]
        full_qkv = jnp.concatenate([*blocks, *outs], axis=1)
        full_qkv = lax.all_gather(full_qkv, everyone, axis=0, tiled=True)
        rest = after(jnp.concatenate(mlp, axis=1), full_qkv, *gates)
        rest = lax.all_gather(rest, everyone, axis=0, tiled=True)
        pick = lax.axis_index("core").reshape(1)
        return full_qkv, block, full_qkv[:, 2 * block :], rest, pick, vectors

    def turned(self):
        me = lax.axis_index(("dev", "core"))
        return [((k ^ me) % 2) * 2 + (k ^ me) // 2 for k in range(4)]

    def halve(self, block):
        upper = lax.axis_index("core") == 0
        rows = block.shape[0] // 2
        low, high = block[:rows], block[rows:]
        keep = jnp.where(upper, low, high)
        got = beside(jnp.where(upper, high, low).astype(BF16)).astype(F32)
        return jnp.where(upper, keep, got), jnp.where(upper, got, keep)

    def mlp_grads(self, grads):
        return lax.psum_scatter(grads, ("z", "y"), scatter_dimension=0, tiled=True)

    def mlp_halves(self, grads):
        return self.halve(grads.astype(F32))

    def attention_grads(self, grad_qkv, grad_out, *gates):
        block = grad_out.shape[1]
        rows = grad_qkv.shape[0] // 8
        order = grad_out.reshape(4, 2 * rows, block)
        order = jnp.stack([lax.dynamic_index_in_dim(order, k, 0, False) for k in self.turned()])
        both = jnp.concatenate([order.reshape(8 * rows, block), grad_qkv], axis=1)
        both = after(both, *gates)
        return lax.psum_scatter(both, ("z", "y"), scatter_dimension=0, tiled=True), both

    def attention_ends(self, both, block):
        first = lax.axis_index("dev") == 0
        left, right = self.halve(both.astype(F32))
        out = jnp.concatenate([left[:, :block], right[:, :block]], axis=1)
        query, keys, values = (
            jnp.concatenate([left[:, k * block : (k + 1) * block], right[:, k * block : (k + 1) * block]], axis=1)
            for k in (1, 2, 3)
        )
        came = across(jnp.where(first, values, query).astype(BF16)).astype(F32)
        return (
            jnp.concatenate(
                [jnp.where(first, query, keys), came, jnp.where(first, keys, values)], axis=1
            ),
            out,
        )

    def total(self, values):
        everyone = ("dev", "z", "y", "core")
        wide = values.shape[1]
        each = -(-wide // (32 * 128)) * 128
        parts = jnp.pad(values[0], (0, 32 * each - wide)).reshape(32, each)
        parts = lax.all_to_all(parts, everyone, 0, 0, tiled=True)
        mine = jnp.sum(parts, axis=0, keepdims=True)
        every = jnp.broadcast_to(mine, (32, each))
        return lax.all_to_all(every, everyone, 0, 0, tiled=True).reshape(1, -1)[:, :wide]


def norm_back(grad, unit, inverse, gain):
    scaled = grad * gain
    mean = jnp.mean(scaled, axis=-1, keepdims=True)
    along = jnp.mean(scaled * unit, axis=-1, keepdims=True)
    return (scaled - mean - unit * along) * inverse


def gelu_pair(hidden):
    root = 0.7978845608028654
    inner = jnp.tanh(root * (hidden + 0.044715 * hidden * hidden * hidden))
    half = 0.5 * (1.0 + inner)
    slope = half + 0.5 * hidden * (1.0 - inner * inner) * root * (
        1.0 + 3 * 0.044715 * hidden * hidden
    )
    return hidden * half, slope


def per_device(
    sizes,
    patches,
    patch_mask,
    cotangent,
    w_qkv,
    w_out,
    w_up,
    w_down,
    *vectors,
):
    images, tokens, width = patches.shape
    paired = sizes == (2, 4, 2) and images == 4 and Paired is not Native
    route = (Paired if paired else Native)(sizes, images, tokens)
    dev_count = sizes[0]
    team = route.team
    dev = lax.axis_index("dev")
    me = lax.axis_index(("dev", "core"))
    head_count = HEADS // team
    block = head_count * HEAD_DIM
    hidden = w_up.shape[1] // 2

    padded = -(-hidden // 128) * 128
    sides = [
        jnp.concatenate(
            [
                jnp.pad(item[:, side * hidden : (side + 1) * hidden], ((0, 0), (0, padded - hidden)))
                for item in (w_up, w_down)
            ],
            axis=1,
        )
        for side in range(2)
    ]
    marks = jnp.broadcast_to(patch_mask.astype(BF16)[:, :, None], (images, tokens, 128))
    own_in = route.tokens_in(jnp.concatenate([patches, marks, cotangent], axis=2))
    packed = jnp.concatenate(vectors, axis=1)
    own_qkv, qkv_block, full_out, mlp, pick, halves = route.weights(
        w_qkv, w_out, sides, packed, own_in
    )
    own_in, own_grad = own_in[:, : width + 128], own_in[:, width + 128 :]
    rows_all = route.rows_gather(own_in)
    halves = halves.astype(F32)
    full = []
    spot = 0
    for item in vectors:
        full.append(halves[:, spot : spot + item.shape[1]].reshape(1, -1))
        spot += item.shape[1]
    gain_one, shift_one, gain_two, shift_two = full[:4]
    bias_query, bias_value, bias_out, bias_up, bias_down = full[4:]

    qkv_bias = jnp.concatenate(
        [
            lax.dynamic_slice_in_dim(bias_query, me * block, block, 1),
            jnp.zeros((1, block), F32),
            lax.dynamic_slice_in_dim(bias_value, me * block, block, 1),
        ],
        axis=1,
    )
    normed_one, projected = project(
        pick, rows_all, gain_one, shift_one, own_qkv, qkv_block, qkv_bias
    )
    rows_grad = route.rows_gather(after(own_grad, projected))
    seq = projected.shape[0] // route.each
    projected = projected.reshape(route.each, seq, 3 * block)
    marks = rows_all[:, width : width + 1].astype(F32).reshape(route.each, seq, 1)
    length = jnp.sum(marks, axis=1, keepdims=True)
    spot = route.positions(lax.broadcasted_iota(jnp.int32, (route.each, seq, 1), 1))
    mask_bias = jnp.where(spot.astype(F32) < length, 0.0, -1e30).astype(F32)

    attended, lse = attend_fwd(projected, mask_bias, head_count)
    pieces, spots = route.heads_gather(attended.transpose(1, 0, 2).reshape(block, -1))

    def by_piece(whole):
        size = pieces[0].shape[0] // len(spots[0])
        return jnp.stack(
            [
                jnp.concatenate([lax.dynamic_slice_in_dim(whole, at, size, 0) for at in group])
                for group in spots
            ]
        )

    middle, normed_two = attend_out(
        pieces, by_piece(full_out), rows_all, bias_out, gain_two, shift_two
    )
    up_bias = lax.dynamic_slice_in_dim(bias_up, me * hidden, hidden, 1)
    up_bias = jnp.pad(up_bias, ((0, 0), (0, padded - hidden)))

    active, grad_hidden, grad_part_two, up_sums = mlp_turn(
        pick, normed_two, rows_grad, mlp, up_bias
    )
    near_two = route.rows_near(grad_part_two)
    grad_mlp = weight_grads(
        [rows_grad, normed_two], [active, grad_hidden], "mlp_grads"
    )
    sum_mlp = route.mlp_grads(grad_mlp)
    grad_normed_two = after(route.rows_end(near_two), grad_mlp)
    own_middle = route.own_rows(middle)
    own_unit_two, own_inverse_two = centred(own_middle)
    grad_middle = own_grad.astype(F32) + norm_back(
        grad_normed_two, own_unit_two, own_inverse_two, gain_two
    )
    own_branch = grad_middle.astype(BF16)
    mlp_part = mlp_out(pick, after(active, own_branch), mlp)
    grad_branch = route.rows_gather(own_branch, mlp_part)

    grad_projected = attend_bwd(
        projected,
        mask_bias,
        lse,
        grad_branch.reshape(route.each, seq, width),
        lax.dynamic_slice_in_dim(full_out, me * block, block, 0),
        head_count,
    ).reshape(-1, 3 * block)
    my_branch = lax.dynamic_slice_in_dim(after(grad_branch, grad_projected), me * block, block, 1)
    grad_out = out_grads(pieces, my_branch)
    grad_qkv = weight_grads([normed_one], [grad_projected], "qkv_grads")
    sums_out, sent = route.attention_grads(grad_qkv, grad_out, sum_mlp)
    grad_projected = after(grad_projected, grad_qkv, grad_out)

    grad_part_one, norm_sums, proj_sums = project_back(
        pick, grad_projected, own_qkv, qkv_block, rows_all, width
    )
    near_one = route.rows_near(grad_part_one)
    grad_normed_one = route.rows_end(near_one)
    mlp_near = route.rows_near(after(mlp_part, near_one[1]))
    result = (own_middle + route.rows_end(mlp_near) + bias_down).astype(BF16)
    result = route.tokens_out(result)

    own_unit_one, own_inverse_one = centred(
        route.own_rows(after(rows_all, near_one[1]))[:, :width].astype(F32)
    )
    grad_inputs = grad_middle + norm_back(
        grad_normed_one, own_unit_one, own_inverse_one, gain_one
    )
    grad_inputs = after(grad_inputs.astype(BF16), sent)
    grad_patches = route.tokens_out(grad_inputs)

    out_qkv, out_out = route.attention_ends(sums_out, block)
    out_mlp = route.mlp_halves(sum_mlp)
    out_down, out_up = (
        jnp.concatenate([side[:, spot : spot + hidden] for side in out_mlp], axis=1)
        for spot in (0, padded)
    )

    def spread(values, size):
        return lax.dynamic_update_slice(
            jnp.zeros((size,), F32), values, (me * values.shape[0],)
        )

    norm_sums, proj_sums, up_sums = (
        after(item, grad_inputs) for item in (norm_sums, proj_sums, up_sums)
    )
    sums = [
        norm_sums[0],
        norm_sums[1],
        jnp.sum(grad_normed_two * own_unit_two, axis=0),
        jnp.sum(grad_normed_two, axis=0),
        spread(proj_sums[0, :block], width),
        spread(proj_sums[0, 2 * block :], width),
        jnp.sum(own_branch.astype(F32), axis=0),
        spread(up_sums[0, :hidden], hidden * team),
        jnp.sum(after(cotangent, grad_inputs).astype(F32), axis=(0, 1)),
    ]
    flat = route.total(after(jnp.concatenate(sums)[None], grad_inputs))
    out_vectors = []
    spot = 0
    for item in sums:
        size = item.shape[0]
        half = size // dev_count
        out_vectors.append(lax.dynamic_slice(flat, (0, spot + dev * half), (1, half)))
        spot += size
    return (result, grad_patches, out_qkv, out_out, out_up, out_down, *out_vectors)


def solution(mesh):
    dev_count, sa_count = mesh.devices.shape

    def whole(*args):
        zed = args[0].shape[0] // dev_count
        why = sa_count // (2 * zed)
        sizes = (dev_count, zed, why)
        inner = Mesh(mesh.devices.reshape(dev_count, zed, why, 2), ("dev", "z", "y", "core"))
        rows = ("z", "y", "core")
        token = P("dev", rows, None)
        weight = P(rows, "dev")
        vector = P(None, "dev")
        return jax.shard_map(
            functools.partial(per_device, sizes),
            mesh=inner,
            in_specs=(token, P("dev", rows), token) + (weight,) * 4 + (vector,) * 9,
            out_specs=(token, token) + (weight,) * 4 + (vector,) * 9,
            check_vma=False,
        )(*args)

    return whole
```

```python
import functools

import jax
import jax.numpy as jnp
from jax import lax
from jax.experimental import pallas as pl
from jax.experimental.pallas import tpu as pltpu
from jax.experimental.layout import Layout, with_layout_constraint
from jax.sharding import Mesh
from jax.sharding import PartitionSpec as P

HEADS = 16
HEAD_DIM = 72
SCALE = HEAD_DIM ** (-0.5)
Q_BLOCK = 256
BEHIND = ("mlp_out", "attend_bwd", "out_grads", "qkv_grads", "project_back")
F32 = jnp.float32
BF16 = jnp.bfloat16


def dot(left, right):
    return jnp.dot(left, right, preferred_element_type=F32)


def dot_tn(left, right):
    return lax.dot_general(left, right, (((0,), (0,)), ((), ())), preferred_element_type=F32)


def dot_nt(left, right):
    return lax.dot_general(left, right, (((1,), (1,)), ((), ())), preferred_element_type=F32)


def row_major(values):
    return with_layout_constraint(values, Layout(tuple(range(values.ndim))))


def after(value, *others):
    if not others:
        return value
    return lax.optimization_barrier((value, *others))[0]


def attend_fwd_body(heads, qkv_ref, bias_ref, out_ref, lse_ref):
    width = heads * HEAD_DIM
    rows = pl.ds(pl.program_id(1) * Q_BLOCK, Q_BLOCK)
    bias = bias_ref[0]
    for head in range(heads):
        low = head * HEAD_DIM
        query = qkv_ref[0, rows, low : low + HEAD_DIM]
        keys = qkv_ref[0, :, width + low : width + low + HEAD_DIM]
        values = qkv_ref[0, :, 2 * width + low : 2 * width + low + HEAD_DIM]
        scores = dot_nt(keys, query) * SCALE + bias
        peak = jnp.max(scores, axis=0, keepdims=True)
        expo = jnp.exp(scores - peak)
        total = jnp.sum(expo, axis=0, keepdims=True)
        mixed = dot_tn(values, expo.astype(BF16)) / total
        out_ref[0, low : low + HEAD_DIM, :] = mixed.astype(BF16)
        lse_ref[0, head : head + 1, :] = peak + jnp.log(total)
    if heads < 8:
        lse_ref[0, heads:, :] = jnp.zeros((8 - heads, Q_BLOCK), F32)


def attend_bwd_body(
    heads, qkv_ref, bias_ref, lse_ref, branch_ref, w_ref, out_ref, key_acc, value_acc, grad_ref
):
    width = heads * HEAD_DIM
    step = pl.program_id(1)
    begin = step * Q_BLOCK
    bias = bias_ref[0]

    @pl.when(step == 0)
    def _():
        key_acc[...] = jnp.zeros_like(key_acc)
        value_acc[...] = jnp.zeros_like(value_acc)

    grad_ref[...] = dot_nt(branch_ref[0], w_ref[...]).astype(BF16)
    for head in range(heads):
        low = head * HEAD_DIM
        rows = pl.ds(begin, Q_BLOCK)
        query = qkv_ref[0, rows, low : low + HEAD_DIM]
        grad = grad_ref[:, low : low + HEAD_DIM]
        keys = qkv_ref[0, :, width + low : width + low + HEAD_DIM]
        values = qkv_ref[0, :, 2 * width + low : 2 * width + low + HEAD_DIM]
        scores = dot_nt(keys, query) * SCALE + bias
        probs = jnp.exp(scores - lse_ref[0, head : head + 1, :])
        value_acc[head] += dot(probs.astype(BF16), grad)
        grad_probs = dot_nt(values, grad)
        term = jnp.sum(probs * grad_probs, axis=0, keepdims=True)
        grad_scores = (probs * (grad_probs - term)).astype(BF16)
        key_acc[head] += dot(grad_scores, query)
        grad_query = dot_tn(grad_scores, keys) * SCALE
        out_ref[0, rows, low : low + HEAD_DIM] = grad_query.astype(BF16)

    @pl.when(step == pl.num_programs(1) - 1)
    def _():
        for head in range(heads):
            low = head * HEAD_DIM
            out_ref[0, :, width + low : width + low + HEAD_DIM] = (key_acc[head] * SCALE).astype(BF16)
            out_ref[0, :, 2 * width + low : 2 * width + low + HEAD_DIM] = value_acc[head].astype(BF16)


def run(body, name, steps, operands, specs, outs, out_specs, flops, scratch=(), pick=None):
    share = 50 if name in BEHIND else 1
    size = sum(item.size * item.dtype.itemsize for item in operands)
    picks = () if pick is None else (pick,)
    return pl.pallas_call(
        body,
        name=name,
        grid_spec=pltpu.PrefetchScalarGridSpec(
            num_scalar_prefetch=len(picks),
            grid=steps,
            in_specs=specs,
            out_specs=out_specs,
            scratch_shapes=scratch,
        ),
        out_shape=outs,
        cost_estimate=pl.CostEstimate(
            flops=flops // share, transcendentals=0, bytes_accessed=size // share
        ),
        compiler_params=pltpu.CompilerParams(vmem_limit_bytes=50 << 20),
    )(*picks, *operands)


def rows_spec(wide):
    return pl.BlockSpec((Q_BLOCK, wide), lambda i, *_: (i, 0))


def fixed(item):
    shape = item.shape
    return pl.BlockSpec(shape, lambda *_: (0,) * len(shape))


def picked(item, wide):
    return pl.BlockSpec((item.shape[0], wide), lambda i, pick: (0, pick[0]))


def shaped(shape, dtype):
    return jax.ShapeDtypeStruct(shape, dtype)


def attend_fwd(qkv, bias, heads):
    images, seq, wide = qkv.shape
    width = heads * HEAD_DIM
    return run(
        functools.partial(attend_fwd_body, heads),
        "attend_fwd",
        (images, seq // Q_BLOCK),
        (qkv, bias),
        [
            pl.BlockSpec((1, seq, wide), lambda i, j: (i, 0, 0)),
            pl.BlockSpec((1, seq, 1), lambda i, j: (i, 0, 0)),
        ],
        [shaped((images, width, seq), BF16), shaped((images, 8, seq), F32)],
        [
            pl.BlockSpec((1, width, Q_BLOCK), lambda i, j: (i, 0, j)),
            pl.BlockSpec((1, 8, Q_BLOCK), lambda i, j: (i, 0, j)),
        ],
        4 * images * heads * seq * seq * 128,
    )


def attend_bwd(qkv, bias, lse, branch, w_rows, heads):
    images, seq, wide = qkv.shape
    return run(
        functools.partial(attend_bwd_body, heads),
        "attend_bwd",
        (images, seq // Q_BLOCK),
        (qkv, bias, lse, branch, w_rows),
        [
            pl.BlockSpec((1, seq, wide), lambda i, j: (i, 0, 0)),
            pl.BlockSpec((1, seq, 1), lambda i, j: (i, 0, 0)),
            pl.BlockSpec((1, 8, Q_BLOCK), lambda i, j: (i, 0, j)),
            pl.BlockSpec((1, Q_BLOCK, branch.shape[2]), lambda i, j: (i, j, 0)),
            fixed(w_rows),
        ],
        shaped((images, seq, wide), BF16),
        pl.BlockSpec((1, seq, wide), lambda i, j: (i, 0, 0)),
        10 * images * heads * seq * seq * 128,
        [
            pltpu.VMEM((heads, seq, HEAD_DIM), F32),
            pltpu.VMEM((heads, seq, HEAD_DIM), F32),
            pltpu.VMEM((Q_BLOCK, heads * HEAD_DIM), BF16),
        ],
    )


def centred(values):
    centre = values - jnp.mean(values, axis=-1, keepdims=True)
    spread = jnp.mean(centre * centre, axis=-1, keepdims=True)
    inverse = lax.rsqrt(spread + 1e-06)
    return centre * inverse, inverse


def project(pick, rows_all, gain, shift, weight, block, bias):
    count, width = rows_all.shape[0], gain.shape[1]
    wide = bias.shape[1]

    def body(_, rows_ref, gain_ref, shift_ref, weight_ref, bias_ref, normed_ref, out_ref):
        unit = centred(rows_ref[:, :width].astype(F32))[0]
        normed = (unit * gain_ref[...] + shift_ref[...]).astype(BF16)
        normed_ref[...] = normed
        out_ref[...] = (dot(normed, weight_ref[:, :wide]) + bias_ref[...]).astype(BF16)

    operands = (rows_all, gain, shift, weight, bias)
    return run(
        body,
        "project",
        (count // Q_BLOCK,),
        operands,
        [rows_spec(rows_all.shape[1]), fixed(gain), fixed(shift), picked(weight, block), fixed(bias)],
        [shaped((count, width), BF16), shaped((count, wide), BF16)],
        [rows_spec(width), rows_spec(wide)],
        2 * count * width * wide,
        pick=pick,
    )


def attend_out(pieces, weights, rows_all, bias, gain, shift):
    count, width = rows_all.shape[0], gain.shape[1]
    total = len(pieces)
    piece = pieces[0].shape[0]

    def body(*refs):
        piece_refs = refs[:total]
        weight_ref, rows_ref, bias_ref, gain_ref, shift_ref = refs[total:-2]
        middle_ref, normed_ref = refs[-2:]
        branch = dot_tn(piece_refs[0][...], weight_ref[0])
        for k in range(1, total):
            branch += dot_tn(piece_refs[k][...], weight_ref[k])
        middle = rows_ref[:, :width].astype(F32) + (branch + bias_ref[...])
        middle_ref[...] = middle
        normed_ref[...] = (centred(middle)[0] * gain_ref[...] + shift_ref[...]).astype(BF16)

    return run(
        body,
        "attend_out",
        (count // Q_BLOCK,),
        (*pieces, weights, rows_all, bias, gain, shift),
        [pl.BlockSpec((piece, Q_BLOCK), lambda i: (0, i))] * total
        + [fixed(weights), rows_spec(rows_all.shape[1])]
        + [fixed(bias), fixed(gain), fixed(shift)],
        [shaped((count, width), F32), shaped((count, width), BF16)],
        [rows_spec(width), rows_spec(width)],
        2 * count * width * width,
    )


def mlp_turn(pick, normed, grad, mlp, bias):
    count, width = normed.shape
    hidden = bias.shape[1]

    def body(_, normed_ref, grad_ref, mlp_ref, bias_ref, active_ref, slope_ref, back_ref, sums_ref):
        pre = dot(normed_ref[...], mlp_ref[:, :hidden]) + bias_ref[...]
        active, slope = gelu_pair(pre)
        active_ref[...] = active.astype(BF16)
        grad_hidden = (dot(grad_ref[...], mlp_ref[:, hidden : 2 * hidden]) * slope).astype(BF16)
        slope_ref[...] = grad_hidden
        back_ref[...] = dot_nt(grad_hidden, mlp_ref[:, :hidden]).astype(BF16)
        sums = jnp.sum(grad_hidden.astype(F32), axis=0, keepdims=True)

        @pl.when(pl.program_id(0) == 0)
        def _():
            sums_ref[...] = sums

        @pl.when(pl.program_id(0) > 0)
        def _():
            sums_ref[...] += sums

    return run(
        body,
        "mlp_turn",
        (count // Q_BLOCK,),
        (normed, grad, mlp, bias),
        [rows_spec(width), rows_spec(width), picked(mlp, 2 * hidden), fixed(bias)],
        [
            shaped((count, hidden), BF16),
            shaped((count, hidden), BF16),
            shaped((count, width), BF16),
            shaped((1, hidden), F32),
        ],
        [rows_spec(hidden), rows_spec(hidden), rows_spec(width), fixed(bias)],
        6 * count * width * hidden,
        pick=pick,
    )


def mlp_out(pick, active, mlp):
    count, hidden = active.shape
    width = mlp.shape[0]

    def body(_, active_ref, mlp_ref, out_ref):
        out_ref[...] = dot_nt(active_ref[...], mlp_ref[:, hidden : 2 * hidden]).astype(BF16)

    return run(
        body,
        "mlp_out",
        (count // Q_BLOCK,),
        (active, mlp),
        [rows_spec(hidden), picked(mlp, 2 * hidden)],
        shaped((count, width), BF16),
        rows_spec(width),
        2 * count * width * hidden,
        pick=pick,
    )


def weight_grads(lefts, rights, name):
    count, width = lefts[0].shape
    wides = [item.shape[1] for item in rights]
    tile = 384
    total = len(lefts)

    def body(*refs):
        out_ref = refs[-1]
        spot = 0
        for k in range(total):
            product = dot_tn(refs[k][...], refs[total + k][...])
            out_ref[:, spot : spot + wides[k]] = product.astype(BF16)
            spot += wides[k]

    return run(
        body,
        name,
        (width // tile,),
        (*lefts, *rights),
        [pl.BlockSpec((count, tile), lambda i, *_: (0, i))] * total + [fixed(item) for item in rights],
        shaped((width, sum(wides)), BF16),
        pl.BlockSpec((tile, sum(wides)), lambda i: (i, 0)),
        2 * count * width * sum(wides),
    )


def out_grads(pieces, branch):
    total = len(pieces)
    piece = pieces[0].shape[0]
    wide = branch.shape[1]

    def body(*refs):
        for k in range(total):
            product = dot(refs[k][...], refs[total][...])
            refs[-1][k * piece : (k + 1) * piece, :] = product.astype(BF16)

    operands = (*pieces, branch)
    out = shaped((total * piece, wide), BF16)
    return run(
        body,
        "out_grads",
        (1,),
        operands,
        [fixed(item) for item in operands],
        out,
        fixed(out),
        2 * branch.shape[0] * total * piece * wide,
    )


def project_back(pick, grad, weight, block, rows_all, width):
    count, wide = grad.shape

    def body(_, grad_ref, weight_ref, rows_ref, back_ref, norm_ref, bias_ref):
        back = dot_nt(grad_ref[...], weight_ref[:, :wide])
        back_ref[...] = back.astype(BF16)
        unit = centred(rows_ref[:, :width].astype(F32))[0]
        gain = jnp.sum(back * unit, axis=0, keepdims=True)
        shift = jnp.sum(back, axis=0, keepdims=True)
        bias = jnp.sum(grad_ref[...].astype(F32), axis=0, keepdims=True)

        @pl.when(pl.program_id(0) == 0)
        def _():
            norm_ref[...] = jnp.zeros_like(norm_ref)
            bias_ref[...] = jnp.zeros_like(bias_ref)

        norm_ref[0:1] += gain
        norm_ref[1:2] += shift
        bias_ref[...] += bias

    return run(
        body,
        "project_back",
        (count // Q_BLOCK,),
        (grad, weight, rows_all),
        [rows_spec(wide), picked(weight, block), rows_spec(rows_all.shape[1])],
        [shaped((count, width), BF16), shaped((2, width), F32), shaped((1, wide), F32)],
        [
            rows_spec(width),
            pl.BlockSpec((2, width), lambda *_: (0, 0)),
            pl.BlockSpec((1, wide), lambda *_: (0, 0)),
        ],
        2 * count * width * wide,
        pick=pick,
    )


class Native:
    def __init__(self, sizes, images, tokens):
        self.dev, self.zed, self.why = sizes
        self.images = images
        self.tokens = tokens
        self.team = self.dev * 2
        self.groups = self.zed * self.why
        self.each = images * self.dev // self.groups
        self.piece = tokens // self.dev
        self.rows = self.each * self.groups * self.piece

    def positions(self, row):
        place = row % self.piece
        group = (row // self.piece) % self.groups
        team = row // (self.piece * self.groups)
        owner = group * 2 + team % 2
        return owner * self.tokens + (team // 2) * self.piece + place

    def tokens_in(self, values):
        wide = values.shape[-1]
        split = values.reshape(self.images, self.dev, self.piece, wide)
        split = lax.all_to_all(split, "dev", 1, 0, tiled=True)
        split = split.reshape(self.groups, self.each, self.piece, wide)
        split = lax.all_to_all(split, ("z", "y"), 0, 0, tiled=True)
        return split.transpose(1, 0, 2, 3).reshape(self.rows, wide)

    def tokens_out(self, values):
        wide = values.shape[-1]
        split = values.reshape(self.each, self.groups, self.piece, wide).transpose(1, 0, 2, 3)
        split = lax.all_to_all(split, ("z", "y"), 0, 0, tiled=True)
        split = split.reshape(self.dev * self.images, 1, self.piece, wide)
        split = lax.all_to_all(split, "dev", 0, 1, tiled=True)
        return split.reshape(self.images, self.tokens, wide)

    def rows_gather(self, values, *gates):
        wide = values.shape[-1]
        whole = lax.all_gather(values, ("dev", "core"), axis=0, tiled=True)
        whole = whole.reshape(self.team, self.each, -1, wide).transpose(1, 0, 2, 3)
        return whole.reshape(self.team * self.rows, wide)

    def rows_scatter(self, values):
        wide = values.shape[-1]
        split = values.astype(BF16).reshape(self.each, self.team, -1, wide).transpose(1, 0, 2, 3)
        split = split.reshape(self.team * self.rows, wide)
        return lax.psum_scatter(
            split, ("dev", "core"), scatter_dimension=0, tiled=True
        ).astype(F32)

    def rows_near(self, values):
        return values, values

    def rows_end(self, sums):
        return self.rows_scatter(sums[0])

    def own_rows(self, values):
        wide = values.shape[-1]
        me = lax.axis_index(("dev", "core"))
        split = values.reshape(self.each, self.team, -1, wide)
        return lax.dynamic_slice_in_dim(split, me, 1, 1).reshape(self.rows, wide)

    def heads_gather(self, values):
        return [lax.all_gather(values, ("dev", "core"), axis=0, tiled=True)], [[0]]

    def weights(self, w_qkv, w_out, mlp, packed, *gates):
        whole = lax.all_gather(w_qkv, "dev", axis=1, tiled=True)
        rows, wide = whole.shape
        split = whole.reshape(rows, 3, self.team, wide // (3 * self.team))
        split = lax.dynamic_slice_in_dim(split, 2 * lax.axis_index("dev"), 2, 2)
        split = split.transpose(0, 2, 1, 3).reshape(rows, -1)
        split = lax.all_to_all(split, "core", 1, 0, tiled=True)
        full_qkv = lax.all_gather(split, ("z", "y"), axis=0, tiled=True)
        full_out = lax.all_gather(w_out, "dev", axis=1, tiled=True)
        full_out = lax.all_gather(full_out, ("z", "y", "core"), axis=0, tiled=True)
        mlp = jnp.concatenate(mlp, axis=1)
        mlp = lax.all_to_all(mlp, "core", 1, 0, tiled=True)
        mlp = lax.all_gather(mlp, ("z", "y"), axis=0, tiled=True)
        vectors = lax.all_gather(packed, "dev", axis=0, tiled=True)
        return full_qkv, full_qkv.shape[1], full_out, mlp, jnp.zeros((1,), jnp.int32), vectors

    def mlp_grads(self, grads):
        return lax.psum_scatter(grads, ("z", "y"), scatter_dimension=0, tiled=True)

    def mlp_halves(self, grads):
        grads = lax.all_to_all(grads, "core", 0, 1, tiled=True).astype(F32)
        half = grads.shape[1] // 2
        return grads[:, :half], grads[:, half:]

    def attention_grads(self, grad_qkv, grad_out):
        return grad_qkv, grad_out

    def attention_sums(self, parts, *gates):
        both = jnp.concatenate([parts[1], parts[0]], axis=1)
        return lax.psum_scatter(both, ("z", "y"), scatter_dimension=0, tiled=True), both

    def attention_ends(self, both, block):
        out = lax.all_to_all(both[:, :block], "core", 0, 1, tiled=True)
        piece = lax.all_to_all(both[:, block:], "core", 0, 1, tiled=True)
        rows = piece.shape[0]
        piece = piece.reshape(rows, 2, 3, block).transpose(0, 2, 1, 3).reshape(rows, 3, 1, -1)
        whole = lax.all_gather(piece, "dev", axis=2, tiled=True)
        whole = whole.reshape(rows, self.dev, 6 * block)
        mine = lax.dynamic_slice_in_dim(whole, lax.axis_index("dev"), 1, 1)[:, 0]
        return mine.astype(F32), out.astype(F32)

    def total(self, values):
        return lax.psum(values, ("dev", "z", "y", "core"))


def joint(move):
    pairs = []
    for dev in range(2):
        for zed in range(4):
            for why in range(2):
                for core in range(2):
                    to = move(dev, zed, why, core)
                    source = ((dev * 4 + zed) * 2 + why) * 2 + core
                    pairs.append((source, ((to[0] * 4 + to[1]) * 2 + to[2]) * 2 + to[3]))
    return pairs


def send(values, move):
    return lax.ppermute(values, ("dev", "z", "y", "core"), joint(move))


def across(values):
    return send(values, lambda d, z, y, c: (1 - d, z, y, c))


def beside(values):
    return send(values, lambda d, z, y, c: (d, z, y, 1 - c))


def upright(values):
    return send(values, lambda d, z, y, c: (d, z, 1 - y, c))


class Paired(Native):
    def positions(self, row):
        place = row % self.tokens
        turn = (row // self.tokens) % 4
        team = row // (self.tokens * 4)
        zed = (lax.axis_index("z") - turn) % 4
        return ((zed * 2 + team // 2) * 2 + team % 2) * self.tokens + place

    def tokens_in(self, values):
        zed = lax.axis_index("z")
        pieces = []
        for turn in range(4):
            piece = lax.dynamic_slice_in_dim(values, (zed + turn) % 4, 1, 0)[0]
            pieces.append(send(piece, lambda d, z, y, c: (y, (z + turn) % 4, d, c)))
        return jnp.concatenate(pieces, axis=0)

    def tokens_out(self, values):
        zed = lax.axis_index("z")
        rows = self.tokens
        pieces = []
        for turn in range(4):
            piece = values[turn * rows : (turn + 1) * rows]
            pieces.append(send(piece, lambda d, z, y, c: (y, (z - turn) % 4, d, c)))
        order = (jnp.arange(4) - zed) % 4
        result = pieces[0][None]
        for turn in range(1, 4):
            result = jnp.where((order == turn)[:, None, None], pieces[turn][None], result)
        return result

    def rows_gather(self, values, *gates):
        me = lax.axis_index(("dev", "core"))
        rows, wide = values.shape
        mine = jnp.concatenate([values, after(across(values), *gates)], axis=0)
        whole = jnp.zeros((4 * rows, wide), values.dtype)
        for step, pair in enumerate((mine, beside(mine))):
            for far in range(2):
                piece = pair[far * rows : (far + 1) * rows]
                whole = lax.dynamic_update_slice(whole, piece, ((me ^ (step + 2 * far)) * rows, 0))
        return whole

    def rows_scatter(self, values):
        return self.rows_end(self.rows_near(values))

    def rows_near(self, values):
        rows = self.rows
        me = lax.axis_index(("dev", "core"))

        def part(step):
            return lax.dynamic_slice_in_dim(values, (me ^ step) * rows, rows, 0)

        near = jnp.concatenate([part(1), part(3)], axis=0)
        came = beside(near.astype(BF16))
        low, high = came[:rows].astype(F32), came[rows:].astype(F32)
        return part(0) + low, (part(2) + high).astype(BF16)

    def rows_end(self, sums):
        return sums[0] + across(sums[1]).astype(F32)

    def own_rows(self, values):
        me = lax.axis_index(("dev", "core"))
        return lax.dynamic_slice_in_dim(values, me * self.rows, self.rows, 0)

    def heads_gather(self, values):
        me = lax.axis_index(("dev", "core"))
        mine = jnp.concatenate([values, across(values)], axis=0)
        pieces = [mine, beside(mine)]
        block = values.shape[0]
        spots = [[(me ^ (step + 2 * far)) * block for far in range(2)] for step in range(2)]
        return pieces, spots

    def weights(self, w_qkv, w_out, mlp, packed, *gates):
        third = w_qkv.shape[1] // 3
        half = third // 2
        wide = w_out.shape[1]
        count = packed.shape[1]
        first = lax.axis_index("dev") == 0
        lines = -(-count // ((third + wide) * 8)) * 8
        sheet = jnp.pad(packed[0], (0, lines * (third + wide) - count)).reshape(lines, -1)
        message = jnp.concatenate([w_qkv[:, third : 2 * third], w_out], axis=1)
        came = across(jnp.concatenate([message, sheet], axis=0))
        rows = w_qkv.shape[0]
        vectors = came[rows:].reshape(1, -1)[:, :count]
        vectors = jnp.concatenate(
            [jnp.where(first, packed, vectors), jnp.where(first, vectors, packed)], axis=0
        )
        came_qkv, came_out = came[:rows, :third], came[:rows, third:]
        low, high = w_qkv[:, :third], w_qkv[:, 2 * third :]
        query = jnp.where(first, low, came_qkv)
        keys = jnp.where(first, high, low)
        values = jnp.where(first, came_qkv, high)
        blocks = [
            jnp.concatenate(
                [item[:, side * half : (side + 1) * half] for item in (query, keys, values)], axis=1
            )
            for side in range(2)
        ]
        block = -(-3 * half // 128) * 128
        blocks = [jnp.pad(item, ((0, 0), (0, block - 3 * half))) for item in blocks]
        everyone = ("z", "y", "core")
        outs = [jnp.where(first, w_out, came_out), jnp.where(first, came_out, w_out)]
        full_qkv = jnp.concatenate([*blocks, *outs], axis=1)
        full_qkv = lax.all_gather(full_qkv, everyone, axis=0, tiled=True)
        rest = after(jnp.concatenate(mlp, axis=1), full_qkv, *gates)
        rest = lax.all_gather(rest, everyone, axis=0, tiled=True)
        pick = lax.axis_index("core").reshape(1)
        return full_qkv, block, full_qkv[:, 2 * block :], rest, pick, vectors

    def turned(self):
        me = lax.axis_index(("dev", "core"))
        return [((k ^ me) % 2) * 2 + (k ^ me) // 2 for k in range(4)]

    def halve(self, block):
        upper = lax.axis_index("core") == 0
        rows = block.shape[0] // 2
        low, high = block[:rows], block[rows:]
        keep = jnp.where(upper, low, high)
        got = beside(jnp.where(upper, high, low).astype(BF16)).astype(F32)
        return jnp.where(upper, keep, got), jnp.where(upper, got, keep)

    def mlp_grads(self, grads):
        return lax.psum_scatter(grads, ("z", "y"), scatter_dimension=0, tiled=True)

    def mlp_halves(self, grads):
        return self.halve(grads.astype(F32))

    def attention_grads(self, grad_qkv, grad_out):
        block = grad_out.shape[1]
        rows = grad_qkv.shape[0] // 8
        why = lax.axis_index("y")
        order = grad_out.reshape(4, 2, rows, block)
        order = jnp.stack([lax.dynamic_index_in_dim(order, k, 0, False) for k in self.turned()])
        both = jnp.concatenate([order, grad_qkv.reshape(4, 2, rows, -1)], axis=3)
        mine = lax.dynamic_index_in_dim(both, why, 1, False)
        return mine, upright(lax.dynamic_index_in_dim(both, 1 - why, 1, False))

    def attention_sums(self, parts, *gates):
        mine = parts[0].astype(F32) + after(parts[1], *gates).astype(F32)
        mine = mine.astype(BF16).reshape(-1, mine.shape[2])
        return lax.psum_scatter(mine, "z", scatter_dimension=0, tiled=True), mine

    def attention_ends(self, both, block):
        first = lax.axis_index("dev") == 0
        left, right = self.halve(both.astype(F32))
        out = jnp.concatenate([left[:, :block], right[:, :block]], axis=1)
        query, keys, values = (
            jnp.concatenate([left[:, k * block : (k + 1) * block], right[:, k * block : (k + 1) * block]], axis=1)
            for k in (1, 2, 3)
        )
        came = across(jnp.where(first, values, query).astype(BF16)).astype(F32)
        return (
            jnp.concatenate(
                [jnp.where(first, query, keys), came, jnp.where(first, keys, values)], axis=1
            ),
            out,
        )

    def total(self, values):
        everyone = ("dev", "z", "y", "core")
        wide = values.shape[1]
        each = -(-wide // (32 * 128)) * 128
        parts = jnp.pad(values[0], (0, 32 * each - wide)).reshape(32, each)
        parts = lax.all_to_all(parts, everyone, 0, 0, tiled=True)
        mine = jnp.sum(parts, axis=0, keepdims=True)
        every = jnp.broadcast_to(mine, (32, each))
        return lax.all_to_all(every, everyone, 0, 0, tiled=True).reshape(1, -1)[:, :wide]


def norm_back(grad, unit, inverse, gain):
    scaled = grad * gain
    mean = jnp.mean(scaled, axis=-1, keepdims=True)
    along = jnp.mean(scaled * unit, axis=-1, keepdims=True)
    return (scaled - mean - unit * along) * inverse


def gelu_pair(hidden):
    root = 0.7978845608028654
    inner = jnp.tanh(root * (hidden + 0.044715 * hidden * hidden * hidden))
    half = 0.5 * (1.0 + inner)
    slope = half + 0.5 * hidden * (1.0 - inner * inner) * root * (
        1.0 + 3 * 0.044715 * hidden * hidden
    )
    return hidden * half, slope


def per_device(
    sizes,
    patches,
    patch_mask,
    cotangent,
    w_qkv,
    w_out,
    w_up,
    w_down,
    *vectors,
):
    images, tokens, width = patches.shape
    paired = sizes == (2, 4, 2) and images == 4 and Paired is not Native
    route = (Paired if paired else Native)(sizes, images, tokens)
    dev_count = sizes[0]
    team = route.team
    dev = lax.axis_index("dev")
    me = lax.axis_index(("dev", "core"))
    head_count = HEADS // team
    block = head_count * HEAD_DIM
    hidden = w_up.shape[1] // 2

    padded = -(-hidden // 128) * 128
    sides = [
        jnp.concatenate(
            [
                jnp.pad(item[:, side * hidden : (side + 1) * hidden], ((0, 0), (0, padded - hidden)))
                for item in (w_up, w_down)
            ],
            axis=1,
        )
        for side in range(2)
    ]
    marks = jnp.broadcast_to(patch_mask.astype(BF16)[:, :, None], (images, tokens, 128))
    own_in = route.tokens_in(jnp.concatenate([patches, marks, cotangent], axis=2))
    packed = jnp.concatenate(vectors, axis=1)
    own_qkv, qkv_block, full_out, mlp, pick, halves = route.weights(
        w_qkv, w_out, sides, packed, own_in
    )
    own_in, own_grad = own_in[:, : width + 128], own_in[:, width + 128 :]
    rows_all = route.rows_gather(own_in)
    halves = halves.astype(F32)
    full = []
    spot = 0
    for item in vectors:
        full.append(halves[:, spot : spot + item.shape[1]].reshape(1, -1))
        spot += item.shape[1]
    gain_one, shift_one, gain_two, shift_two = full[:4]
    bias_query, bias_value, bias_out, bias_up, bias_down = full[4:]

    qkv_bias = jnp.concatenate(
        [
            lax.dynamic_slice_in_dim(bias_query, me * block, block, 1),
            jnp.zeros((1, block), F32),
            lax.dynamic_slice_in_dim(bias_value, me * block, block, 1),
        ],
        axis=1,
    )
    normed_one, projected = project(
        pick, rows_all, gain_one, shift_one, own_qkv, qkv_block, qkv_bias
    )
    rows_grad = route.rows_gather(after(own_grad, projected))
    seq = projected.shape[0] // route.each
    projected = projected.reshape(route.each, seq, 3 * block)
    marks = rows_all[:, width : width + 1].astype(F32).reshape(route.each, seq, 1)
    length = jnp.sum(marks, axis=1, keepdims=True)
    spot = route.positions(lax.broadcasted_iota(jnp.int32, (route.each, seq, 1), 1))
    mask_bias = jnp.where(spot.astype(F32) < length, 0.0, -1e30).astype(F32)

    attended, lse = attend_fwd(projected, mask_bias, head_count)
    pieces, spots = route.heads_gather(attended.transpose(1, 0, 2).reshape(block, -1))

    def by_piece(whole):
        size = pieces[0].shape[0] // len(spots[0])
        return jnp.stack(
            [
                jnp.concatenate([lax.dynamic_slice_in_dim(whole, at, size, 0) for at in group])
                for group in spots
            ]
        )

    middle, normed_two = attend_out(
        pieces, by_piece(full_out), rows_all, bias_out, gain_two, shift_two
    )
    up_bias = lax.dynamic_slice_in_dim(bias_up, me * hidden, hidden, 1)
    up_bias = jnp.pad(up_bias, ((0, 0), (0, padded - hidden)))

    active, grad_hidden, grad_part_two, up_sums = mlp_turn(
        pick, normed_two, rows_grad, mlp, up_bias
    )
    near_two = route.rows_near(grad_part_two)
    grad_mlp = weight_grads(
        [rows_grad, normed_two], [active, grad_hidden], "mlp_grads"
    )
    sum_mlp = route.mlp_grads(grad_mlp)
    grad_normed_two = after(route.rows_end(near_two), grad_mlp)
    own_middle = route.own_rows(middle)
    own_unit_two, own_inverse_two = centred(own_middle)
    grad_middle = own_grad.astype(F32) + norm_back(
        grad_normed_two, own_unit_two, own_inverse_two, gain_two
    )
    own_branch = grad_middle.astype(BF16)
    mlp_part = mlp_out(pick, after(active, own_branch), mlp)
    grad_branch = route.rows_gather(own_branch, mlp_part)

    grad_projected = attend_bwd(
        projected,
        mask_bias,
        lse,
        grad_branch.reshape(route.each, seq, width),
        lax.dynamic_slice_in_dim(full_out, me * block, block, 0),
        head_count,
    ).reshape(-1, 3 * block)
    my_branch = lax.dynamic_slice_in_dim(after(grad_branch, grad_projected), me * block, block, 1)
    grad_out = out_grads(pieces, my_branch)
    grad_qkv = weight_grads([normed_one], [grad_projected], "qkv_grads")
    attn_parts = route.attention_grads(grad_qkv, grad_out)
    grad_projected = after(grad_projected, attn_parts[0])

    grad_part_one, norm_sums, proj_sums = project_back(
        pick, grad_projected, own_qkv, qkv_block, rows_all, width
    )
    near_one = route.rows_near(grad_part_one)
    grad_normed_one = route.rows_end(near_one)
    mlp_near = route.rows_near(after(mlp_part, near_one[1]))
    result = (own_middle + route.rows_end(mlp_near) + bias_down).astype(BF16)
    result = route.tokens_out(result)

    own_unit_one, own_inverse_one = centred(
        route.own_rows(after(rows_all, near_one[1]))[:, :width].astype(F32)
    )
    grad_inputs = grad_middle + norm_back(
        grad_normed_one, own_unit_one, own_inverse_one, gain_one
    )
    sums_out, sent = route.attention_sums(attn_parts, grad_inputs, sum_mlp)
    grad_inputs = after(grad_inputs.astype(BF16), sent)
    grad_patches = route.tokens_out(grad_inputs)

    out_qkv, out_out = route.attention_ends(sums_out, block)
    out_mlp = route.mlp_halves(sum_mlp)
    out_down, out_up = (
        jnp.concatenate([side[:, spot : spot + hidden] for side in out_mlp], axis=1)
        for spot in (0, padded)
    )

    def spread(values, size):
        return lax.dynamic_update_slice(
            jnp.zeros((size,), F32), values, (me * values.shape[0],)
        )

    norm_sums, proj_sums, up_sums = (
        after(item, grad_inputs) for item in (norm_sums, proj_sums, up_sums)
    )
    sums = [
        norm_sums[0],
        norm_sums[1],
        jnp.sum(grad_normed_two * own_unit_two, axis=0),
        jnp.sum(grad_normed_two, axis=0),
        spread(proj_sums[0, :block], width),
        spread(proj_sums[0, 2 * block :], width),
        jnp.sum(own_branch.astype(F32), axis=0),
        spread(up_sums[0, :hidden], hidden * team),
        jnp.sum(after(cotangent, grad_inputs).astype(F32), axis=(0, 1)),
    ]
    flat = route.total(after(jnp.concatenate(sums)[None], grad_inputs))
    out_vectors = []
    spot = 0
    for item in sums:
        size = item.shape[0]
        half = size // dev_count
        out_vectors.append(lax.dynamic_slice(flat, (0, spot + dev * half), (1, half)))
        spot += size
    return (result, grad_patches, out_qkv, out_out, out_up, out_down, *out_vectors)


def solution(mesh):
    dev_count, sa_count = mesh.devices.shape

    def whole(*args):
        zed = args[0].shape[0] // dev_count
        why = sa_count // (2 * zed)
        sizes = (dev_count, zed, why)
        inner = Mesh(mesh.devices.reshape(dev_count, zed, why, 2), ("dev", "z", "y", "core"))
        rows = ("z", "y", "core")
        token = P("dev", rows, None)
        weight = P(rows, "dev")
        vector = P(None, "dev")
        return jax.shard_map(
            functools.partial(per_device, sizes),
            mesh=inner,
            in_specs=(token, P("dev", rows), token) + (weight,) * 4 + (vector,) * 9,
            out_specs=(token, token) + (weight,) * 4 + (vector,) * 9,
            check_vma=False,
        )(*args)

    return whole
```

```python
import functools

import jax
import jax.numpy as jnp
from jax import lax
from jax.experimental import pallas as pl
from jax.experimental.pallas import tpu as pltpu
from jax.experimental.layout import Layout, with_layout_constraint
from jax.sharding import Mesh
from jax.sharding import PartitionSpec as P

HEADS = 16
HEAD_DIM = 72
SCALE = HEAD_DIM ** (-0.5)
Q_BLOCK = 256
BEHIND = ("mlp_out", "attend_bwd", "out_grads", "qkv_grads", "project_back")
F32 = jnp.float32
BF16 = jnp.bfloat16


def dot(left, right):
    return jnp.dot(left, right, preferred_element_type=F32)


def dot_tn(left, right):
    return lax.dot_general(left, right, (((0,), (0,)), ((), ())), preferred_element_type=F32)


def dot_nt(left, right):
    return lax.dot_general(left, right, (((1,), (1,)), ((), ())), preferred_element_type=F32)


def row_major(values):
    return with_layout_constraint(values, Layout(tuple(range(values.ndim))))


def after(value, *others):
    if not others:
        return value
    return lax.optimization_barrier((value, *others))[0]


def attend_fwd_body(heads, qkv_ref, bias_ref, out_ref, lse_ref):
    width = heads * HEAD_DIM
    rows = pl.ds(pl.program_id(1) * Q_BLOCK, Q_BLOCK)
    bias = bias_ref[0]
    for head in range(heads):
        low = head * HEAD_DIM
        query = qkv_ref[0, rows, low : low + HEAD_DIM]
        keys = qkv_ref[0, :, width + low : width + low + HEAD_DIM]
        values = qkv_ref[0, :, 2 * width + low : 2 * width + low + HEAD_DIM]
        scores = dot_nt(keys, query) * SCALE + bias
        peak = jnp.max(scores, axis=0, keepdims=True)
        expo = jnp.exp(scores - peak)
        total = jnp.sum(expo, axis=0, keepdims=True)
        mixed = dot_tn(values, expo.astype(BF16)) / total
        out_ref[0, low : low + HEAD_DIM, :] = mixed.astype(BF16)
        lse_ref[0, head : head + 1, :] = peak + jnp.log(total)
    if heads < 8:
        lse_ref[0, heads:, :] = jnp.zeros((8 - heads, Q_BLOCK), F32)


def attend_bwd_body(
    heads, qkv_ref, bias_ref, lse_ref, branch_ref, w_ref, out_ref, key_acc, value_acc, grad_ref
):
    width = heads * HEAD_DIM
    step = pl.program_id(1)
    begin = step * Q_BLOCK
    bias = bias_ref[0]

    @pl.when(step == 0)
    def _():
        key_acc[...] = jnp.zeros_like(key_acc)
        value_acc[...] = jnp.zeros_like(value_acc)

    grad_ref[...] = dot_nt(branch_ref[0], w_ref[...]).astype(BF16)
    for head in range(heads):
        low = head * HEAD_DIM
        rows = pl.ds(begin, Q_BLOCK)
        query = qkv_ref[0, rows, low : low + HEAD_DIM]
        grad = grad_ref[:, low : low + HEAD_DIM]
        keys = qkv_ref[0, :, width + low : width + low + HEAD_DIM]
        values = qkv_ref[0, :, 2 * width + low : 2 * width + low + HEAD_DIM]
        scores = dot_nt(keys, query) * SCALE + bias
        probs = jnp.exp(scores - lse_ref[0, head : head + 1, :])
        value_acc[head] += dot(probs.astype(BF16), grad)
        grad_probs = dot_nt(values, grad)
        term = jnp.sum(probs * grad_probs, axis=0, keepdims=True)
        grad_scores = (probs * (grad_probs - term)).astype(BF16)
        key_acc[head] += dot(grad_scores, query)
        grad_query = dot_tn(grad_scores, keys) * SCALE
        out_ref[0, rows, low : low + HEAD_DIM] = grad_query.astype(BF16)

    @pl.when(step == pl.num_programs(1) - 1)
    def _():
        for head in range(heads):
            low = head * HEAD_DIM
            out_ref[0, :, width + low : width + low + HEAD_DIM] = (key_acc[head] * SCALE).astype(BF16)
            out_ref[0, :, 2 * width + low : 2 * width + low + HEAD_DIM] = value_acc[head].astype(BF16)


def run(body, name, steps, operands, specs, outs, out_specs, flops, scratch=(), pick=None):
    share = 50 if name in BEHIND else 1
    size = sum(item.size * item.dtype.itemsize for item in operands)
    picks = () if pick is None else (pick,)
    return pl.pallas_call(
        body,
        name=name,
        grid_spec=pltpu.PrefetchScalarGridSpec(
            num_scalar_prefetch=len(picks),
            grid=steps,
            in_specs=specs,
            out_specs=out_specs,
            scratch_shapes=scratch,
        ),
        out_shape=outs,
        cost_estimate=pl.CostEstimate(
            flops=flops // share, transcendentals=0, bytes_accessed=size // share
        ),
        compiler_params=pltpu.CompilerParams(vmem_limit_bytes=50 << 20),
    )(*picks, *operands)


def rows_spec(wide):
    return pl.BlockSpec((Q_BLOCK, wide), lambda i, *_: (i, 0))


def fixed(item):
    shape = item.shape
    return pl.BlockSpec(shape, lambda *_: (0,) * len(shape))


def picked(item, wide):
    return pl.BlockSpec((item.shape[0], wide), lambda i, pick: (0, pick[0]))


def shaped(shape, dtype):
    return jax.ShapeDtypeStruct(shape, dtype)


def attend_fwd(qkv, bias, heads):
    images, seq, wide = qkv.shape
    width = heads * HEAD_DIM
    return run(
        functools.partial(attend_fwd_body, heads),
        "attend_fwd",
        (images, seq // Q_BLOCK),
        (qkv, bias),
        [
            pl.BlockSpec((1, seq, wide), lambda i, j: (i, 0, 0)),
            pl.BlockSpec((1, seq, 1), lambda i, j: (i, 0, 0)),
        ],
        [shaped((images, width, seq), BF16), shaped((images, 8, seq), F32)],
        [
            pl.BlockSpec((1, width, Q_BLOCK), lambda i, j: (i, 0, j)),
            pl.BlockSpec((1, 8, Q_BLOCK), lambda i, j: (i, 0, j)),
        ],
        4 * images * heads * seq * seq * 128,
    )


def attend_bwd(qkv, bias, lse, branch, w_rows, heads):
    images, seq, wide = qkv.shape
    return run(
        functools.partial(attend_bwd_body, heads),
        "attend_bwd",
        (images, seq // Q_BLOCK),
        (qkv, bias, lse, branch, w_rows),
        [
            pl.BlockSpec((1, seq, wide), lambda i, j: (i, 0, 0)),
            pl.BlockSpec((1, seq, 1), lambda i, j: (i, 0, 0)),
            pl.BlockSpec((1, 8, Q_BLOCK), lambda i, j: (i, 0, j)),
            pl.BlockSpec((1, Q_BLOCK, branch.shape[2]), lambda i, j: (i, j, 0)),
            fixed(w_rows),
        ],
        shaped((images, seq, wide), BF16),
        pl.BlockSpec((1, seq, wide), lambda i, j: (i, 0, 0)),
        10 * images * heads * seq * seq * 128,
        [
            pltpu.VMEM((heads, seq, HEAD_DIM), F32),
            pltpu.VMEM((heads, seq, HEAD_DIM), F32),
            pltpu.VMEM((Q_BLOCK, heads * HEAD_DIM), BF16),
        ],
    )


def centred(values):
    centre = values - jnp.mean(values, axis=-1, keepdims=True)
    spread = jnp.mean(centre * centre, axis=-1, keepdims=True)
    inverse = lax.rsqrt(spread + 1e-06)
    return centre * inverse, inverse


def project(pick, rows_all, gain, shift, weight, block, bias):
    count, width = rows_all.shape[0], gain.shape[1]
    wide = bias.shape[1]

    def body(_, rows_ref, gain_ref, shift_ref, weight_ref, bias_ref, normed_ref, out_ref):
        unit = centred(rows_ref[:, :width].astype(F32))[0]
        normed = (unit * gain_ref[...] + shift_ref[...]).astype(BF16)
        normed_ref[...] = normed
        out_ref[...] = (dot(normed, weight_ref[:, :wide]) + bias_ref[...]).astype(BF16)

    operands = (rows_all, gain, shift, weight, bias)
    return run(
        body,
        "project",
        (count // Q_BLOCK,),
        operands,
        [rows_spec(rows_all.shape[1]), fixed(gain), fixed(shift), picked(weight, block), fixed(bias)],
        [shaped((count, width), BF16), shaped((count, wide), BF16)],
        [rows_spec(width), rows_spec(wide)],
        2 * count * width * wide,
        pick=pick,
    )


def attend_out(pieces, weights, rows_all, bias, gain, shift):
    count, width = rows_all.shape[0], gain.shape[1]
    total = len(pieces)
    piece = pieces[0].shape[0]

    def body(*refs):
        piece_refs = refs[:total]
        weight_ref, rows_ref, bias_ref, gain_ref, shift_ref = refs[total:-2]
        middle_ref, normed_ref = refs[-2:]
        branch = dot_tn(piece_refs[0][...], weight_ref[0])
        for k in range(1, total):
            branch += dot_tn(piece_refs[k][...], weight_ref[k])
        middle = rows_ref[:, :width].astype(F32) + (branch + bias_ref[...])
        middle_ref[...] = middle
        normed_ref[...] = (centred(middle)[0] * gain_ref[...] + shift_ref[...]).astype(BF16)

    return run(
        body,
        "attend_out",
        (count // Q_BLOCK,),
        (*pieces, weights, rows_all, bias, gain, shift),
        [pl.BlockSpec((piece, Q_BLOCK), lambda i: (0, i))] * total
        + [fixed(weights), rows_spec(rows_all.shape[1])]
        + [fixed(bias), fixed(gain), fixed(shift)],
        [shaped((count, width), F32), shaped((count, width), BF16)],
        [rows_spec(width), rows_spec(width)],
        2 * count * width * width,
    )


def mlp_turn(pick, normed, grad, mlp, bias):
    count, width = normed.shape
    hidden = bias.shape[1]

    def body(_, normed_ref, grad_ref, mlp_ref, bias_ref, active_ref, slope_ref, back_ref, sums_ref):
        pre = dot(normed_ref[...], mlp_ref[:, :hidden]) + bias_ref[...]
        active, slope = gelu_pair(pre)
        active_ref[...] = active.astype(BF16)
        grad_hidden = (dot(grad_ref[...], mlp_ref[:, hidden : 2 * hidden]) * slope).astype(BF16)
        slope_ref[...] = grad_hidden
        back_ref[...] = dot_nt(grad_hidden, mlp_ref[:, :hidden]).astype(BF16)
        sums = jnp.sum(grad_hidden.astype(F32), axis=0, keepdims=True)

        @pl.when(pl.program_id(0) == 0)
        def _():
            sums_ref[...] = sums

        @pl.when(pl.program_id(0) > 0)
        def _():
            sums_ref[...] += sums

    return run(
        body,
        "mlp_turn",
        (count // Q_BLOCK,),
        (normed, grad, mlp, bias),
        [rows_spec(width), rows_spec(width), picked(mlp, 2 * hidden), fixed(bias)],
        [
            shaped((count, hidden), BF16),
            shaped((count, hidden), BF16),
            shaped((count, width), BF16),
            shaped((1, hidden), F32),
        ],
        [rows_spec(hidden), rows_spec(hidden), rows_spec(width), fixed(bias)],
        6 * count * width * hidden,
        pick=pick,
    )


def mlp_out(pick, active, mlp):
    count, hidden = active.shape
    width = mlp.shape[0]

    def body(_, active_ref, mlp_ref, out_ref):
        out_ref[...] = dot_nt(active_ref[...], mlp_ref[:, hidden : 2 * hidden]).astype(BF16)

    return run(
        body,
        "mlp_out",
        (count // Q_BLOCK,),
        (active, mlp),
        [rows_spec(hidden), picked(mlp, 2 * hidden)],
        shaped((count, width), BF16),
        rows_spec(width),
        2 * count * width * hidden,
        pick=pick,
    )


def weight_grads(lefts, rights, name):
    count, width = lefts[0].shape
    wides = [item.shape[1] for item in rights]
    tile = 384
    total = len(lefts)

    def body(*refs):
        out_ref = refs[-1]
        spot = 0
        for k in range(total):
            product = dot_tn(refs[k][...], refs[total + k][...])
            out_ref[:, spot : spot + wides[k]] = product.astype(BF16)
            spot += wides[k]

    return run(
        body,
        name,
        (width // tile,),
        (*lefts, *rights),
        [pl.BlockSpec((count, tile), lambda i, *_: (0, i))] * total + [fixed(item) for item in rights],
        shaped((width, sum(wides)), BF16),
        pl.BlockSpec((tile, sum(wides)), lambda i: (i, 0)),
        2 * count * width * sum(wides),
    )


def out_grads(pieces, branch):
    total = len(pieces)
    piece = pieces[0].shape[0]
    wide = branch.shape[1]

    def body(*refs):
        for k in range(total):
            product = dot(refs[k][...], refs[total][...])
            refs[-1][k * piece : (k + 1) * piece, :] = product.astype(BF16)

    operands = (*pieces, branch)
    out = shaped((total * piece, wide), BF16)
    return run(
        body,
        "out_grads",
        (1,),
        operands,
        [fixed(item) for item in operands],
        out,
        fixed(out),
        2 * branch.shape[0] * total * piece * wide,
    )


def project_back(pick, grad, weight, block, rows_all, width):
    count, wide = grad.shape

    def body(_, grad_ref, weight_ref, rows_ref, back_ref, norm_ref, bias_ref):
        back = dot_nt(grad_ref[...], weight_ref[:, :wide])
        back_ref[...] = back.astype(BF16)
        unit = centred(rows_ref[:, :width].astype(F32))[0]
        gain = jnp.sum(back * unit, axis=0, keepdims=True)
        shift = jnp.sum(back, axis=0, keepdims=True)
        bias = jnp.sum(grad_ref[...].astype(F32), axis=0, keepdims=True)

        @pl.when(pl.program_id(0) == 0)
        def _():
            norm_ref[...] = jnp.zeros_like(norm_ref)
            bias_ref[...] = jnp.zeros_like(bias_ref)

        norm_ref[0:1] += gain
        norm_ref[1:2] += shift
        bias_ref[...] += bias

    return run(
        body,
        "project_back",
        (count // Q_BLOCK,),
        (grad, weight, rows_all),
        [rows_spec(wide), picked(weight, block), rows_spec(rows_all.shape[1])],
        [shaped((count, width), BF16), shaped((2, width), F32), shaped((1, wide), F32)],
        [
            rows_spec(width),
            pl.BlockSpec((2, width), lambda *_: (0, 0)),
            pl.BlockSpec((1, wide), lambda *_: (0, 0)),
        ],
        2 * count * width * wide,
        pick=pick,
    )


class Native:
    def __init__(self, sizes, images, tokens):
        self.dev, self.zed, self.why = sizes
        self.images = images
        self.tokens = tokens
        self.team = self.dev * 2
        self.groups = self.zed * self.why
        self.each = images * self.dev // self.groups
        self.piece = tokens // self.dev
        self.rows = self.each * self.groups * self.piece

    def positions(self, row):
        place = row % self.piece
        group = (row // self.piece) % self.groups
        team = row // (self.piece * self.groups)
        owner = group * 2 + team % 2
        return owner * self.tokens + (team // 2) * self.piece + place

    def tokens_in(self, values):
        wide = values.shape[-1]
        split = values.reshape(self.images, self.dev, self.piece, wide)
        split = lax.all_to_all(split, "dev", 1, 0, tiled=True)
        split = split.reshape(self.groups, self.each, self.piece, wide)
        split = lax.all_to_all(split, ("z", "y"), 0, 0, tiled=True)
        return split.transpose(1, 0, 2, 3).reshape(self.rows, wide)

    def tokens_out(self, values):
        wide = values.shape[-1]
        split = values.reshape(self.each, self.groups, self.piece, wide).transpose(1, 0, 2, 3)
        split = lax.all_to_all(split, ("z", "y"), 0, 0, tiled=True)
        split = split.reshape(self.dev * self.images, 1, self.piece, wide)
        split = lax.all_to_all(split, "dev", 0, 1, tiled=True)
        return split.reshape(self.images, self.tokens, wide)

    def rows_gather(self, values, *gates):
        wide = values.shape[-1]
        whole = lax.all_gather(values, ("dev", "core"), axis=0, tiled=True)
        whole = whole.reshape(self.team, self.each, -1, wide).transpose(1, 0, 2, 3)
        return whole.reshape(self.team * self.rows, wide)

    def rows_scatter(self, values):
        wide = values.shape[-1]
        split = values.astype(BF16).reshape(self.each, self.team, -1, wide).transpose(1, 0, 2, 3)
        split = split.reshape(self.team * self.rows, wide)
        return lax.psum_scatter(
            split, ("dev", "core"), scatter_dimension=0, tiled=True
        ).astype(F32)

    def rows_near(self, values):
        return values, values

    def rows_end(self, sums):
        return self.rows_scatter(sums[0])

    def own_rows(self, values):
        wide = values.shape[-1]
        me = lax.axis_index(("dev", "core"))
        split = values.reshape(self.each, self.team, -1, wide)
        return lax.dynamic_slice_in_dim(split, me, 1, 1).reshape(self.rows, wide)

    def heads_gather(self, values):
        return [lax.all_gather(values, ("dev", "core"), axis=0, tiled=True)], [[0]]

    def weights(self, w_qkv, w_out, mlp, packed, *gates):
        whole = lax.all_gather(w_qkv, "dev", axis=1, tiled=True)
        rows, wide = whole.shape
        split = whole.reshape(rows, 3, self.team, wide // (3 * self.team))
        split = lax.dynamic_slice_in_dim(split, 2 * lax.axis_index("dev"), 2, 2)
        split = split.transpose(0, 2, 1, 3).reshape(rows, -1)
        split = lax.all_to_all(split, "core", 1, 0, tiled=True)
        full_qkv = lax.all_gather(split, ("z", "y"), axis=0, tiled=True)
        full_out = lax.all_gather(w_out, "dev", axis=1, tiled=True)
        full_out = lax.all_gather(full_out, ("z", "y", "core"), axis=0, tiled=True)
        mlp = jnp.concatenate(mlp, axis=1)
        mlp = lax.all_to_all(mlp, "core", 1, 0, tiled=True)
        mlp = lax.all_gather(mlp, ("z", "y"), axis=0, tiled=True)
        vectors = lax.all_gather(packed, "dev", axis=0, tiled=True)
        return full_qkv, full_qkv.shape[1], full_out, mlp, jnp.zeros((1,), jnp.int32), vectors

    def mlp_grads(self, grads):
        return lax.psum_scatter(grads, ("z", "y"), scatter_dimension=0, tiled=True)

    def mlp_halves(self, grads):
        grads = lax.all_to_all(grads, "core", 0, 1, tiled=True).astype(F32)
        half = grads.shape[1] // 2
        return grads[:, :half], grads[:, half:]

    def attention_grads(self, grad_qkv, grad_out):
        return grad_qkv, grad_out

    def attention_sums(self, parts, *gates):
        both = jnp.concatenate([parts[1], parts[0]], axis=1)
        return lax.psum_scatter(both, ("z", "y"), scatter_dimension=0, tiled=True), both

    def attention_ends(self, both, block):
        out = lax.all_to_all(both[:, :block], "core", 0, 1, tiled=True)
        piece = lax.all_to_all(both[:, block:], "core", 0, 1, tiled=True)
        rows = piece.shape[0]
        piece = piece.reshape(rows, 2, 3, block).transpose(0, 2, 1, 3).reshape(rows, 3, 1, -1)
        whole = lax.all_gather(piece, "dev", axis=2, tiled=True)
        whole = whole.reshape(rows, self.dev, 6 * block)
        mine = lax.dynamic_slice_in_dim(whole, lax.axis_index("dev"), 1, 1)[:, 0]
        return mine.astype(F32), out.astype(F32)

    def total(self, values):
        return lax.psum(values, ("dev", "z", "y", "core"))


def joint(move):
    pairs = []
    for dev in range(2):
        for zed in range(4):
            for why in range(2):
                for core in range(2):
                    to = move(dev, zed, why, core)
                    source = ((dev * 4 + zed) * 2 + why) * 2 + core
                    pairs.append((source, ((to[0] * 4 + to[1]) * 2 + to[2]) * 2 + to[3]))
    return pairs


def send(values, move):
    return lax.ppermute(values, ("dev", "z", "y", "core"), joint(move))


def across(values):
    return send(values, lambda d, z, y, c: (1 - d, z, y, c))


def beside(values):
    return send(values, lambda d, z, y, c: (d, z, y, 1 - c))


def upright(values):
    return send(values, lambda d, z, y, c: (d, z, 1 - y, c))


class Paired(Native):
    def positions(self, row):
        place = row % self.tokens
        turn = (row // self.tokens) % 4
        team = row // (self.tokens * 4)
        zed = (lax.axis_index("z") - turn) % 4
        return ((zed * 2 + team // 2) * 2 + team % 2) * self.tokens + place

    def tokens_in(self, values):
        zed = lax.axis_index("z")
        pieces = []
        for turn in range(4):
            piece = lax.dynamic_slice_in_dim(values, (zed + turn) % 4, 1, 0)[0]
            pieces.append(send(piece, lambda d, z, y, c: (y, (z + turn) % 4, d, c)))
        return jnp.concatenate(pieces, axis=0)

    def tokens_out(self, values):
        zed = lax.axis_index("z")
        rows = self.tokens
        pieces = []
        for turn in range(4):
            piece = values[turn * rows : (turn + 1) * rows]
            pieces.append(send(piece, lambda d, z, y, c: (y, (z - turn) % 4, d, c)))
        order = (jnp.arange(4) - zed) % 4
        result = pieces[0][None]
        for turn in range(1, 4):
            result = jnp.where((order == turn)[:, None, None], pieces[turn][None], result)
        return result

    def rows_gather(self, values, *gates):
        me = lax.axis_index(("dev", "core"))
        rows, wide = values.shape
        mine = jnp.concatenate([values, after(across(values), *gates)], axis=0)
        whole = jnp.zeros((4 * rows, wide), values.dtype)
        for step, pair in enumerate((mine, beside(mine))):
            for far in range(2):
                piece = pair[far * rows : (far + 1) * rows]
                whole = lax.dynamic_update_slice(whole, piece, ((me ^ (step + 2 * far)) * rows, 0))
        return whole

    def rows_scatter(self, values):
        return self.rows_end(self.rows_near(values))

    def rows_near(self, values):
        rows = self.rows
        me = lax.axis_index(("dev", "core"))

        def part(step):
            return lax.dynamic_slice_in_dim(values, (me ^ step) * rows, rows, 0)

        near = jnp.concatenate([part(1), part(3)], axis=0)
        came = beside(near.astype(BF16))
        low, high = came[:rows].astype(F32), came[rows:].astype(F32)
        return part(0) + low, (part(2) + high).astype(BF16)

    def rows_end(self, sums):
        return sums[0] + across(sums[1]).astype(F32)

    def own_rows(self, values):
        me = lax.axis_index(("dev", "core"))
        return lax.dynamic_slice_in_dim(values, me * self.rows, self.rows, 0)

    def heads_gather(self, values):
        me = lax.axis_index(("dev", "core"))
        mine = jnp.concatenate([values, across(values)], axis=0)
        pieces = [mine, beside(mine)]
        block = values.shape[0]
        spots = [[(me ^ (step + 2 * far)) * block for far in range(2)] for step in range(2)]
        return pieces, spots

    def weights(self, w_qkv, w_out, mlp, packed, *gates):
        third = w_qkv.shape[1] // 3
        half = third // 2
        wide = w_out.shape[1]
        count = packed.shape[1]
        first = lax.axis_index("dev") == 0
        lines = -(-count // ((third + wide) * 8)) * 8
        sheet = jnp.pad(packed[0], (0, lines * (third + wide) - count)).reshape(lines, -1)
        message = jnp.concatenate([w_qkv[:, third : 2 * third], w_out], axis=1)
        came = across(jnp.concatenate([message, sheet], axis=0))
        rows = w_qkv.shape[0]
        vectors = came[rows:].reshape(1, -1)[:, :count]
        vectors = jnp.concatenate(
            [jnp.where(first, packed, vectors), jnp.where(first, vectors, packed)], axis=0
        )
        came_qkv, came_out = came[:rows, :third], came[:rows, third:]
        low, high = w_qkv[:, :third], w_qkv[:, 2 * third :]
        query = jnp.where(first, low, came_qkv)
        keys = jnp.where(first, high, low)
        values = jnp.where(first, came_qkv, high)
        blocks = [
            jnp.concatenate(
                [item[:, side * half : (side + 1) * half] for item in (query, keys, values)], axis=1
            )
            for side in range(2)
        ]
        block = -(-3 * half // 128) * 128
        blocks = [jnp.pad(item, ((0, 0), (0, block - 3 * half))) for item in blocks]
        everyone = ("z", "y", "core")
        outs = [jnp.where(first, w_out, came_out), jnp.where(first, came_out, w_out)]
        full_qkv = jnp.concatenate([*blocks, *outs], axis=1)
        full_qkv = lax.all_gather(full_qkv, everyone, axis=0, tiled=True)
        rest = after(jnp.concatenate(mlp, axis=1), full_qkv, *gates)
        rest = lax.all_gather(rest, everyone, axis=0, tiled=True)
        pick = lax.axis_index("core").reshape(1)
        return full_qkv, block, full_qkv[:, 2 * block :], rest, pick, vectors

    def turned(self):
        me = lax.axis_index(("dev", "core"))
        return [((k ^ me) % 2) * 2 + (k ^ me) // 2 for k in range(4)]

    def halve(self, block):
        upper = lax.axis_index("core") == 0
        rows = block.shape[0] // 2
        low, high = block[:rows], block[rows:]
        keep = jnp.where(upper, low, high)
        got = beside(jnp.where(upper, high, low).astype(BF16)).astype(F32)
        return jnp.where(upper, keep, got), jnp.where(upper, got, keep)

    def mlp_grads(self, grads):
        return lax.psum_scatter(grads, ("z", "y"), scatter_dimension=0, tiled=True)

    def mlp_halves(self, grads):
        return self.halve(grads.astype(F32))

    def attention_grads(self, grad_qkv, grad_out):
        block = grad_out.shape[1]
        rows = grad_qkv.shape[0] // 8
        why = lax.axis_index("y")
        order = grad_out.reshape(4, 2, rows, block)
        order = jnp.stack([lax.dynamic_index_in_dim(order, k, 0, False) for k in self.turned()])
        both = jnp.concatenate([order, grad_qkv.reshape(4, 2, rows, -1)], axis=3)
        mine = lax.dynamic_index_in_dim(both, why, 1, False)
        return mine, upright(lax.dynamic_index_in_dim(both, 1 - why, 1, False))

    def attention_sums(self, parts, *gates):
        mine = parts[0].astype(F32) + after(parts[1], *gates).astype(F32)
        mine = mine.astype(BF16).reshape(-1, mine.shape[2])
        return lax.psum_scatter(mine, "z", scatter_dimension=0, tiled=True), mine

    def attention_ends(self, both, block):
        first = lax.axis_index("dev") == 0
        left, right = self.halve(both.astype(F32))
        out = jnp.concatenate([left[:, :block], right[:, :block]], axis=1)
        query, keys, values = (
            jnp.concatenate([left[:, k * block : (k + 1) * block], right[:, k * block : (k + 1) * block]], axis=1)
            for k in (1, 2, 3)
        )
        came = across(jnp.where(first, values, query).astype(BF16)).astype(F32)
        return (
            jnp.concatenate(
                [jnp.where(first, query, keys), came, jnp.where(first, keys, values)], axis=1
            ),
            out,
        )

    def total(self, values):
        everyone = ("dev", "z", "y", "core")
        wide = values.shape[1]
        each = -(-wide // (32 * 128)) * 128
        parts = jnp.pad(values[0], (0, 32 * each - wide)).reshape(32, each)
        parts = lax.all_to_all(parts, everyone, 0, 0, tiled=True)
        mine = jnp.sum(parts, axis=0, keepdims=True)
        every = jnp.broadcast_to(mine, (32, each))
        return lax.all_to_all(every, everyone, 0, 0, tiled=True).reshape(1, -1)[:, :wide]


def norm_back(grad, unit, inverse, gain):
    scaled = grad * gain
    mean = jnp.mean(scaled, axis=-1, keepdims=True)
    along = jnp.mean(scaled * unit, axis=-1, keepdims=True)
    return (scaled - mean - unit * along) * inverse


def gelu_pair(hidden):
    root = 0.7978845608028654
    inner = jnp.tanh(root * (hidden + 0.044715 * hidden * hidden * hidden))
    half = 0.5 * (1.0 + inner)
    slope = half + 0.5 * hidden * (1.0 - inner * inner) * root * (
        1.0 + 3 * 0.044715 * hidden * hidden
    )
    return hidden * half, slope


def per_device(
    sizes,
    patches,
    patch_mask,
    cotangent,
    w_qkv,
    w_out,
    w_up,
    w_down,
    *vectors,
):
    images, tokens, width = patches.shape
    paired = sizes == (2, 4, 2) and images == 4 and Paired is not Native
    route = (Paired if paired else Native)(sizes, images, tokens)
    dev_count = sizes[0]
    team = route.team
    dev = lax.axis_index("dev")
    me = lax.axis_index(("dev", "core"))
    head_count = HEADS // team
    block = head_count * HEAD_DIM
    hidden = w_up.shape[1] // 2

    padded = -(-hidden // 128) * 128
    sides = [
        jnp.concatenate(
            [
                jnp.pad(item[:, side * hidden : (side + 1) * hidden], ((0, 0), (0, padded - hidden)))
                for item in (w_up, w_down)
            ],
            axis=1,
        )
        for side in range(2)
    ]
    marks = jnp.broadcast_to(patch_mask.astype(BF16)[:, :, None], (images, tokens, 128))
    own_in = route.tokens_in(jnp.concatenate([patches, marks, cotangent], axis=2))
    packed = jnp.concatenate(vectors, axis=1)
    own_qkv, qkv_block, full_out, mlp, pick, halves = route.weights(
        w_qkv, w_out, sides, packed, own_in
    )
    own_in, own_grad = own_in[:, : width + 128], own_in[:, width + 128 :]
    rows_all = route.rows_gather(own_in)
    halves = halves.astype(F32)
    full = []
    spot = 0
    for item in vectors:
        full.append(halves[:, spot : spot + item.shape[1]].reshape(1, -1))
        spot += item.shape[1]
    gain_one, shift_one, gain_two, shift_two = full[:4]
    bias_query, bias_value, bias_out, bias_up, bias_down = full[4:]

    qkv_bias = jnp.concatenate(
        [
            lax.dynamic_slice_in_dim(bias_query, me * block, block, 1),
            jnp.zeros((1, block), F32),
            lax.dynamic_slice_in_dim(bias_value, me * block, block, 1),
        ],
        axis=1,
    )
    normed_one, projected = project(
        pick, rows_all, gain_one, shift_one, own_qkv, qkv_block, qkv_bias
    )
    rows_grad = route.rows_gather(after(own_grad, projected))
    seq = projected.shape[0] // route.each
    projected = projected.reshape(route.each, seq, 3 * block)
    marks = rows_all[:, width : width + 1].astype(F32).reshape(route.each, seq, 1)
    length = jnp.sum(marks, axis=1, keepdims=True)
    spot = route.positions(lax.broadcasted_iota(jnp.int32, (route.each, seq, 1), 1))
    mask_bias = jnp.where(spot.astype(F32) < length, 0.0, -1e30).astype(F32)

    attended, lse = attend_fwd(projected, mask_bias, head_count)
    pieces, spots = route.heads_gather(attended.transpose(1, 0, 2).reshape(block, -1))

    def by_piece(whole):
        size = pieces[0].shape[0] // len(spots[0])
        return jnp.stack(
            [
                jnp.concatenate([lax.dynamic_slice_in_dim(whole, at, size, 0) for at in group])
                for group in spots
            ]
        )

    middle, normed_two = attend_out(
        pieces, by_piece(full_out), rows_all, bias_out, gain_two, shift_two
    )
    up_bias = lax.dynamic_slice_in_dim(bias_up, me * hidden, hidden, 1)
    up_bias = jnp.pad(up_bias, ((0, 0), (0, padded - hidden)))

    active, grad_hidden, grad_part_two, up_sums = mlp_turn(
        pick, normed_two, rows_grad, mlp, up_bias
    )
    near_two = route.rows_near(grad_part_two)
    grad_mlp = weight_grads(
        [rows_grad, normed_two], [active, grad_hidden], "mlp_grads"
    )
    sum_mlp = route.mlp_grads(grad_mlp)
    grad_normed_two = after(route.rows_end(near_two), grad_mlp)
    own_middle = route.own_rows(middle)
    own_unit_two, own_inverse_two = centred(own_middle)
    grad_middle = own_grad.astype(F32) + norm_back(
        grad_normed_two, own_unit_two, own_inverse_two, gain_two
    )
    own_branch = grad_middle.astype(BF16)
    mlp_part = mlp_out(pick, after(active, own_branch), mlp)
    grad_branch = route.rows_gather(own_branch, mlp_part)

    grad_projected = attend_bwd(
        projected,
        mask_bias,
        lse,
        grad_branch.reshape(route.each, seq, width),
        lax.dynamic_slice_in_dim(full_out, me * block, block, 0),
        head_count,
    ).reshape(-1, 3 * block)
    my_branch = lax.dynamic_slice_in_dim(after(grad_branch, grad_projected), me * block, block, 1)
    grad_out = out_grads(pieces, my_branch)
    grad_qkv = weight_grads([normed_one], [grad_projected], "qkv_grads")
    attn_parts = route.attention_grads(grad_qkv, grad_out)
    grad_projected = after(grad_projected, attn_parts[0])

    grad_part_one, norm_sums, proj_sums = project_back(
        pick, grad_projected, own_qkv, qkv_block, rows_all, width
    )
    near_one = route.rows_near(grad_part_one)
    grad_normed_one = route.rows_end(near_one)
    mlp_near = route.rows_near(after(mlp_part, near_one[1]))

    own_unit_one, own_inverse_one = centred(
        route.own_rows(after(rows_all, near_one[1]))[:, :width].astype(F32)
    )
    grad_inputs = grad_middle + norm_back(
        grad_normed_one, own_unit_one, own_inverse_one, gain_one
    )
    sums_out, sent = route.attention_sums(attn_parts, grad_inputs, sum_mlp)
    grad_inputs = after(grad_inputs.astype(BF16), sent)
    grad_patches = route.tokens_out(grad_inputs)
    mlp_near = (mlp_near[0], after(mlp_near[1], sent))
    result = (own_middle + route.rows_end(mlp_near) + bias_down).astype(BF16)
    leaving = result
    result = route.tokens_out(result)

    out_qkv, out_out = route.attention_ends(sums_out, block)
    out_mlp = route.mlp_halves(sum_mlp)
    out_down, out_up = (
        jnp.concatenate([side[:, spot : spot + hidden] for side in out_mlp], axis=1)
        for spot in (0, padded)
    )

    def spread(values, size):
        return lax.dynamic_update_slice(
            jnp.zeros((size,), F32), values, (me * values.shape[0],)
        )

    norm_sums, proj_sums, up_sums = (
        after(item, grad_inputs) for item in (norm_sums, proj_sums, up_sums)
    )
    sums = [
        norm_sums[0],
        norm_sums[1],
        jnp.sum(grad_normed_two * own_unit_two, axis=0),
        jnp.sum(grad_normed_two, axis=0),
        spread(proj_sums[0, :block], width),
        spread(proj_sums[0, 2 * block :], width),
        jnp.sum(own_branch.astype(F32), axis=0),
        spread(up_sums[0, :hidden], hidden * team),
        jnp.sum(after(cotangent, grad_inputs).astype(F32), axis=(0, 1)),
    ]
    flat = route.total(after(jnp.concatenate(sums)[None], grad_inputs, leaving))
    out_vectors = []
    spot = 0
    for item in sums:
        size = item.shape[0]
        half = size // dev_count
        out_vectors.append(lax.dynamic_slice(flat, (0, spot + dev * half), (1, half)))
        spot += size
    return (result, grad_patches, out_qkv, out_out, out_up, out_down, *out_vectors)


def solution(mesh):
    dev_count, sa_count = mesh.devices.shape

    def whole(*args):
        zed = args[0].shape[0] // dev_count
        why = sa_count // (2 * zed)
        sizes = (dev_count, zed, why)
        inner = Mesh(mesh.devices.reshape(dev_count, zed, why, 2), ("dev", "z", "y", "core"))
        rows = ("z", "y", "core")
        token = P("dev", rows, None)
        weight = P(rows, "dev")
        vector = P(None, "dev")
        return jax.shard_map(
            functools.partial(per_device, sizes),
            mesh=inner,
            in_specs=(token, P("dev", rows), token) + (weight,) * 4 + (vector,) * 9,
            out_specs=(token, token) + (weight,) * 4 + (vector,) * 9,
            check_vma=False,
        )(*args)

    return whole
```

```python
import functools

import jax
import jax.numpy as jnp
from jax import lax
from jax.experimental import pallas as pl
from jax.experimental.pallas import tpu as pltpu
from jax.experimental.layout import Layout, with_layout_constraint
from jax.sharding import Mesh
from jax.sharding import PartitionSpec as P

HEADS = 16
HEAD_DIM = 72
SCALE = HEAD_DIM ** (-0.5)
Q_BLOCK = 256
BEHIND = ("mlp_out", "attend_bwd", "out_grads", "qkv_grads", "project_back")
F32 = jnp.float32
BF16 = jnp.bfloat16


def dot(left, right):
    return jnp.dot(left, right, preferred_element_type=F32)


def dot_tn(left, right):
    return lax.dot_general(left, right, (((0,), (0,)), ((), ())), preferred_element_type=F32)


def dot_nt(left, right):
    return lax.dot_general(left, right, (((1,), (1,)), ((), ())), preferred_element_type=F32)


def row_major(values):
    return with_layout_constraint(values, Layout(tuple(range(values.ndim))))


def after(value, *others):
    if not others:
        return value
    return lax.optimization_barrier((value, *others))[0]


def attend_fwd_body(heads, qkv_ref, bias_ref, out_ref, lse_ref):
    width = heads * HEAD_DIM
    rows = pl.ds(pl.program_id(1) * Q_BLOCK, Q_BLOCK)
    bias = bias_ref[0]
    for head in range(heads):
        low = head * HEAD_DIM
        query = qkv_ref[0, rows, low : low + HEAD_DIM]
        keys = qkv_ref[0, :, width + low : width + low + HEAD_DIM]
        values = qkv_ref[0, :, 2 * width + low : 2 * width + low + HEAD_DIM]
        scores = dot_nt(keys, query) * SCALE + bias
        peak = jnp.max(scores, axis=0, keepdims=True)
        expo = jnp.exp(scores - peak)
        total = jnp.sum(expo, axis=0, keepdims=True)
        mixed = dot_tn(values, expo.astype(BF16)) / total
        out_ref[0, low : low + HEAD_DIM, :] = mixed.astype(BF16)
        lse_ref[0, head : head + 1, :] = peak + jnp.log(total)
    if heads < 8:
        lse_ref[0, heads:, :] = jnp.zeros((8 - heads, Q_BLOCK), F32)


def attend_bwd_body(
    heads, qkv_ref, bias_ref, lse_ref, branch_ref, w_ref, out_ref, key_acc, value_acc, grad_ref
):
    width = heads * HEAD_DIM
    step = pl.program_id(1)
    begin = step * Q_BLOCK
    bias = bias_ref[0]

    @pl.when(step == 0)
    def _():
        key_acc[...] = jnp.zeros_like(key_acc)
        value_acc[...] = jnp.zeros_like(value_acc)

    grad_ref[...] = dot_nt(branch_ref[0], w_ref[...]).astype(BF16)
    for head in range(heads):
        low = head * HEAD_DIM
        rows = pl.ds(begin, Q_BLOCK)
        query = qkv_ref[0, rows, low : low + HEAD_DIM]
        grad = grad_ref[:, low : low + HEAD_DIM]
        keys = qkv_ref[0, :, width + low : width + low + HEAD_DIM]
        values = qkv_ref[0, :, 2 * width + low : 2 * width + low + HEAD_DIM]
        scores = dot_nt(keys, query) * SCALE + bias
        probs = jnp.exp(scores - lse_ref[0, head : head + 1, :])
        value_acc[head] += dot(probs.astype(BF16), grad)
        grad_probs = dot_nt(values, grad)
        term = jnp.sum(probs * grad_probs, axis=0, keepdims=True)
        grad_scores = (probs * (grad_probs - term)).astype(BF16)
        key_acc[head] += dot(grad_scores, query)
        grad_query = dot_tn(grad_scores, keys) * SCALE
        out_ref[0, rows, low : low + HEAD_DIM] = grad_query.astype(BF16)

    @pl.when(step == pl.num_programs(1) - 1)
    def _():
        for head in range(heads):
            low = head * HEAD_DIM
            out_ref[0, :, width + low : width + low + HEAD_DIM] = (key_acc[head] * SCALE).astype(BF16)
            out_ref[0, :, 2 * width + low : 2 * width + low + HEAD_DIM] = value_acc[head].astype(BF16)


def run(body, name, steps, operands, specs, outs, out_specs, flops, scratch=(), pick=None):
    share = 50 if name in BEHIND else 1
    size = sum(item.size * item.dtype.itemsize for item in operands)
    picks = () if pick is None else (pick,)
    return pl.pallas_call(
        body,
        name=name,
        grid_spec=pltpu.PrefetchScalarGridSpec(
            num_scalar_prefetch=len(picks),
            grid=steps,
            in_specs=specs,
            out_specs=out_specs,
            scratch_shapes=scratch,
        ),
        out_shape=outs,
        cost_estimate=pl.CostEstimate(
            flops=flops // share, transcendentals=0, bytes_accessed=size // share
        ),
        compiler_params=pltpu.CompilerParams(vmem_limit_bytes=50 << 20),
    )(*picks, *operands)


def rows_spec(wide):
    return pl.BlockSpec((Q_BLOCK, wide), lambda i, *_: (i, 0))


def fixed(item):
    shape = item.shape
    return pl.BlockSpec(shape, lambda *_: (0,) * len(shape))


def picked(item, wide):
    return pl.BlockSpec((item.shape[0], wide), lambda i, pick: (0, pick[0]))


def shaped(shape, dtype):
    return jax.ShapeDtypeStruct(shape, dtype)


def attend_fwd(qkv, bias, heads):
    images, seq, wide = qkv.shape
    width = heads * HEAD_DIM
    return run(
        functools.partial(attend_fwd_body, heads),
        "attend_fwd",
        (images, seq // Q_BLOCK),
        (qkv, bias),
        [
            pl.BlockSpec((1, seq, wide), lambda i, j: (i, 0, 0)),
            pl.BlockSpec((1, seq, 1), lambda i, j: (i, 0, 0)),
        ],
        [shaped((images, width, seq), BF16), shaped((images, 8, seq), F32)],
        [
            pl.BlockSpec((1, width, Q_BLOCK), lambda i, j: (i, 0, j)),
            pl.BlockSpec((1, 8, Q_BLOCK), lambda i, j: (i, 0, j)),
        ],
        4 * images * heads * seq * seq * 128,
    )


def attend_bwd(qkv, bias, lse, branch, w_rows, heads):
    images, seq, wide = qkv.shape
    return run(
        functools.partial(attend_bwd_body, heads),
        "attend_bwd",
        (images, seq // Q_BLOCK),
        (qkv, bias, lse, branch, w_rows),
        [
            pl.BlockSpec((1, seq, wide), lambda i, j: (i, 0, 0)),
            pl.BlockSpec((1, seq, 1), lambda i, j: (i, 0, 0)),
            pl.BlockSpec((1, 8, Q_BLOCK), lambda i, j: (i, 0, j)),
            pl.BlockSpec((1, Q_BLOCK, branch.shape[2]), lambda i, j: (i, j, 0)),
            fixed(w_rows),
        ],
        shaped((images, seq, wide), BF16),
        pl.BlockSpec((1, seq, wide), lambda i, j: (i, 0, 0)),
        10 * images * heads * seq * seq * 128,
        [
            pltpu.VMEM((heads, seq, HEAD_DIM), F32),
            pltpu.VMEM((heads, seq, HEAD_DIM), F32),
            pltpu.VMEM((Q_BLOCK, heads * HEAD_DIM), BF16),
        ],
    )


def centred(values):
    centre = values - jnp.mean(values, axis=-1, keepdims=True)
    spread = jnp.mean(centre * centre, axis=-1, keepdims=True)
    inverse = lax.rsqrt(spread + 1e-06)
    return centre * inverse, inverse


def project(pick, rows_all, gain, shift, weight, block, bias):
    count, width = rows_all.shape[0], gain.shape[1]
    wide = bias.shape[1]

    def body(_, rows_ref, gain_ref, shift_ref, weight_ref, bias_ref, normed_ref, out_ref):
        unit = centred(rows_ref[:, :width].astype(F32))[0]
        normed = (unit * gain_ref[...] + shift_ref[...]).astype(BF16)
        normed_ref[...] = normed
        out_ref[...] = (dot(normed, weight_ref[:, :wide]) + bias_ref[...]).astype(BF16)

    operands = (rows_all, gain, shift, weight, bias)
    return run(
        body,
        "project",
        (count // Q_BLOCK,),
        operands,
        [rows_spec(rows_all.shape[1]), fixed(gain), fixed(shift), picked(weight, block), fixed(bias)],
        [shaped((count, width), BF16), shaped((count, wide), BF16)],
        [rows_spec(width), rows_spec(wide)],
        2 * count * width * wide,
        pick=pick,
    )


def attend_out(pieces, weights, rows_all, bias, gain, shift):
    count, width = rows_all.shape[0], gain.shape[1]
    total = len(pieces)
    piece = pieces[0].shape[0]

    def body(*refs):
        piece_refs = refs[:total]
        weight_ref, rows_ref, bias_ref, gain_ref, shift_ref = refs[total:-2]
        middle_ref, normed_ref = refs[-2:]
        branch = dot_tn(piece_refs[0][...], weight_ref[0])
        for k in range(1, total):
            branch += dot_tn(piece_refs[k][...], weight_ref[k])
        middle = rows_ref[:, :width].astype(F32) + (branch + bias_ref[...])
        middle_ref[...] = middle
        normed_ref[...] = (centred(middle)[0] * gain_ref[...] + shift_ref[...]).astype(BF16)

    return run(
        body,
        "attend_out",
        (count // Q_BLOCK,),
        (*pieces, weights, rows_all, bias, gain, shift),
        [pl.BlockSpec((piece, Q_BLOCK), lambda i: (0, i))] * total
        + [fixed(weights), rows_spec(rows_all.shape[1])]
        + [fixed(bias), fixed(gain), fixed(shift)],
        [shaped((count, width), F32), shaped((count, width), BF16)],
        [rows_spec(width), rows_spec(width)],
        2 * count * width * width,
    )


def mlp_turn(pick, normed, grad, mlp, bias):
    count, width = normed.shape
    hidden = bias.shape[1]

    def body(_, normed_ref, grad_ref, mlp_ref, bias_ref, active_ref, slope_ref, back_ref, sums_ref):
        pre = dot(normed_ref[...], mlp_ref[:, :hidden]) + bias_ref[...]
        active, slope = gelu_pair(pre)
        active_ref[...] = active.astype(BF16)
        grad_hidden = (dot(grad_ref[...], mlp_ref[:, hidden : 2 * hidden]) * slope).astype(BF16)
        slope_ref[...] = grad_hidden
        back_ref[...] = dot_nt(grad_hidden, mlp_ref[:, :hidden]).astype(BF16)
        sums = jnp.sum(grad_hidden.astype(F32), axis=0, keepdims=True)

        @pl.when(pl.program_id(0) == 0)
        def _():
            sums_ref[...] = sums

        @pl.when(pl.program_id(0) > 0)
        def _():
            sums_ref[...] += sums

    return run(
        body,
        "mlp_turn",
        (count // Q_BLOCK,),
        (normed, grad, mlp, bias),
        [rows_spec(width), rows_spec(width), picked(mlp, 2 * hidden), fixed(bias)],
        [
            shaped((count, hidden), BF16),
            shaped((count, hidden), BF16),
            shaped((count, width), BF16),
            shaped((1, hidden), F32),
        ],
        [rows_spec(hidden), rows_spec(hidden), rows_spec(width), fixed(bias)],
        6 * count * width * hidden,
        pick=pick,
    )


def mlp_out(pick, active, mlp):
    count, hidden = active.shape
    width = mlp.shape[0]

    def body(_, active_ref, mlp_ref, out_ref):
        out_ref[...] = dot_nt(active_ref[...], mlp_ref[:, hidden : 2 * hidden]).astype(BF16)

    return run(
        body,
        "mlp_out",
        (count // Q_BLOCK,),
        (active, mlp),
        [rows_spec(hidden), picked(mlp, 2 * hidden)],
        shaped((count, width), BF16),
        rows_spec(width),
        2 * count * width * hidden,
        pick=pick,
    )


def weight_grads(lefts, rights, name):
    count, width = lefts[0].shape
    wides = [item.shape[1] for item in rights]
    tile = 384
    total = len(lefts)

    def body(*refs):
        out_ref = refs[-1]
        spot = 0
        for k in range(total):
            product = dot_tn(refs[k][...], refs[total + k][...])
            out_ref[:, spot : spot + wides[k]] = product.astype(BF16)
            spot += wides[k]

    return run(
        body,
        name,
        (width // tile,),
        (*lefts, *rights),
        [pl.BlockSpec((count, tile), lambda i, *_: (0, i))] * total + [fixed(item) for item in rights],
        shaped((width, sum(wides)), BF16),
        pl.BlockSpec((tile, sum(wides)), lambda i: (i, 0)),
        2 * count * width * sum(wides),
    )


def out_grads(pieces, branch):
    total = len(pieces)
    piece = pieces[0].shape[0]
    wide = branch.shape[1]

    def body(*refs):
        for k in range(total):
            product = dot(refs[k][...], refs[total][...])
            refs[-1][k * piece : (k + 1) * piece, :] = product.astype(BF16)

    operands = (*pieces, branch)
    out = shaped((total * piece, wide), BF16)
    return run(
        body,
        "out_grads",
        (1,),
        operands,
        [fixed(item) for item in operands],
        out,
        fixed(out),
        2 * branch.shape[0] * total * piece * wide,
    )


def project_back(pick, grad, weight, block, rows_all, width):
    count, wide = grad.shape

    def body(_, grad_ref, weight_ref, rows_ref, back_ref, norm_ref, bias_ref):
        back = dot_nt(grad_ref[...], weight_ref[:, :wide])
        back_ref[...] = back.astype(BF16)
        unit = centred(rows_ref[:, :width].astype(F32))[0]
        gain = jnp.sum(back * unit, axis=0, keepdims=True)
        shift = jnp.sum(back, axis=0, keepdims=True)
        bias = jnp.sum(grad_ref[...].astype(F32), axis=0, keepdims=True)

        @pl.when(pl.program_id(0) == 0)
        def _():
            norm_ref[...] = jnp.zeros_like(norm_ref)
            bias_ref[...] = jnp.zeros_like(bias_ref)

        norm_ref[0:1] += gain
        norm_ref[1:2] += shift
        bias_ref[...] += bias

    return run(
        body,
        "project_back",
        (count // Q_BLOCK,),
        (grad, weight, rows_all),
        [rows_spec(wide), picked(weight, block), rows_spec(rows_all.shape[1])],
        [shaped((count, width), BF16), shaped((2, width), F32), shaped((1, wide), F32)],
        [
            rows_spec(width),
            pl.BlockSpec((2, width), lambda *_: (0, 0)),
            pl.BlockSpec((1, wide), lambda *_: (0, 0)),
        ],
        2 * count * width * wide,
        pick=pick,
    )


class Native:
    def __init__(self, sizes, images, tokens):
        self.dev, self.zed, self.why = sizes
        self.images = images
        self.tokens = tokens
        self.team = self.dev * 2
        self.groups = self.zed * self.why
        self.each = images * self.dev // self.groups
        self.piece = tokens // self.dev
        self.rows = self.each * self.groups * self.piece

    def positions(self, row):
        place = row % self.piece
        group = (row // self.piece) % self.groups
        team = row // (self.piece * self.groups)
        owner = group * 2 + team % 2
        return owner * self.tokens + (team // 2) * self.piece + place

    def tokens_in(self, values):
        wide = values.shape[-1]
        split = values.reshape(self.images, self.dev, self.piece, wide)
        split = lax.all_to_all(split, "dev", 1, 0, tiled=True)
        split = split.reshape(self.groups, self.each, self.piece, wide)
        split = lax.all_to_all(split, ("z", "y"), 0, 0, tiled=True)
        return split.transpose(1, 0, 2, 3).reshape(self.rows, wide)

    def tokens_out(self, values):
        wide = values.shape[-1]
        split = values.reshape(self.each, self.groups, self.piece, wide).transpose(1, 0, 2, 3)
        split = lax.all_to_all(split, ("z", "y"), 0, 0, tiled=True)
        split = split.reshape(self.dev * self.images, 1, self.piece, wide)
        split = lax.all_to_all(split, "dev", 0, 1, tiled=True)
        return split.reshape(self.images, self.tokens, wide)

    def rows_gather(self, values, *gates):
        wide = values.shape[-1]
        whole = lax.all_gather(values, ("dev", "core"), axis=0, tiled=True)
        whole = whole.reshape(self.team, self.each, -1, wide).transpose(1, 0, 2, 3)
        return whole.reshape(self.team * self.rows, wide)

    def rows_scatter(self, values):
        wide = values.shape[-1]
        split = values.astype(BF16).reshape(self.each, self.team, -1, wide).transpose(1, 0, 2, 3)
        split = split.reshape(self.team * self.rows, wide)
        return lax.psum_scatter(
            split, ("dev", "core"), scatter_dimension=0, tiled=True
        ).astype(F32)

    def rows_near(self, values):
        return values, values

    def rows_end(self, sums):
        return self.rows_scatter(sums[0])

    def own_rows(self, values):
        wide = values.shape[-1]
        me = lax.axis_index(("dev", "core"))
        split = values.reshape(self.each, self.team, -1, wide)
        return lax.dynamic_slice_in_dim(split, me, 1, 1).reshape(self.rows, wide)

    def heads_gather(self, values):
        return [lax.all_gather(values, ("dev", "core"), axis=0, tiled=True)], [[0]]

    def weights(self, w_qkv, w_out, mlp, packed, *gates):
        whole = lax.all_gather(w_qkv, "dev", axis=1, tiled=True)
        rows, wide = whole.shape
        split = whole.reshape(rows, 3, self.team, wide // (3 * self.team))
        split = lax.dynamic_slice_in_dim(split, 2 * lax.axis_index("dev"), 2, 2)
        split = split.transpose(0, 2, 1, 3).reshape(rows, -1)
        split = lax.all_to_all(split, "core", 1, 0, tiled=True)
        full_qkv = lax.all_gather(split, ("z", "y"), axis=0, tiled=True)
        full_out = lax.all_gather(w_out, "dev", axis=1, tiled=True)
        full_out = lax.all_gather(full_out, ("z", "y", "core"), axis=0, tiled=True)
        mlp = jnp.concatenate(mlp, axis=1)
        mlp = lax.all_to_all(mlp, "core", 1, 0, tiled=True)
        mlp = lax.all_gather(mlp, ("z", "y"), axis=0, tiled=True)
        vectors = lax.all_gather(packed, "dev", axis=0, tiled=True)
        return full_qkv, full_qkv.shape[1], full_out, mlp, jnp.zeros((1,), jnp.int32), vectors

    def mlp_grads(self, grads):
        return lax.psum_scatter(grads, ("z", "y"), scatter_dimension=0, tiled=True)

    def mlp_halves(self, grads):
        grads = lax.all_to_all(grads, "core", 0, 1, tiled=True).astype(F32)
        half = grads.shape[1] // 2
        return grads[:, :half], grads[:, half:]

    def attention_grads(self, grad_qkv, grad_out):
        return grad_qkv, grad_out

    def attention_sums(self, parts, *gates):
        both = jnp.concatenate([parts[1], parts[0]], axis=1)
        return lax.psum_scatter(both, ("z", "y"), scatter_dimension=0, tiled=True), both

    def attention_ends(self, both, block):
        out = lax.all_to_all(both[:, :block], "core", 0, 1, tiled=True)
        piece = lax.all_to_all(both[:, block:], "core", 0, 1, tiled=True)
        rows = piece.shape[0]
        piece = piece.reshape(rows, 2, 3, block).transpose(0, 2, 1, 3).reshape(rows, 3, 1, -1)
        whole = lax.all_gather(piece, "dev", axis=2, tiled=True)
        whole = whole.reshape(rows, self.dev, 6 * block)
        mine = lax.dynamic_slice_in_dim(whole, lax.axis_index("dev"), 1, 1)[:, 0]
        return mine.astype(F32), out.astype(F32)

    def total(self, values):
        return lax.psum(values, ("dev", "z", "y", "core"))


def joint(move):
    pairs = []
    for dev in range(2):
        for zed in range(4):
            for why in range(2):
                for core in range(2):
                    to = move(dev, zed, why, core)
                    source = ((dev * 4 + zed) * 2 + why) * 2 + core
                    pairs.append((source, ((to[0] * 4 + to[1]) * 2 + to[2]) * 2 + to[3]))
    return pairs


def send(values, move):
    return lax.ppermute(values, ("dev", "z", "y", "core"), joint(move))


def across(values):
    return send(values, lambda d, z, y, c: (1 - d, z, y, c))


def beside(values):
    return send(values, lambda d, z, y, c: (d, z, y, 1 - c))


def upright(values):
    return send(values, lambda d, z, y, c: (d, z, 1 - y, c))


class Paired(Native):
    def positions(self, row):
        place = row % self.tokens
        turn = (row // self.tokens) % 4
        team = row // (self.tokens * 4)
        zed = (lax.axis_index("z") - turn) % 4
        return ((zed * 2 + team // 2) * 2 + team % 2) * self.tokens + place

    def tokens_in(self, values):
        zed = lax.axis_index("z")
        pieces = []
        for turn in range(4):
            piece = lax.dynamic_slice_in_dim(values, (zed + turn) % 4, 1, 0)[0]
            pieces.append(send(piece, lambda d, z, y, c: (y, (z + turn) % 4, d, c)))
        return jnp.concatenate(pieces, axis=0)

    def tokens_out(self, values):
        zed = lax.axis_index("z")
        rows = self.tokens
        pieces = []
        for turn in range(4):
            piece = values[turn * rows : (turn + 1) * rows]
            pieces.append(send(piece, lambda d, z, y, c: (y, (z - turn) % 4, d, c)))
        order = (jnp.arange(4) - zed) % 4
        result = pieces[0][None]
        for turn in range(1, 4):
            result = jnp.where((order == turn)[:, None, None], pieces[turn][None], result)
        return result

    def rows_gather(self, values, *gates):
        me = lax.axis_index(("dev", "core"))
        rows, wide = values.shape
        mine = jnp.concatenate([values, after(across(values), *gates)], axis=0)
        whole = jnp.zeros((4 * rows, wide), values.dtype)
        for step, pair in enumerate((mine, beside(mine))):
            for far in range(2):
                piece = pair[far * rows : (far + 1) * rows]
                whole = lax.dynamic_update_slice(whole, piece, ((me ^ (step + 2 * far)) * rows, 0))
        return whole

    def rows_scatter(self, values):
        return self.rows_end(self.rows_near(values))

    def rows_near(self, values):
        rows = self.rows
        me = lax.axis_index(("dev", "core"))

        def part(step):
            return lax.dynamic_slice_in_dim(values, (me ^ step) * rows, rows, 0)

        near = jnp.concatenate([part(1), part(3)], axis=0)
        came = beside(near.astype(BF16))
        low, high = came[:rows].astype(F32), came[rows:].astype(F32)
        return part(0) + low, (part(2) + high).astype(BF16)

    def rows_end(self, sums):
        return sums[0] + across(sums[1]).astype(F32)

    def own_rows(self, values):
        me = lax.axis_index(("dev", "core"))
        return lax.dynamic_slice_in_dim(values, me * self.rows, self.rows, 0)

    def heads_gather(self, values):
        me = lax.axis_index(("dev", "core"))
        mine = jnp.concatenate([values, across(values)], axis=0)
        pieces = [mine, beside(mine)]
        block = values.shape[0]
        spots = [[(me ^ (step + 2 * far)) * block for far in range(2)] for step in range(2)]
        return pieces, spots

    def weights(self, w_qkv, w_out, mlp, packed, *gates):
        third = w_qkv.shape[1] // 3
        half = third // 2
        wide = w_out.shape[1]
        count = packed.shape[1]
        first = lax.axis_index("dev") == 0
        lines = -(-count // ((third + wide) * 8)) * 8
        sheet = jnp.pad(packed[0], (0, lines * (third + wide) - count)).reshape(lines, -1)
        message = jnp.concatenate([w_qkv[:, third : 2 * third], w_out], axis=1)
        came = across(jnp.concatenate([message, sheet], axis=0))
        rows = w_qkv.shape[0]
        vectors = came[rows:].reshape(1, -1)[:, :count]
        vectors = jnp.concatenate(
            [jnp.where(first, packed, vectors), jnp.where(first, vectors, packed)], axis=0
        )
        came_qkv, came_out = came[:rows, :third], came[:rows, third:]
        low, high = w_qkv[:, :third], w_qkv[:, 2 * third :]
        query = jnp.where(first, low, came_qkv)
        keys = jnp.where(first, high, low)
        values = jnp.where(first, came_qkv, high)
        blocks = [
            jnp.concatenate(
                [item[:, side * half : (side + 1) * half] for item in (query, keys, values)], axis=1
            )
            for side in range(2)
        ]
        block = -(-3 * half // 128) * 128
        blocks = [jnp.pad(item, ((0, 0), (0, block - 3 * half))) for item in blocks]
        everyone = ("z", "y", "core")
        outs = [jnp.where(first, w_out, came_out), jnp.where(first, came_out, w_out)]
        full_qkv = jnp.concatenate([*blocks, *outs], axis=1)
        full_qkv = lax.all_gather(full_qkv, everyone, axis=0, tiled=True)
        rest = after(jnp.concatenate(mlp, axis=1), full_qkv, *gates)
        rest = lax.all_gather(rest, everyone, axis=0, tiled=True)
        pick = lax.axis_index("core").reshape(1)
        return full_qkv, block, full_qkv[:, 2 * block :], rest, pick, vectors

    def turned(self):
        me = lax.axis_index(("dev", "core"))
        return [((k ^ me) % 2) * 2 + (k ^ me) // 2 for k in range(4)]

    def halve(self, block):
        upper = lax.axis_index("core") == 0
        rows = block.shape[0] // 2
        low, high = block[:rows], block[rows:]
        keep = jnp.where(upper, low, high)
        got = beside(jnp.where(upper, high, low).astype(BF16)).astype(F32)
        return jnp.where(upper, keep, got), jnp.where(upper, got, keep)

    def mlp_grads(self, grads):
        return lax.psum_scatter(grads, ("z", "y"), scatter_dimension=0, tiled=True)

    def mlp_halves(self, grads):
        return self.halve(grads.astype(F32))

    def attention_grads(self, grad_qkv, grad_out):
        block = grad_out.shape[1]
        rows = grad_qkv.shape[0] // 8
        why = lax.axis_index("y")
        order = grad_out.reshape(4, 2, rows, block)
        order = jnp.stack([lax.dynamic_index_in_dim(order, k, 0, False) for k in self.turned()])
        both = jnp.concatenate([order, grad_qkv.reshape(4, 2, rows, -1)], axis=3)
        mine = lax.dynamic_index_in_dim(both, why, 1, False)
        return mine, upright(lax.dynamic_index_in_dim(both, 1 - why, 1, False))

    def attention_sums(self, parts, *gates):
        mine = parts[0].astype(F32) + after(parts[1], *gates).astype(F32)
        mine = mine.astype(BF16).reshape(-1, mine.shape[2])
        return lax.psum_scatter(mine, "z", scatter_dimension=0, tiled=True), mine

    def attention_ends(self, both, block):
        first = lax.axis_index("dev") == 0
        left, right = self.halve(both.astype(F32))
        out = jnp.concatenate([left[:, :block], right[:, :block]], axis=1)
        query, keys, values = (
            jnp.concatenate([left[:, k * block : (k + 1) * block], right[:, k * block : (k + 1) * block]], axis=1)
            for k in (1, 2, 3)
        )
        came = across(jnp.where(first, values, query).astype(BF16)).astype(F32)
        return (
            jnp.concatenate(
                [jnp.where(first, query, keys), came, jnp.where(first, keys, values)], axis=1
            ),
            out,
        )

    def total(self, values):
        everyone = ("dev", "z", "y", "core")
        wide = values.shape[1]
        each = -(-wide // (32 * 128)) * 128
        parts = jnp.pad(values[0], (0, 32 * each - wide)).reshape(32, each)
        parts = lax.all_to_all(parts, everyone, 0, 0, tiled=True)
        mine = jnp.sum(parts, axis=0, keepdims=True)
        every = jnp.broadcast_to(mine, (32, each))
        return lax.all_to_all(every, everyone, 0, 0, tiled=True).reshape(1, -1)[:, :wide]


def norm_back(grad, unit, inverse, gain):
    scaled = grad * gain
    mean = jnp.mean(scaled, axis=-1, keepdims=True)
    along = jnp.mean(scaled * unit, axis=-1, keepdims=True)
    return (scaled - mean - unit * along) * inverse


def gelu_pair(hidden):
    root = 0.7978845608028654
    inner = jnp.tanh(root * (hidden + 0.044715 * hidden * hidden * hidden))
    half = 0.5 * (1.0 + inner)
    slope = half + 0.5 * hidden * (1.0 - inner * inner) * root * (
        1.0 + 3 * 0.044715 * hidden * hidden
    )
    return hidden * half, slope


def per_device(
    sizes,
    patches,
    patch_mask,
    cotangent,
    w_qkv,
    w_out,
    w_up,
    w_down,
    *vectors,
):
    images, tokens, width = patches.shape
    paired = sizes == (2, 4, 2) and images == 4 and Paired is not Native
    route = (Paired if paired else Native)(sizes, images, tokens)
    dev_count = sizes[0]
    team = route.team
    dev = lax.axis_index("dev")
    me = lax.axis_index(("dev", "core"))
    head_count = HEADS // team
    block = head_count * HEAD_DIM
    hidden = w_up.shape[1] // 2

    padded = -(-hidden // 128) * 128
    sides = [
        jnp.concatenate(
            [
                jnp.pad(item[:, side * hidden : (side + 1) * hidden], ((0, 0), (0, padded - hidden)))
                for item in (w_up, w_down)
            ],
            axis=1,
        )
        for side in range(2)
    ]
    marks = jnp.broadcast_to(patch_mask.astype(BF16)[:, :, None], (images, tokens, 128))
    own_in = route.tokens_in(jnp.concatenate([patches, marks, cotangent], axis=2))
    own_in, own_grad = own_in[:, : width + 128], own_in[:, width + 128 :]
    rows_all = route.rows_gather(own_in)
    packed = jnp.concatenate(vectors, axis=1)
    own_qkv, qkv_block, full_out, mlp, pick, halves = route.weights(
        w_qkv, w_out, sides, packed, rows_all
    )
    halves = halves.astype(F32)
    full = []
    spot = 0
    for item in vectors:
        full.append(halves[:, spot : spot + item.shape[1]].reshape(1, -1))
        spot += item.shape[1]
    gain_one, shift_one, gain_two, shift_two = full[:4]
    bias_query, bias_value, bias_out, bias_up, bias_down = full[4:]

    qkv_bias = jnp.concatenate(
        [
            lax.dynamic_slice_in_dim(bias_query, me * block, block, 1),
            jnp.zeros((1, block), F32),
            lax.dynamic_slice_in_dim(bias_value, me * block, block, 1),
        ],
        axis=1,
    )
    normed_one, projected = project(
        pick, rows_all, gain_one, shift_one, own_qkv, qkv_block, qkv_bias
    )
    rows_grad = route.rows_gather(after(own_grad, projected))
    seq = projected.shape[0] // route.each
    projected = projected.reshape(route.each, seq, 3 * block)
    marks = rows_all[:, width : width + 1].astype(F32).reshape(route.each, seq, 1)
    length = jnp.sum(marks, axis=1, keepdims=True)
    spot = route.positions(lax.broadcasted_iota(jnp.int32, (route.each, seq, 1), 1))
    mask_bias = jnp.where(spot.astype(F32) < length, 0.0, -1e30).astype(F32)

    attended, lse = attend_fwd(projected, mask_bias, head_count)
    pieces, spots = route.heads_gather(attended.transpose(1, 0, 2).reshape(block, -1))

    def by_piece(whole):
        size = pieces[0].shape[0] // len(spots[0])
        return jnp.stack(
            [
                jnp.concatenate([lax.dynamic_slice_in_dim(whole, at, size, 0) for at in group])
                for group in spots
            ]
        )

    middle, normed_two = attend_out(
        pieces, by_piece(full_out), rows_all, bias_out, gain_two, shift_two
    )
    up_bias = lax.dynamic_slice_in_dim(bias_up, me * hidden, hidden, 1)
    up_bias = jnp.pad(up_bias, ((0, 0), (0, padded - hidden)))

    active, grad_hidden, grad_part_two, up_sums = mlp_turn(
        pick, normed_two, rows_grad, mlp, up_bias
    )
    near_two = route.rows_near(grad_part_two)
    grad_mlp = weight_grads(
        [rows_grad, normed_two], [active, grad_hidden], "mlp_grads"
    )
    sum_mlp = route.mlp_grads(grad_mlp)
    grad_normed_two = after(route.rows_end(near_two), grad_mlp)
    own_middle = route.own_rows(middle)
    own_unit_two, own_inverse_two = centred(own_middle)
    grad_middle = own_grad.astype(F32) + norm_back(
        grad_normed_two, own_unit_two, own_inverse_two, gain_two
    )
    own_branch = grad_middle.astype(BF16)
    mlp_part = mlp_out(pick, after(active, own_branch), mlp)
    grad_branch = route.rows_gather(own_branch, mlp_part)

    grad_projected = attend_bwd(
        projected,
        mask_bias,
        lse,
        grad_branch.reshape(route.each, seq, width),
        lax.dynamic_slice_in_dim(full_out, me * block, block, 0),
        head_count,
    ).reshape(-1, 3 * block)
    my_branch = lax.dynamic_slice_in_dim(after(grad_branch, grad_projected), me * block, block, 1)
    grad_out = out_grads(pieces, my_branch)
    grad_qkv = weight_grads([normed_one], [grad_projected], "qkv_grads")
    attn_parts = route.attention_grads(grad_qkv, grad_out)
    grad_projected = after(grad_projected, attn_parts[0])

    grad_part_one, norm_sums, proj_sums = project_back(
        pick, grad_projected, own_qkv, qkv_block, rows_all, width
    )
    near_one = route.rows_near(grad_part_one)
    grad_normed_one = route.rows_end(near_one)
    mlp_near = route.rows_near(after(mlp_part, near_one[1]))

    own_unit_one, own_inverse_one = centred(
        route.own_rows(after(rows_all, near_one[1]))[:, :width].astype(F32)
    )
    grad_inputs = grad_middle + norm_back(
        grad_normed_one, own_unit_one, own_inverse_one, gain_one
    )
    sums_out, sent = route.attention_sums(attn_parts, grad_inputs, sum_mlp)
    grad_inputs = after(grad_inputs.astype(BF16), sent)
    grad_patches = route.tokens_out(grad_inputs)
    mlp_near = (mlp_near[0], after(mlp_near[1], sent))
    result = (own_middle + route.rows_end(mlp_near) + bias_down).astype(BF16)
    leaving = result
    result = route.tokens_out(result)

    out_qkv, out_out = route.attention_ends(sums_out, block)
    out_mlp = route.mlp_halves(sum_mlp)
    out_down, out_up = (
        jnp.concatenate([side[:, spot : spot + hidden] for side in out_mlp], axis=1)
        for spot in (0, padded)
    )

    def spread(values, size):
        return lax.dynamic_update_slice(
            jnp.zeros((size,), F32), values, (me * values.shape[0],)
        )

    norm_sums, proj_sums, up_sums = (
        after(item, grad_inputs) for item in (norm_sums, proj_sums, up_sums)
    )
    sums = [
        norm_sums[0],
        norm_sums[1],
        jnp.sum(grad_normed_two * own_unit_two, axis=0),
        jnp.sum(grad_normed_two, axis=0),
        spread(proj_sums[0, :block], width),
        spread(proj_sums[0, 2 * block :], width),
        jnp.sum(own_branch.astype(F32), axis=0),
        spread(up_sums[0, :hidden], hidden * team),
        jnp.sum(after(cotangent, grad_inputs).astype(F32), axis=(0, 1)),
    ]
    flat = route.total(after(jnp.concatenate(sums)[None], grad_inputs, leaving))
    out_vectors = []
    spot = 0
    for item in sums:
        size = item.shape[0]
        half = size // dev_count
        out_vectors.append(lax.dynamic_slice(flat, (0, spot + dev * half), (1, half)))
        spot += size
    return (result, grad_patches, out_qkv, out_out, out_up, out_down, *out_vectors)


def solution(mesh):
    dev_count, sa_count = mesh.devices.shape

    def whole(*args):
        zed = args[0].shape[0] // dev_count
        why = sa_count // (2 * zed)
        sizes = (dev_count, zed, why)
        inner = Mesh(mesh.devices.reshape(dev_count, zed, why, 2), ("dev", "z", "y", "core"))
        rows = ("z", "y", "core")
        token = P("dev", rows, None)
        weight = P(rows, "dev")
        vector = P(None, "dev")
        return jax.shard_map(
            functools.partial(per_device, sizes),
            mesh=inner,
            in_specs=(token, P("dev", rows), token) + (weight,) * 4 + (vector,) * 9,
            out_specs=(token, token) + (weight,) * 4 + (vector,) * 9,
            check_vma=False,
        )(*args)

    return whole
```
